32 devices in a mesh: gx: 8 (over y, x, core), vert: 4 (over z).
Axes of the slice: x: 2, y: 2, z: 4, core: 2. Of those that a mesh axis runs over, the one named last changes fastest.
Arguments:
- phase_field: float32 [64, 32, 32, 256], P('vert', 'gx'), may hold values from -0.2 to 1.2
- kappa_table: float32 [24, 3], replicated, may hold values from 0.2 to 2
- eps_table: float32 [12, 6], replicated, may hold values from -0.3 to 0.3
- orient_index: int32 [64], P('vert'), may hold values from 0 to 23
- family_index: int32 [64], P('vert'), may hold values from 0 to 11
Outputs:
- phase_next: float32 [64, 32, 32, 256], P('vert', 'gx')
- stress: float32 [6, 32, 32, 256], P(None, 'gx')
The draws below stay inside these ranges and needn't reach their ends.
All inputs are finite; a program needn't handle non-finite values.
Results may differ from the reference program's by a relative error of at most 0.0003.
Values sent between devices are 32-bit elements; how exact they have to be, the bound alone decides.
A program may use at most 64 MiB of HBM per device.

```python
import math
import jax
import jax.numpy as jnp
from jax import lax

NVAR = 64
NFAM = 12
NORI = 24
NY = 32
NZ = 256
NX = 32


def with_ends(values, key, low, top_value):
    dims = values.shape
    spot = [jax.random.randint(jax.random.fold_in(key, axis), (), 0, dims[axis]) for axis in range(len(dims))]
    values = values.at[tuple(spot)].set(low)
    longest = dims.index(max(dims))
    spot[longest] = (spot[longest] + 1) % dims[longest]
    return values.at[tuple(spot)].set(top_value)


def shard_levels(own_key, extent, pieces, smallest, largest):
    def one(position, blocks):
        steps = jax.random.uniform(jax.random.fold_in(jax.random.fold_in(own_key, 6), position), (blocks,), jnp.float32, smallest / len(pieces), largest / len(pieces))
        return jnp.repeat(jnp.exp(steps), extent[position] // blocks).reshape((-1,) + (1,) * (len(extent) - position - 1))

    gain = one(*pieces[0])
    for cut in pieces[1:]:
        gain = gain * one(*cut)
    return gain


def noise(key, dims, deviation, bound, kind=jnp.bfloat16):
    drawn = deviation * jax.random.normal(key, dims, jnp.float32)
    return jnp.clip(drawn, min=-bound, max=bound).astype(kind)


def setup_inputs(seed: int = 0) -> dict:
    seeds = jax.random.split(jax.random.key(seed), 6)
    phase_field = jnp.clip(-0.2 + 1.4000001 * jax.random.uniform(seeds[0], (NVAR, NX, NY, NZ), jnp.float32) ** shard_levels(seeds[0], (NVAR, NX, NY, NZ), ((0, 4), (1, 8)), -0.2, 0.2), -0.2, 1.2)
    kappa_table = jnp.clip(jnp.exp(jax.random.uniform(seeds[1], (NORI, 3), jnp.float32, math.log(0.2), math.log(2.0))), 0.2, 2.0)
    eps_table = noise(seeds[2], (NFAM, 6), 0.05, 0.3, jnp.float32)
    orient_index = with_ends(jax.random.randint(seeds[3], (NVAR,), 0, NORI), jax.random.fold_in(seeds[3], 1), 0, NORI - 1).astype(jnp.int32)
    family_index = with_ends(jax.random.randint(seeds[4], (NVAR,), 0, NFAM), jax.random.fold_in(seeds[4], 1), 0, NFAM - 1).astype(jnp.int32)
    return dict(phase_field=phase_field, kappa_table=kappa_table, eps_table=eps_table, orient_index=orient_index, family_index=family_index)


LAME_LAMBDA = 1.5
SHEAR_MOD = 1.0
TIME_STEP = 0.1
CROSS_COUPLING = 0.02
HIGHEST = lax.Precision.HIGHEST
TENSOR_SLOTS = ((0, 5, 4), (5, 1, 3), (4, 3, 2))
VOIGT_PAIRS = ((0, 0), (1, 1), (2, 2), (1, 2), (0, 2), (0, 1))

def signed_wave(first_row, row_count, full_count):
    positions = first_row + jnp.arange(row_count, dtype=jnp.int32)
    shifted = jnp.where(positions * 2 >= full_count, positions - full_count, positions)
    return shifted.astype(jnp.float32) / full_count

def wave_normals(x_wave, y_wave, z_wave):
    x_grid = x_wave[:, None, None]
    y_grid = y_wave[None, :, None]
    z_grid = z_wave[None, None, :]
    length_sq = x_grid * x_grid + y_grid * y_grid + z_grid * z_grid
    positive = length_sq > 0
    safe_length = jnp.where(positive, length_sq, 1.0)
    inverse_len = jnp.where(positive, lax.rsqrt(safe_length), 0.0)
    return [x_grid * inverse_len, y_grid * inverse_len, z_grid * inverse_len]

def green_stress(strain, normals):
    trace_strain = strain[0] + strain[1] + strain[2]
    stiffened = [LAME_LAMBDA * trace_strain + 2.0 * SHEAR_MOD * strain[number] if number < 3 else 2.0 * SHEAR_MOD * strain[number] for number in range(6)]
    traction = [sum((stiffened[TENSOR_SLOTS[row_axis][col_axis]] * normals[col_axis] for col_axis in range(3))) for row_axis in range(3)]
    normal_part = normals[0] * traction[0] + normals[1] * traction[1] + normals[2] * traction[2]
    coupling = (LAME_LAMBDA + SHEAR_MOD) / (LAME_LAMBDA + 2.0 * SHEAR_MOD)
    shifted = [(traction[row_axis] - normals[row_axis] * normal_part * coupling) / SHEAR_MOD for row_axis in range(3)]
    excess = [0.5 * (normals[VOIGT_PAIRS[number][0]] * shifted[VOIGT_PAIRS[number][1]] + normals[VOIGT_PAIRS[number][1]] * shifted[VOIGT_PAIRS[number][0]]) - strain[number] for number in range(6)]
    trace_excess = excess[0] + excess[1] + excess[2]
    result = [LAME_LAMBDA * trace_excess + 2.0 * SHEAR_MOD * excess[number] if number < 3 else 2.0 * SHEAR_MOD * excess[number] for number in range(6)]
    return jnp.stack(result)

def reaction_update(variant, laplace, driving, square_sum):
    chemical = 2.0 * variant - 6.0 * variant * variant + 4.0 * variant * variant * variant
    chemical = chemical + 2.0 * CROSS_COUPLING * variant * (square_sum - variant * variant)
    chemical = chemical - 2.0 * variant * driving - laplace
    return variant - TIME_STEP * chemical

def reference(phase_field, kappa_table, eps_table, orient_index, family_index):
    family_hot = (family_index[:, None] == jnp.arange(NFAM, dtype=jnp.int32)[None, :]).astype(jnp.float32)
    orient_hot = (orient_index[:, None] == jnp.arange(NORI, dtype=jnp.int32)[None, :]).astype(jnp.float32)
    eps_var = jnp.dot(family_hot, eps_table, precision=HIGHEST)
    kappa_var = jnp.dot(orient_hot, kappa_table, precision=HIGHEST)

    def accumulate(state_pair, inputs):
        eigen_sum, square_sum = state_pair
        variant, strain_row = inputs
        squared = variant * variant
        return ((eigen_sum + strain_row[:, None, None, None] * squared[None], square_sum + squared), None)
    start_eigen = jnp.zeros((6, NX, NY, NZ), jnp.float32)
    start_square = jnp.zeros((NX, NY, NZ), jnp.float32)
    (eigen_sum, square_sum), unused = lax.scan(accumulate, (start_eigen, start_square), (phase_field, eps_var))
    eigen_hat = jnp.fft.fftn(eigen_sum, axes=(1, 2, 3))
    normals = wave_normals(signed_wave(0, NX, NX), signed_wave(0, NY, NY), signed_wave(0, NZ, NZ))
    real_hat = green_stress(jnp.real(eigen_hat).astype(jnp.float32), normals)
    imag_hat = green_stress(jnp.imag(eigen_hat).astype(jnp.float32), normals)
    stress = jnp.real(jnp.fft.ifftn(real_hat + 1j * imag_hat, axes=(1, 2, 3))).astype(jnp.float32)
    weights = jnp.array([1.0, 1.0, 1.0, 2.0, 2.0, 2.0], jnp.float32)

    def advance(inputs):
        variant, strain_row, kappa_row = inputs
        driving = jnp.einsum('k,kxyz->xyz', strain_row * weights, stress, precision=HIGHEST)
        laplace = kappa_row[0] * (jnp.roll(variant, 1, 0) + jnp.roll(variant, -1, 0) - 2.0 * variant)
        laplace = laplace + kappa_row[1] * (jnp.roll(variant, 1, 1) + jnp.roll(variant, -1, 1) - 2.0 * variant)
        laplace = laplace + kappa_row[2] * (jnp.roll(variant, 1, 2) + jnp.roll(variant, -1, 2) - 2.0 * variant)
        return reaction_update(variant, laplace, driving, square_sum)
    phase_next = lax.map(advance, (phase_field, eps_var, kappa_var))
    return (phase_next, stress)
```

```python
import functools
import math

import jax
import jax.numpy as jnp
import ml_dtypes
import numpy as np
from jax import lax
from jax.experimental import pallas as pl
from jax.experimental.pallas import tpu as pltpu
from jax.sharding import PartitionSpec as P

LAME_LAMBDA = 1.5
SHEAR_MOD = 1.0
TIME_STEP = 0.1
CROSS_COUPLING = 0.02
HIGHEST = lax.Precision.HIGHEST
TENSOR_SLOTS = ((0, 5, 4), (5, 1, 3), (4, 3, 2))
VOIGT_PAIRS = ((0, 0), (1, 1), (2, 2), (1, 2), (0, 2), (0, 1))
PAIRED_FORMS = {1: "pcxyz,pxqk->qckyz", 2: "pcxyz,pyqk->qcxkz", 3: "pcxyz,pzqk->qcxyk"}


def with_halo(block, sides, width):
    for axis, dim in sides:
        count = lax.axis_size(axis)
        forward = [(i, i + 1) for i in range(count - 1)]
        forward.append((count - 1, 0))
        backward = [(target, source) for source, target in forward]
        low = lax.ppermute(
            lax.slice_in_dim(block, block.shape[dim] - width, None, axis=dim), axis, forward
        )
        high = lax.ppermute(lax.slice_in_dim(block, 0, width, axis=dim), axis, backward)
        block = jnp.concatenate([low, block, high], axis=dim)
    return block


def signed_wave(first_row, row_count, full_count):
    positions = first_row + jnp.arange(row_count, dtype=jnp.int32)
    shifted = jnp.where(positions * 2 >= full_count, positions - full_count, positions)
    return shifted.astype(jnp.float32) / full_count


def wave_normals(x_wave, y_wave, z_wave):
    x_grid = x_wave[:, None, None]
    y_grid = y_wave[None, :, None]
    z_grid = z_wave[None, None, :]
    length_sq = x_grid * x_grid + y_grid * y_grid + z_grid * z_grid
    positive = length_sq > 0
    safe_length = jnp.where(positive, length_sq, 1.0)
    inverse_len = jnp.where(positive, lax.rsqrt(safe_length), 0.0)
    return [x_grid * inverse_len, y_grid * inverse_len, z_grid * inverse_len]


def green_stress(strain, normals):
    trace_strain = strain[0] + strain[1] + strain[2]
    stiffened = [
        (
            LAME_LAMBDA * trace_strain + 2.0 * SHEAR_MOD * strain[number]
            if number < 3
            else 2.0 * SHEAR_MOD * strain[number]
        )
        for number in range(6)
    ]
    traction = [
        sum(
            (
                stiffened[TENSOR_SLOTS[row_axis][col_axis]] * normals[col_axis]
                for col_axis in range(3)
            )
        )
        for row_axis in range(3)
    ]
    normal_part = normals[0] * traction[0] + normals[1] * traction[1] + normals[2] * traction[2]
    coupling = (LAME_LAMBDA + SHEAR_MOD) / (LAME_LAMBDA + 2.0 * SHEAR_MOD)
    shifted = [
        (traction[row_axis] - normals[row_axis] * normal_part * coupling) / SHEAR_MOD
        for row_axis in range(3)
    ]
    excess = [
        0.5
        * (
            normals[VOIGT_PAIRS[number][0]] * shifted[VOIGT_PAIRS[number][1]]
            + normals[VOIGT_PAIRS[number][1]] * shifted[VOIGT_PAIRS[number][0]]
        )
        - strain[number]
        for number in range(6)
    ]
    trace_excess = excess[0] + excess[1] + excess[2]
    result = [
        (
            LAME_LAMBDA * trace_excess + 2.0 * SHEAR_MOD * excess[number]
            if number < 3
            else 2.0 * SHEAR_MOD * excess[number]
        )
        for number in range(6)
    ]
    return result


def reaction_update(variant, laplace, driving, square_sum):
    chemical = 2.0 * variant - 6.0 * variant * variant + 4.0 * variant * variant * variant
    chemical = chemical + 2.0 * CROSS_COUPLING * variant * (square_sum - variant * variant)
    chemical = chemical - 2.0 * variant * driving - laplace
    return variant - TIME_STEP * chemical


def dft_tables(length):
    positions = jnp.arange(length, dtype=jnp.int32)
    products = positions[:, None] * positions[None, :] % length
    angles = products.astype(jnp.float32) * (2.0 * math.pi / length)
    return (jnp.cos(angles), jnp.sin(angles))


def paired_table(length, inverse):
    cosine_table, sine_table = dft_tables(length)
    cross_term = sine_table if inverse else -sine_table
    from_real = jnp.stack([cosine_table, cross_term], axis=1)
    from_imag = jnp.stack([-cross_term, cosine_table], axis=1)
    table = jnp.stack([from_real, from_imag])
    if inverse:
        table = table * (1.0 / length)
    return table


def transform(real_part, imag_part, axis_dim, inverse):
    length = real_part.shape[axis_dim]
    table = paired_table(length, inverse)
    if imag_part is None:
        pattern = PAIRED_FORMS[axis_dim].replace("p", "")
        result = jnp.einsum(pattern, real_part, table[0], precision=HIGHEST)
        return (result[0], result[1])
    stacked = jnp.stack([real_part, imag_part])
    result = jnp.einsum(PAIRED_FORMS[axis_dim], stacked, table, precision=HIGHEST)
    return (result[0], result[1])


def transform_real(real_part, imag_part, axis_dim):
    length = real_part.shape[axis_dim]
    table = paired_table(length, True)[:, :, 0, :]
    pattern = PAIRED_FORMS[axis_dim].replace("q", "")
    stacked = jnp.stack([real_part, imag_part])
    return jnp.einsum(pattern, stacked, table, precision=HIGHEST)


def forward_x(halves):
    return transform(halves[0], halves[1], 1, False)


def forward_y(halves):
    return transform(halves[0], halves[1], 2, False)


def backward_x(halves):
    return transform(halves[0], halves[1], 1, True)


def backward_z(halves):
    return transform_real(halves[0], halves[1], 3)


def general_body(phase_field, kappa_table, eps_table, orient_index, family_index):
    slab_count = lax.axis_size("gx")
    count_var, slab_width, width_y, width_z = phase_field.shape
    total_x = slab_width * slab_count
    family_hot = (
        family_index[:, None] == jnp.arange(eps_table.shape[0], dtype=jnp.int32)[None, :]
    ).astype(jnp.float32)
    orient_hot = (
        orient_index[:, None] == jnp.arange(kappa_table.shape[0], dtype=jnp.int32)[None, :]
    ).astype(jnp.float32)
    eps_var = jnp.dot(family_hot, eps_table, precision=HIGHEST)
    kappa_var = jnp.dot(orient_hot, kappa_table, precision=HIGHEST)
    padded = with_halo(phase_field, (("gx", 1),), 1)
    squared = phase_field * phase_field
    eigen_sum = jnp.einsum("vk,vxyz->kxyz", eps_var, squared, precision=HIGHEST)
    local_square = jnp.sum(squared, axis=0)
    eigen_sum = lax.psum_scatter(eigen_sum, "vert", scatter_dimension=2, tiled=True)
    square_sum = lax.psum(local_square, "vert")
    real_part, imag_part = transform(eigen_sum, None, 3, False)
    real_part, imag_part = forward_x(
        (
            lax.all_to_all(real_part, "gx", split_axis=3, concat_axis=1, tiled=True),
            lax.all_to_all(imag_part, "gx", split_axis=3, concat_axis=1, tiled=True),
        )
    )
    real_part, imag_part = forward_y(
        (
            lax.all_to_all(real_part, "vert", split_axis=1, concat_axis=2, tiled=True),
            lax.all_to_all(imag_part, "vert", split_axis=1, concat_axis=2, tiled=True),
        )
    )
    x_start = lax.axis_index("vert") * real_part.shape[1]
    z_start = lax.axis_index("gx") * real_part.shape[3]
    normals = wave_normals(
        signed_wave(x_start, real_part.shape[1], total_x),
        signed_wave(0, width_y, width_y),
        signed_wave(z_start, real_part.shape[3], width_z),
    )
    real_part = jnp.stack(green_stress(real_part, normals))
    imag_part = jnp.stack(green_stress(imag_part, normals))
    real_part, imag_part = transform(real_part, imag_part, 2, True)
    real_part, imag_part = backward_x(
        (
            lax.all_to_all(real_part, "vert", split_axis=2, concat_axis=1, tiled=True),
            lax.all_to_all(imag_part, "vert", split_axis=2, concat_axis=1, tiled=True),
        )
    )
    stress = backward_z(
        (
            lax.all_to_all(real_part, "gx", split_axis=1, concat_axis=3, tiled=True),
            lax.all_to_all(imag_part, "gx", split_axis=1, concat_axis=3, tiled=True),
        )
    )
    stress = lax.all_gather(stress, "vert", axis=2, tiled=True)
    weights = jnp.array([1.0, 1.0, 1.0, 2.0, 2.0, 2.0], jnp.float32)
    driving = jnp.einsum("vk,kxyz->vxyz", eps_var * weights[None, :], stress, precision=HIGHEST)
    kappa_x = kappa_var[:, 0][:, None, None, None]
    kappa_y = kappa_var[:, 1][:, None, None, None]
    kappa_z = kappa_var[:, 2][:, None, None, None]
    laplace = kappa_x * (padded[:, 2:] + padded[:, :-2] - 2.0 * phase_field)
    laplace = laplace + kappa_y * (
        jnp.roll(phase_field, 1, 2) + jnp.roll(phase_field, -1, 2) - 2.0 * phase_field
    )
    laplace = laplace + kappa_z * (
        jnp.roll(phase_field, 1, 3) + jnp.roll(phase_field, -1, 3) - 2.0 * phase_field
    )
    phase_next = reaction_update(phase_field, laplace, driving, square_sum[None])
    return (phase_next, stress)


MESH = pl.DeviceIdType.MESH
VMEM_SPEC = pl.BlockSpec(memory_space=pltpu.VMEM)
ANY_SPEC = pl.BlockSpec(memory_space=pl.ANY)
SMEM_SPEC = pl.BlockSpec(memory_space=pltpu.SMEM)
VMEM_LIMIT = 56 * 1024 * 1024


def split_table(table):
    high = table.astype(np.float32).astype(ml_dtypes.bfloat16)
    low = (table - high.astype(np.float64)).astype(np.float32).astype(ml_dtypes.bfloat16)
    return jnp.asarray(np.stack([high, low]))


def trig(length):
    positions = np.arange(length)
    angles = (positions[:, None] * positions[None, :] % length) * (2.0 * np.pi / length)
    return np.cos(angles), np.sin(angles)


def z_tables(length):
    half = length // 2
    cosine, sine = trig(length)
    forward = np.concatenate([cosine[:, : half + 1], -sine[:, 1:half]], axis=1)
    weight = np.full(length, 2.0)
    weight[[0, half]] = 1.0
    inverse = forward.T * weight[:, None] / length
    return forward, inverse


def y_tables(length, width):
    half = length // 2
    cosine, sine = trig(length)
    eye = np.eye(width)
    full = np.array([[cosine, sine], [-sine, cosine]])
    edge = np.zeros_like(full)
    low, high, ends = slice(1, half), slice(half + 1, length), [0, half]
    edge[0, 0, low], edge[1, 0, low] = cosine[low], -sine[low]
    edge[0, 1, high], edge[1, 1, high] = cosine[high], -sine[high]
    edge[0, 0, ends], edge[1, 1, ends] = cosine[ends], cosine[ends]
    weight = np.full(length, 2.0)
    weight[ends] = 1.0
    forward, inverse = [], []
    size = 2 * width * length
    for table, scale in ((full, np.ones(length)), (edge, weight)):
        grid = np.einsum("abky,xw->kaxbwy", table, eye)
        forward.append(grid.reshape(size, size))
        grid = np.einsum("abky,xw,k->bwykax", table, eye, scale / length)
        inverse.append(grid.reshape(size, size))
    return np.concatenate(forward), np.concatenate(inverse)


def x_tables(slabs, width):
    length = slabs * width
    cosine, sine = (part.reshape(length, slabs, width) for part in trig(length))
    zero = np.zeros_like(cosine)
    from_real = np.stack([np.stack([cosine, zero], 2), np.stack([-sine, zero], 2)])
    from_imag = np.stack([np.stack([zero, sine], 2), np.stack([zero, cosine], 2)])
    rows = np.stack([from_real, from_imag])
    forward = rows.reshape(4 * length, 2 * length)
    inverse = (rows[0] + rows[1]).reshape(2 * length, 2 * length).T / length
    return forward, inverse


def halves(value):
    high = value.astype(jnp.bfloat16)
    return high, (value - high.astype(jnp.float32)).astype(jnp.bfloat16)


def mm(left, right):
    return jnp.dot(left, right, preferred_element_type=jnp.float32)


def table_left(table_ref, value):
    high, low = halves(value)
    return mm(table_ref[0], high) + (mm(table_ref[0], low) + mm(table_ref[1], high))


def table_right(value, table_ref):
    high, low = halves(value)
    return mm(high, table_ref[0]) + (mm(low, table_ref[0]) + mm(high, table_ref[1]))


def first_lane(shape):
    return lax.broadcasted_iota(jnp.int32, shape, len(shape) - 1) == 0


def spectrum_kernel(family_ref, eps_ref, phase_ref, z_ref, y_ref, out_ref, square_ref, eigen_ref):
    count, _, ny, nz = phase_ref.shape
    width = pl.num_programs(0)
    plane = pl.program_id(0)
    planes = square_ref.shape[0]
    step = 32

    def accumulate(index, carry):
        rows = pl.ds(pl.multiple_of(index * step, step), step)
        sums = [jnp.zeros((step, nz), jnp.float32) for _ in range(7)]
        for number in range(count):
            value = phase_ref[number, 0, rows, :]
            value = value * value
            family = family_ref[number]
            for comp in range(6):
                sums[comp] = sums[comp] + eps_ref[comp, family] * value
            sums[6] = sums[6] + value
        for comp in range(6):
            eigen_ref[comp, plane, rows, :] = sums[comp]
        square_ref[plane, rows, :] = sums[6]
        return carry

    lax.fori_loop(0, ny // step, accumulate, 0)
    half = nz // 2
    size = 2 * planes * ny

    @pl.when(plane == width - 1)
    def _():
        first = first_lane((size, half))

        def transform_pair(pair, carry):
            rows = planes * ny
            lines = table_right(eigen_ref[pl.ds(2 * pair, 2)].reshape(2 * rows, nz), z_ref)
            upper, lower = lines[:rows], lines[rows:]
            columns = [
                jnp.concatenate([upper[:, :half], upper[:, half:]]),
                jnp.concatenate([lower[:, :half], lower[:, half:]]),
            ]
            both = table_left(y_ref, jnp.concatenate(columns, axis=1))
            for side in range(2):
                lanes = slice(side * half, (side + 1) * half)
                picked = jnp.where(first, both[size:, lanes], both[:size, lanes])
                out_ref[:, pl.ds(2 * pair + side, 1)] = picked.reshape(ny, 1, 2 * planes, half)
            return carry

        lax.fori_loop(0, 3, transform_pair, 0)


def signed(position, full):
    return jnp.where(position * 2 >= full, position - full, position)


def unit_normals(x_mode, y_mode, z_mode, sizes):
    pair = []
    for flip in (False, True):
        waves = []
        for mode, full in zip((x_mode, y_mode, z_mode), sizes):
            wave = signed(mode, full)
            if flip:
                wave = jnp.where(mode * 2 == full, -wave, wave)
            waves.append(wave.astype(jnp.float32) * (1.0 / full))
        length_sq = waves[0] * waves[0] + waves[1] * waves[1] + waves[2] * waves[2]
        positive = length_sq > 0
        inverse = jnp.where(positive, lax.rsqrt(jnp.where(positive, length_sq, 1.0)), 0.0)
        pair.append([wave * inverse for wave in waves])
    return pair


def exchange_kernel(
    orient_ref, kappa_ref, hat_ref, phase_hbm, square_ref, forward_ref, inverse_ref,
    out_ref, base_ref, phase_ref,
    phase_sem,
    right_recv, left_recv, right_out, left_out, block_sum, cross_recv, cross_out, gathered,
    low_halo, high_halo, square_recv, square_out, square_total,
    sum_send_sem, sum_recv_sem, cross_send_sem, cross_recv_sem, back_send_sem, back_recv_sem,
    gather_send_sem, gather_recv_sem, square_send_sem, square_recv_sem, halo_send_sem, halo_recv_sem,
):
    slabs = lax.axis_size("gx")
    groups = lax.axis_size("vert")
    mine_x = lax.axis_index("gx")
    mine_v = lax.axis_index("vert")
    count, width, ny, nz = phase_ref.shape
    nx = slabs * width
    half = nz // 2
    last = groups - 1
    pieces = sum_send_sem.shape[2]
    piece = slabs // pieces

    def at(axis, offset):
        if axis == "gx":
            return lax.rem(mine_x + offset, slabs)
        return lax.rem(mine_v + offset, groups)

    def copy(src, dst, send_sem, recv_sem, axis, offset):
        return pltpu.make_async_remote_copy(
            src_ref=src, dst_ref=dst, send_sem=send_sem, recv_sem=recv_sem,
            device_id={axis: at(axis, offset)}, device_id_type=MESH,
        )

    phase_copy = pltpu.make_async_copy(phase_hbm, phase_ref, phase_sem)
    phase_copy.start()
    has_left = mine_v > 0
    has_right = mine_v < last
    barrier = pltpu.get_barrier_semaphore()
    for offset in range(1, slabs):
        pl.semaphore_signal(barrier, inc=1, device_id={"gx": at("gx", offset)}, device_id_type=MESH)

    @pl.when(has_left)
    def _():
        pl.semaphore_signal(
            barrier, inc=1, device_id={"vert": at("vert", last)}, device_id_type=MESH
        )

    @pl.when(has_right)
    def _():
        pl.semaphore_signal(barrier, inc=1, device_id={"vert": at("vert", 1)}, device_id_type=MESH)

    pl.semaphore_wait(barrier, slabs - 1 + jnp.where(has_left, 1, 0) + jnp.where(has_right, 1, 0))

    def side(right):
        if right:
            return right_recv, right_out, 0, 1, mine_v == 0
        return left_recv, left_out, 1, last, mine_v == last

    def sum_copy(right, turn, part, src=None):
        recv, out, way, offset, _ = side(right)
        local = pl.ds(part * piece, piece)
        return copy(
            out.at[turn, local] if src is None else src, recv.at[turn, local],
            sum_send_sem.at[way, turn, part], sum_recv_sem.at[way, turn, part], "vert", offset,
        )

    def sends_sum(right, turn):
        return mine_v < last - turn if right else mine_v > turn

    def start_sums(right):
        at_end = side(right)[4]

        @pl.when(at_end)
        def _():
            for turn in range(last):
                owner = last - turn if right else turn
                for part in range(pieces):
                    rows = pl.ds(owner * slabs + part * piece, piece)
                    sum_copy(right, turn, part, hat_ref.at[rows]).start()

    def pass_sum(right, turn, part):
        recv, out, _, _, at_end = side(right)
        owner = last - turn if right else turn
        local = pl.ds(part * piece, piece)
        rows = pl.ds(owner * slabs + part * piece, piece)

        @pl.when(jnp.logical_not(at_end) & sends_sum(right, turn))
        def _():
            sum_copy(right, turn, part).wait_recv()
            out[turn, local] = hat_ref[rows] + recv[turn, local]
            sum_copy(right, turn, part).start()

    def end_sum(right, turn, part):
        at_end = side(right)[4]
        owner = last - turn if right else turn

        @pl.when(jnp.logical_not(at_end) & (mine_v == owner))
        def _():
            sum_copy(right, turn, part).wait_recv()

    def square_copy(right, src=None):
        way = 0 if right else 1
        return copy(
            square_out.at[way] if src is None else src, square_recv.at[way],
            square_send_sem.at[way], square_recv_sem.at[way], "vert", 1 if right else last,
        )

    def square_hop(hop):
        for right in (True, False):
            way = 0 if right else 1

            @pl.when(mine_v == (hop if right else last - hop))
            def _():
                if hop == 0:
                    square_copy(right, square_ref).start()
                else:
                    square_copy(right).wait_recv()
                    square_out[way] = square_ref[...] + square_recv[way]
                    square_copy(right).start()

    for right in (True, False):
        start_sums(right)
    square_hop(0)
    halo_copies = [
        copy(phase_hbm.at[:, width - 1], low_halo, halo_send_sem.at[0], halo_recv_sem.at[0], "gx", 1),
        copy(phase_hbm.at[:, 0], high_halo, halo_send_sem.at[1], halo_recv_sem.at[1], "gx", slabs - 1),
    ]
    for item in halo_copies:
        item.start()
    lower = mine_v * 2 < groups
    for when, order in ((lower, (True, False)), (jnp.logical_not(lower), (False, True))):

        @pl.when(when)
        def _():
            for turn in range(last):
                for right in order:
                    for part in range(pieces):
                        pass_sum(right, turn, part)

    for right in (True, False):
        for turn in range(last):
            for part in range(pieces):
                end_sum(right, turn, part)

    block_sum[...] = hat_ref[pl.ds(mine_v * slabs, slabs)]

    @pl.when(has_left)
    def _():
        block_sum[...] = block_sum[...] + right_recv[last - mine_v]

    @pl.when(has_right)
    def _():
        block_sum[...] = block_sum[...] + left_recv[mine_v]

    cross_copies = []
    for offset in range(1, slabs):
        cross_copies.append(copy(
            block_sum.at[at("gx", offset)], cross_recv.at[mine_x],
            cross_send_sem.at[offset - 1], cross_recv_sem.at[offset - 1], "gx", offset,
        ))
        cross_copies[-1].start()

    if last > 1:
        square_hop(1)
    shape = (nx, half)
    y_mode = jnp.full(shape, 0, jnp.int32) + (mine_v * slabs + mine_x)
    x_mode = lax.broadcasted_iota(jnp.int32, shape, 0)
    lane = lax.broadcasted_iota(jnp.int32, shape, 1)
    ends = (y_mode == 0) | (y_mode * 2 == ny)
    upper = y_mode * 2 > ny
    edge = lane == 0
    z_first = jnp.where(edge & upper, half, lane)
    z_second = jnp.where(edge & (upper | ends), half, lane)
    normal_sets = [
        unit_normals(x_mode, y_mode, z_mode, (nx, ny, nz)) for z_mode in (z_first, z_second)
    ]
    cross_recv[mine_x] = block_sum[mine_x]
    for item in cross_copies:
        item.wait_recv()
    for hop in range(2, last):
        square_hop(hop)

    parts = []
    for comp in range(6):
        modes = table_left(forward_ref, cross_recv[:, comp].reshape(2 * nx, half))
        parts.append([modes[i * nx : (i + 1) * nx] for i in range(4)])
    stresses = []
    for part in range(2):
        total = None
        for source in range(2):
            strain = [parts[comp][2 * source + part] for comp in range(6)]
            for normals in normal_sets[source]:
                value = green_stress(strain, normals)
                total = value if total is None else [a + b for a, b in zip(total, value)]
        stresses.append([0.5 * value for value in total])
    for comp in range(6):
        lines = table_left(inverse_ref, jnp.concatenate([stresses[0][comp], stresses[1][comp]]))
        cross_out[:, comp] = lines.reshape(slabs, 2 * width, half)

    mine = mine_v * slabs + mine_x
    back_copies = []
    for offset in range(1, slabs):
        back_copies.append(copy(
            cross_out.at[at("gx", offset)], gathered.at[mine],
            back_send_sem.at[offset - 1], back_recv_sem.at[offset - 1], "gx", offset,
        ))
        back_copies[-1].start()
    gathered[mine] = cross_out[mine_x]

    def gather_copy(right, group, row):
        way = 0 if right else 1
        place = gathered.at[group * slabs + row]
        return copy(
            place, place, gather_send_sem.at[way, group, row],
            gather_recv_sem.at[way, group, row], "vert", 1 if right else last,
        )

    def row_of(offset):
        return lax.rem(mine_x + slabs - offset, slabs)

    def send_row(row):
        for right, able in ((True, has_right), (False, has_left)):

            @pl.when(able)
            def _():
                gather_copy(right, mine_v, row).start()

    send_row(mine_x)
    for offset in range(1, slabs):
        back_copies[offset - 1].wait_recv()
        send_row(row_of(offset))

    def over_rows(able, action):
        @pl.when(able)
        def _():
            def one(offset, carry):
                action(row_of(offset))
                return carry

            lax.fori_loop(0, slabs, one, 0)

    def forward_rows(stage):
        for right, able, exists, group in (
            (True, has_right, mine_v >= stage, mine_v - stage),
            (False, has_left, mine_v + stage <= last, mine_v + stage),
        ):

            def relay(row):
                gather_copy(right, group, row).wait_recv()

                @pl.when(able)
                def _():
                    gather_copy(right, group, row).start()

            over_rows(exists, relay)

    forward_rows(1)
    for right, at_last in ((True, mine_v == last), (False, mine_v == 0)):

        @pl.when(at_last)
        def _():
            square_copy(right).wait_recv()

    square_total[...] = square_ref[...]

    @pl.when(has_left)
    def _():
        square_total[...] = square_total[...] + square_recv[0]

    @pl.when(has_right)
    def _():
        square_total[...] = square_total[...] + square_recv[1]

    phase_copy.wait()
    for item in halo_copies:
        item.wait_recv()

    def react(number, carry):
        orient = orient_ref[number]
        kappa = [kappa_ref[dim, orient] for dim in range(3)]
        for plane in range(width):
            value = phase_ref[number, plane]
            low = low_halo[number] if plane == 0 else phase_ref[number, plane - 1]
            high = high_halo[number] if plane == width - 1 else phase_ref[number, plane + 1]
            twice = 2.0 * value
            laplace = kappa[0] * (low + high - twice)
            laplace = laplace + kappa[1] * (
                pltpu.roll(value, 1, 0) + pltpu.roll(value, ny - 1, 0) - twice
            )
            laplace = laplace + kappa[2] * (
                pltpu.roll(value, 1, 1) + pltpu.roll(value, nz - 1, 1) - twice
            )
            square = value * value
            chemical = twice - 6.0 * square + 4.0 * square * value
            chemical = chemical + 2.0 * CROSS_COUPLING * value * (square_total[plane] - square)
            base_ref[number, plane] = value - TIME_STEP * (chemical - laplace)
        return carry

    shares = max(last - 1, 1)
    for share in range(shares):
        begin, end = count * share // shares, count * (share + 1) // shares
        lax.fori_loop(begin, end, react, 0)
        if share + 2 < groups:
            forward_rows(share + 2)

    out_ref[...] = gathered[...]
    for item in halo_copies + cross_copies + back_copies:
        item.wait_send()
    for right in (True, False):
        for turn in range(last):
            for part in range(pieces):

                @pl.when(sends_sum(right, turn))
                def _():
                    sum_copy(right, turn, part).wait_send()

    for right, able in ((True, has_right), (False, has_left)):

        @pl.when(able)
        def _():
            square_copy(right).wait_send()

        for stage in range(groups):
            group = mine_v - stage if right else mine_v + stage
            exists = able & ((mine_v >= stage) if right else (mine_v + stage <= last))
            over_rows(exists, lambda row: gather_copy(right, group, row).wait_send())


def update_kernel(
    family_ref, eps_ref, hat_ref, phase_ref, base_ref, y_ref, z_ref, next_ref, stress_ref
):
    count, width, ny, nz = next_ref.shape
    first = pl.program_id(0) * count
    half = nz // 2
    size = 2 * width * ny

    @pl.when(pl.program_id(0) == 0)
    def _():
        first_column = first_lane((size, half))

        def transform_pair(pair, carry):
            modes = [hat_ref[:, pl.ds(2 * pair + side, 1)].reshape(size, half) for side in range(2)]
            both = table_left(y_ref, jnp.concatenate(modes, axis=1))
            lines = []
            for side in range(2):
                lanes = slice(side * half, (side + 1) * half)
                picked = jnp.where(first_column, both[size:, lanes], both[:size, lanes])
                lines.append(jnp.concatenate([picked[: size // 2], picked[size // 2 :]], axis=1))
            planes = table_right(jnp.concatenate(lines), z_ref)
            stress_ref[pl.ds(2 * pair, 2)] = planes.reshape(2, width, ny, nz)
            return carry

        lax.fori_loop(0, 3, transform_pair, 0)

    step = 16

    def finish(index, carry):
        plane = index // (ny // step)
        rows = pl.ds(pl.multiple_of(index % (ny // step) * step, step), step)
        stress = [stress_ref[comp, plane, rows, :] for comp in range(6)]
        for number in range(count):
            family = family_ref[first + number]
            total = eps_ref[0, family] * stress[0]
            for comp in range(1, 6):
                factor = eps_ref[comp, family] * (1.0 if comp < 3 else 2.0)
                total = total + factor * stress[comp]
            value = phase_ref[first + number, plane, rows, :]
            next_ref[number, plane, rows, :] = (
                base_ref[first + number, plane, rows, :] + (2.0 * TIME_STEP) * value * total
            )
        return carry

    lax.fori_loop(0, width * (ny // step), finish, 0)


def body(phase_field, kappa_table, eps_table, orient_index, family_index):
    slabs = lax.axis_size("gx")
    groups = lax.axis_size("vert")
    count, width, ny, nz = phase_field.shape
    half = nz // 2
    if slabs * groups != ny or width * 2 != 8 or half % 128 or ny % 16 or groups < 2:
        return general_body(phase_field, kappa_table, eps_table, orient_index, family_index)
    f32 = jnp.float32
    y_forward, y_inverse = (split_table(table) for table in y_tables(ny, width))
    z_forward, z_inverse = (split_table(table) for table in z_tables(nz))
    x_forward, x_inverse = (split_table(table) for table in x_tables(slabs, width))
    tile = (6, 2 * width, half)
    hat, square = pl.pallas_call(
        spectrum_kernel,
        out_shape=(
            jax.ShapeDtypeStruct((ny, *tile), f32),
            jax.ShapeDtypeStruct((width, ny, nz), f32),
        ),
        grid=(width,),
        in_specs=[
            SMEM_SPEC, SMEM_SPEC, pl.BlockSpec((count, 1, ny, nz), lambda i: (0, i, 0, 0)),
            VMEM_SPEC, VMEM_SPEC,
        ],
        out_specs=(VMEM_SPEC, VMEM_SPEC),
        scratch_shapes=[pltpu.VMEM((6, width, ny, nz), f32)],
        compiler_params=pltpu.CompilerParams(vmem_limit_bytes=VMEM_LIMIT),
        name="spectrum",
    )(family_index, eps_table.T, phase_field, z_forward, y_forward)
    dma = pltpu.SemaphoreType.DMA
    halo = (count, ny, nz)
    pieces = 2 if slabs % 2 == 0 else 1
    hat, base, phase = pl.pallas_call(
        exchange_kernel,
        out_shape=(
            pltpu.VMEM((ny, *tile), f32),
            pltpu.VMEM(phase_field.shape, f32),
            pltpu.VMEM(phase_field.shape, f32),
        ),
        in_specs=[SMEM_SPEC, SMEM_SPEC, VMEM_SPEC, ANY_SPEC, VMEM_SPEC, VMEM_SPEC, VMEM_SPEC],
        out_specs=(VMEM_SPEC, VMEM_SPEC, VMEM_SPEC),
        scratch_shapes=[
            dma,
            *[pltpu.VMEM((groups - 1, slabs, *tile), f32) for _ in range(4)],
            *[pltpu.VMEM((slabs, *tile), f32) for _ in range(3)],
            pltpu.VMEM((ny, *tile), f32),
            pltpu.VMEM(halo, f32), pltpu.VMEM(halo, f32),
            pltpu.VMEM((2, width, ny, nz), f32), pltpu.VMEM((2, width, ny, nz), f32),
            pltpu.VMEM((width, ny, nz), f32),
            dma((2, groups - 1, pieces)), dma((2, groups - 1, pieces)),
            dma((slabs - 1,)), dma((slabs - 1,)),
            dma((slabs - 1,)), dma((slabs - 1,)),
            dma((2, groups, slabs)), dma((2, groups, slabs)),
            dma((2,)), dma((2,)),
            dma((2,)), dma((2,)),
        ],
        compiler_params=pltpu.CompilerParams(
            vmem_limit_bytes=16 * 1024 * 1024, collective_id=0, has_side_effects=True
        ),
        name="exchange",
    )(orient_index, kappa_table.T, hat, phase_field, square, x_forward, x_inverse)
    steps = 4 if count % 4 == 0 else 1
    block = pl.BlockSpec((count // steps, width, ny, nz), lambda i: (i, 0, 0, 0))
    phase_next, stress = pl.pallas_call(
        update_kernel,
        grid=(steps,),
        out_shape=(
            jax.ShapeDtypeStruct(phase_field.shape, f32),
            jax.ShapeDtypeStruct((6, width, ny, nz), f32),
        ),
        in_specs=[SMEM_SPEC, SMEM_SPEC, VMEM_SPEC, VMEM_SPEC, VMEM_SPEC, VMEM_SPEC, VMEM_SPEC],
        out_specs=(block, pl.BlockSpec((6, width, ny, nz), lambda i: (0, 0, 0, 0))),
        compiler_params=pltpu.CompilerParams(vmem_limit_bytes=16 * 1024 * 1024),
        name="update",
    )(family_index, eps_table.T, hat, phase, base, y_inverse, z_inverse)
    return (phase_next, stress)


def solution(mesh):
    return jax.shard_map(
        body,
        mesh=mesh,
        in_specs=(P("vert", "gx", None, None), P(), P(), P("vert"), P("vert")),
        out_specs=(P("vert", "gx", None, None), P(None, "gx", None, None)),
        check_vma=False,
    )
```

```python
import functools
import math

import jax
import jax.numpy as jnp
import ml_dtypes
import numpy as np
from jax import lax
from jax.experimental import pallas as pl
from jax.experimental.pallas import tpu as pltpu
from jax.sharding import PartitionSpec as P

LAME_LAMBDA = 1.5
SHEAR_MOD = 1.0
TIME_STEP = 0.1
CROSS_COUPLING = 0.02
HIGHEST = lax.Precision.HIGHEST
TENSOR_SLOTS = ((0, 5, 4), (5, 1, 3), (4, 3, 2))
VOIGT_PAIRS = ((0, 0), (1, 1), (2, 2), (1, 2), (0, 2), (0, 1))
PAIRED_FORMS = {1: "pcxyz,pxqk->qckyz", 2: "pcxyz,pyqk->qcxkz", 3: "pcxyz,pzqk->qcxyk"}


def with_halo(block, sides, width):
    for axis, dim in sides:
        count = lax.axis_size(axis)
        forward = [(i, i + 1) for i in range(count - 1)]
        forward.append((count - 1, 0))
        backward = [(target, source) for source, target in forward]
        low = lax.ppermute(
            lax.slice_in_dim(block, block.shape[dim] - width, None, axis=dim), axis, forward
        )
        high = lax.ppermute(lax.slice_in_dim(block, 0, width, axis=dim), axis, backward)
        block = jnp.concatenate([low, block, high], axis=dim)
    return block


def signed_wave(first_row, row_count, full_count):
    positions = first_row + jnp.arange(row_count, dtype=jnp.int32)
    shifted = jnp.where(positions * 2 >= full_count, positions - full_count, positions)
    return shifted.astype(jnp.float32) / full_count


def wave_normals(x_wave, y_wave, z_wave):
    x_grid = x_wave[:, None, None]
    y_grid = y_wave[None, :, None]
    z_grid = z_wave[None, None, :]
    length_sq = x_grid * x_grid + y_grid * y_grid + z_grid * z_grid
    positive = length_sq > 0
    safe_length = jnp.where(positive, length_sq, 1.0)
    inverse_len = jnp.where(positive, lax.rsqrt(safe_length), 0.0)
    return [x_grid * inverse_len, y_grid * inverse_len, z_grid * inverse_len]


def green_stress(strain, normals):
    trace_strain = strain[0] + strain[1] + strain[2]
    stiffened = [
        (
            LAME_LAMBDA * trace_strain + 2.0 * SHEAR_MOD * strain[number]
            if number < 3
            else 2.0 * SHEAR_MOD * strain[number]
        )
        for number in range(6)
    ]
    traction = [
        sum(
            (
                stiffened[TENSOR_SLOTS[row_axis][col_axis]] * normals[col_axis]
                for col_axis in range(3)
            )
        )
        for row_axis in range(3)
    ]
    normal_part = normals[0] * traction[0] + normals[1] * traction[1] + normals[2] * traction[2]
    coupling = (LAME_LAMBDA + SHEAR_MOD) / (LAME_LAMBDA + 2.0 * SHEAR_MOD)
    shifted = [
        (traction[row_axis] - normals[row_axis] * normal_part * coupling) / SHEAR_MOD
        for row_axis in range(3)
    ]
    excess = [
        0.5
        * (
            normals[VOIGT_PAIRS[number][0]] * shifted[VOIGT_PAIRS[number][1]]
            + normals[VOIGT_PAIRS[number][1]] * shifted[VOIGT_PAIRS[number][0]]
        )
        - strain[number]
        for number in range(6)
    ]
    trace_excess = excess[0] + excess[1] + excess[2]
    result = [
        (
            LAME_LAMBDA * trace_excess + 2.0 * SHEAR_MOD * excess[number]
            if number < 3
            else 2.0 * SHEAR_MOD * excess[number]
        )
        for number in range(6)
    ]
    return result


def reaction_update(variant, laplace, driving, square_sum):
    chemical = 2.0 * variant - 6.0 * variant * variant + 4.0 * variant * variant * variant
    chemical = chemical + 2.0 * CROSS_COUPLING * variant * (square_sum - variant * variant)
    chemical = chemical - 2.0 * variant * driving - laplace
    return variant - TIME_STEP * chemical


def dft_tables(length):
    positions = jnp.arange(length, dtype=jnp.int32)
    products = positions[:, None] * positions[None, :] % length
    angles = products.astype(jnp.float32) * (2.0 * math.pi / length)
    return (jnp.cos(angles), jnp.sin(angles))


def paired_table(length, inverse):
    cosine_table, sine_table = dft_tables(length)
    cross_term = sine_table if inverse else -sine_table
    from_real = jnp.stack([cosine_table, cross_term], axis=1)
    from_imag = jnp.stack([-cross_term, cosine_table], axis=1)
    table = jnp.stack([from_real, from_imag])
    if inverse:
        table = table * (1.0 / length)
    return table


def transform(real_part, imag_part, axis_dim, inverse):
    length = real_part.shape[axis_dim]
    table = paired_table(length, inverse)
    if imag_part is None:
        pattern = PAIRED_FORMS[axis_dim].replace("p", "")
        result = jnp.einsum(pattern, real_part, table[0], precision=HIGHEST)
        return (result[0], result[1])
    stacked = jnp.stack([real_part, imag_part])
    result = jnp.einsum(PAIRED_FORMS[axis_dim], stacked, table, precision=HIGHEST)
    return (result[0], result[1])


def transform_real(real_part, imag_part, axis_dim):
    length = real_part.shape[axis_dim]
    table = paired_table(length, True)[:, :, 0, :]
    pattern = PAIRED_FORMS[axis_dim].replace("q", "")
    stacked = jnp.stack([real_part, imag_part])
    return jnp.einsum(pattern, stacked, table, precision=HIGHEST)


def forward_x(halves):
    return transform(halves[0], halves[1], 1, False)


def forward_y(halves):
    return transform(halves[0], halves[1], 2, False)


def backward_x(halves):
    return transform(halves[0], halves[1], 1, True)


def backward_z(halves):
    return transform_real(halves[0], halves[1], 3)


def general_body(phase_field, kappa_table, eps_table, orient_index, family_index):
    slab_count = lax.axis_size("gx")
    count_var, slab_width, width_y, width_z = phase_field.shape
    total_x = slab_width * slab_count
    family_hot = (
        family_index[:, None] == jnp.arange(eps_table.shape[0], dtype=jnp.int32)[None, :]
    ).astype(jnp.float32)
    orient_hot = (
        orient_index[:, None] == jnp.arange(kappa_table.shape[0], dtype=jnp.int32)[None, :]
    ).astype(jnp.float32)
    eps_var = jnp.dot(family_hot, eps_table, precision=HIGHEST)
    kappa_var = jnp.dot(orient_hot, kappa_table, precision=HIGHEST)
    padded = with_halo(phase_field, (("gx", 1),), 1)
    squared = phase_field * phase_field
    eigen_sum = jnp.einsum("vk,vxyz->kxyz", eps_var, squared, precision=HIGHEST)
    local_square = jnp.sum(squared, axis=0)
    eigen_sum = lax.psum_scatter(eigen_sum, "vert", scatter_dimension=2, tiled=True)
    square_sum = lax.psum(local_square, "vert")
    real_part, imag_part = transform(eigen_sum, None, 3, False)
    real_part, imag_part = forward_x(
        (
            lax.all_to_all(real_part, "gx", split_axis=3, concat_axis=1, tiled=True),
            lax.all_to_all(imag_part, "gx", split_axis=3, concat_axis=1, tiled=True),
        )
    )
    real_part, imag_part = forward_y(
        (
            lax.all_to_all(real_part, "vert", split_axis=1, concat_axis=2, tiled=True),
            lax.all_to_all(imag_part, "vert", split_axis=1, concat_axis=2, tiled=True),
        )
    )
    x_start = lax.axis_index("vert") * real_part.shape[1]
    z_start = lax.axis_index("gx") * real_part.shape[3]
    normals = wave_normals(
        signed_wave(x_start, real_part.shape[1], total_x),
        signed_wave(0, width_y, width_y),
        signed_wave(z_start, real_part.shape[3], width_z),
    )
    real_part = jnp.stack(green_stress(real_part, normals))
    imag_part = jnp.stack(green_stress(imag_part, normals))
    real_part, imag_part = transform(real_part, imag_part, 2, True)
    real_part, imag_part = backward_x(
        (
            lax.all_to_all(real_part, "vert", split_axis=2, concat_axis=1, tiled=True),
            lax.all_to_all(imag_part, "vert", split_axis=2, concat_axis=1, tiled=True),
        )
    )
    stress = backward_z(
        (
            lax.all_to_all(real_part, "gx", split_axis=1, concat_axis=3, tiled=True),
            lax.all_to_all(imag_part, "gx", split_axis=1, concat_axis=3, tiled=True),
        )
    )
    stress = lax.all_gather(stress, "vert", axis=2, tiled=True)
    weights = jnp.array([1.0, 1.0, 1.0, 2.0, 2.0, 2.0], jnp.float32)
    driving = jnp.einsum("vk,kxyz->vxyz", eps_var * weights[None, :], stress, precision=HIGHEST)
    kappa_x = kappa_var[:, 0][:, None, None, None]
    kappa_y = kappa_var[:, 1][:, None, None, None]
    kappa_z = kappa_var[:, 2][:, None, None, None]
    laplace = kappa_x * (padded[:, 2:] + padded[:, :-2] - 2.0 * phase_field)
    laplace = laplace + kappa_y * (
        jnp.roll(phase_field, 1, 2) + jnp.roll(phase_field, -1, 2) - 2.0 * phase_field
    )
    laplace = laplace + kappa_z * (
        jnp.roll(phase_field, 1, 3) + jnp.roll(phase_field, -1, 3) - 2.0 * phase_field
    )
    phase_next = reaction_update(phase_field, laplace, driving, square_sum[None])
    return (phase_next, stress)


MESH = pl.DeviceIdType.MESH
VMEM_SPEC = pl.BlockSpec(memory_space=pltpu.VMEM)
SMEM_SPEC = pl.BlockSpec(memory_space=pltpu.SMEM)
HBM_SPEC = pl.BlockSpec(memory_space=pltpu.HBM)
VMEM_LIMIT = 20 * 1024 * 1024
SOLVE_LAG = 2


def split_table(table):
    high = table.astype(np.float32).astype(ml_dtypes.bfloat16)
    low = (table - high.astype(np.float64)).astype(np.float32).astype(ml_dtypes.bfloat16)
    return jnp.asarray(np.stack([high, low]))


def trig(length):
    positions = np.arange(length)
    angles = (positions[:, None] * positions[None, :] % length) * (2.0 * np.pi / length)
    return np.cos(angles), np.sin(angles)


def z_tables(length):
    half = length // 2
    cosine, sine = trig(length)
    forward = np.concatenate([cosine[:, : half + 1], -sine[:, 1:half]], axis=1)
    weight = np.full(length, 2.0)
    weight[[0, half]] = 1.0
    inverse = forward.T * weight[:, None] / length
    return forward, inverse


def y_tables(length, width, order):
    half = length // 2
    cosine, sine = trig(length)
    eye = np.eye(width)
    full = np.array([[cosine, sine], [-sine, cosine]])
    edge = np.zeros_like(full)
    low, high, ends = slice(1, half), slice(half + 1, length), [0, half]
    edge[0, 0, low], edge[1, 0, low] = cosine[low], -sine[low]
    edge[0, 1, high], edge[1, 1, high] = cosine[high], -sine[high]
    edge[0, 0, ends], edge[1, 1, ends] = cosine[ends], cosine[ends]
    weight = np.full(length, 2.0)
    weight[ends] = 1.0
    forward, inverse = [], []
    size = 2 * width * length
    for table, scale in ((full, np.ones(length)), (edge, weight)):
        grid = np.einsum("abky,xw->kaxbwy", table, eye)[order]
        forward.append(grid.reshape(size, size))
        grid = np.einsum("abky,xw,k->bwykax", table, eye, scale / length)[:, :, :, order]
        inverse.append(grid.reshape(size, size))
    return np.concatenate(forward), np.concatenate(inverse)


def x_tables(slabs, width):
    length = slabs * width
    cosine, sine = (part.reshape(length, slabs, width) for part in trig(length))
    zero = np.zeros_like(cosine)
    from_real = np.stack([np.stack([cosine, zero], 2), np.stack([-sine, zero], 2)])
    from_imag = np.stack([np.stack([zero, sine], 2), np.stack([zero, cosine], 2)])
    rows = np.stack([from_real, from_imag])
    forward = rows.reshape(4 * length, 2 * length)
    inverse = (rows[0] + rows[1]).reshape(2 * length, 2 * length).T / length
    return forward, inverse


def halves(value):
    high = value.astype(jnp.bfloat16)
    return high, (value - high.astype(jnp.float32)).astype(jnp.bfloat16)


def mm(left, right):
    return jnp.dot(left, right, preferred_element_type=jnp.float32)


def table_left(table_ref, value):
    high, low = halves(value)
    return mm(table_ref[0], high) + (mm(table_ref[0], low) + mm(table_ref[1], high))


def table_right(value, table_ref):
    high, low = halves(value)
    return mm(high, table_ref[0]) + (mm(low, table_ref[0]) + mm(high, table_ref[1]))


def first_lane(shape):
    return lax.broadcasted_iota(jnp.int32, shape, len(shape) - 1) == 0


def signed(position, full):
    return jnp.where(position * 2 >= full, position - full, position)


def unit_normals(x_mode, y_mode, z_mode, sizes):
    pair = []
    for flip in (False, True):
        waves = []
        for mode, full in zip((x_mode, y_mode, z_mode), sizes):
            wave = signed(mode, full)
            if flip:
                wave = jnp.where(mode * 2 == full, -wave, wave)
            waves.append(wave.astype(jnp.float32) * (1.0 / full))
        length_sq = waves[0] * waves[0] + waves[1] * waves[1] + waves[2] * waves[2]
        positive = length_sq > 0
        inverse = jnp.where(positive, lax.rsqrt(jnp.where(positive, length_sq, 1.0)), 0.0)
        pair.append([wave * inverse for wave in waves])
    return pair


def transform_kernel(
    family_ref, orient_ref, eps_ref, kappa_ref, phase_hbm, z_hbm, y_hbm, forward_hbm, inverse_hbm,
    gathered, base_ref, phase_ref, square_total,
    z_ref, y_ref, forward_ref, inverse_ref,
    eigen_ref, hat_ref, right_recv, left_recv, cross_recv, cross_out, low_halo, high_halo,
    square_ref, square_recv, square_out,
    plane_sem, table_sem, sum_send_sem, sum_recv_sem, cross_send_sem, cross_recv_sem,
    back_send_sem, back_recv_sem, gather_send_sem, gather_recv_sem,
    square_send_sem, square_recv_sem, halo_send_sem, halo_recv_sem,
):
    slabs = lax.axis_size("gx")
    groups = lax.axis_size("vert")
    mine_x = lax.axis_index("gx")
    mine_v = lax.axis_index("vert")
    count, width, ny, nz = phase_ref.shape
    nx = slabs * width
    half = nz // 2
    last = groups - 1
    chunks = sum_send_sem.shape[2]
    piece = slabs // chunks
    step = 32

    def at(axis, offset):
        if axis == "gx":
            return lax.rem(mine_x + offset, slabs)
        return lax.rem(mine_v + offset, groups)

    def copy_to(src, dst, send_sem, recv_sem, axis, place):
        return pltpu.make_async_remote_copy(
            src_ref=src, dst_ref=dst, send_sem=send_sem, recv_sem=recv_sem,
            device_id={axis: place}, device_id_type=MESH,
        )

    def copy(src, dst, send_sem, recv_sem, axis, offset):
        return copy_to(src, dst, send_sem, recv_sem, axis, at(axis, offset))

    plane_copies = [
        pltpu.make_async_copy(phase_hbm.at[:, plane], phase_ref.at[:, plane], plane_sem.at[plane])
        for plane in range(width)
    ]
    for item in plane_copies:
        item.start()
    table_copies = [
        pltpu.make_async_copy(src, dst, table_sem.at[index])
        for index, (src, dst) in enumerate((
            (z_hbm, z_ref), (y_hbm, y_ref), (forward_hbm, forward_ref), (inverse_hbm, inverse_ref),
        ))
    ]
    for item in table_copies:
        item.start()

    has_left = mine_v > 0
    has_right = mine_v < last
    barrier = pltpu.get_barrier_semaphore()
    for offset in range(1, slabs):
        pl.semaphore_signal(barrier, inc=1, device_id={"gx": at("gx", offset)}, device_id_type=MESH)

    @pl.when(has_left)
    def _():
        pl.semaphore_signal(
            barrier, inc=1, device_id={"vert": at("vert", last)}, device_id_type=MESH
        )

    @pl.when(has_right)
    def _():
        pl.semaphore_signal(barrier, inc=1, device_id={"vert": at("vert", 1)}, device_id_type=MESH)

    for plane in range(width):
        plane_copies[plane].wait()

        def accumulate(index, carry):
            rows = pl.ds(pl.multiple_of(index * step, step), step)
            sums = [jnp.zeros((step, nz), jnp.float32) for _ in range(7)]
            for number in range(count):
                value = phase_ref[number, plane, rows, :]
                value = value * value
                family = family_ref[number]
                for comp in range(6):
                    sums[comp] = sums[comp] + eps_ref[comp, family] * value
                sums[6] = sums[6] + value
            for comp in range(6):
                eigen_ref[comp, plane, rows, :] = sums[comp]
            square_ref[plane, rows, :] = sums[6]
            return carry

        lax.fori_loop(0, ny // step, accumulate, 0)

    pl.semaphore_wait(barrier, slabs - 1 + jnp.where(has_left, 1, 0) + jnp.where(has_right, 1, 0))
    halo_copies = [
        copy(phase_ref.at[:, width - 1], low_halo, halo_send_sem.at[0], halo_recv_sem.at[0], "gx", 1),
        copy(phase_ref.at[:, 0], high_halo, halo_send_sem.at[1], halo_recv_sem.at[1], "gx", slabs - 1),
    ]
    for item in halo_copies:
        item.start()
    for item in table_copies:
        item.wait()
    size = 2 * width * ny
    first = first_lane((size, half))

    def transform_pair(pair, carry):
        rows = width * ny
        lines = table_right(eigen_ref[pl.ds(2 * pair, 2)].reshape(2 * rows, nz), z_ref)
        upper, lower = lines[:rows], lines[rows:]
        columns = [
            jnp.concatenate([upper[:, :half], upper[:, half:]]),
            jnp.concatenate([lower[:, :half], lower[:, half:]]),
        ]
        both = table_left(y_ref, jnp.concatenate(columns, axis=1))
        for side in range(2):
            lanes = slice(side * half, (side + 1) * half)
            picked = jnp.where(first, both[size:, lanes], both[:size, lanes])
            hat_ref[:, pl.ds(2 * pair + side, 1)] = picked.reshape(ny, 1, 2 * width, half)
        return carry

    lax.fori_loop(0, 3, transform_pair, 0)

    def way_of(right):
        if right:
            return right_recv, 0, 1, mine_v == 0
        return left_recv, 1, last, mine_v == last

    def rows_of(group, chunk):
        return pl.ds(group * slabs + chunk * piece, piece)

    def sum_copy(right, turn, chunk):
        recv, way, offset, _ = way_of(right)
        owner = last - turn if right else turn
        return copy(
            hat_ref.at[rows_of(owner, chunk)], recv.at[turn, pl.ds(chunk * piece, piece)],
            sum_send_sem.at[way, turn, chunk], sum_recv_sem.at[way, turn, chunk], "vert", offset,
        )

    def sends_sum(right, turn):
        return mine_v < last - turn if right else mine_v > turn

    def add_sum(right, turn, chunk):
        owner = last - turn if right else turn
        rows = rows_of(owner, chunk)
        sum_copy(right, turn, chunk).wait_recv()
        hat_ref[rows] = hat_ref[rows] + way_of(right)[0][turn, pl.ds(chunk * piece, piece)]

    def pass_sums(right, chunk):
        at_end = way_of(right)[3]
        for turn in range(last):

            @pl.when(jnp.logical_not(at_end) & sends_sum(right, turn))
            def _():
                add_sum(right, turn, chunk)
                sum_copy(right, turn, chunk).start()

    def end_sums(chunk):
        @pl.when(has_left)
        def _():
            add_sum(True, last - mine_v, chunk)

        @pl.when(has_right)
        def _():
            add_sum(False, mine_v, chunk)

    def source_of(chunk, member):
        return chunk + member * chunks

    my_chunk = lax.rem(mine_x, chunks)
    my_place = my_chunk * piece + mine_x // chunks
    mine = mine_v * slabs + my_place

    def cross_copy(place, source, target):
        return copy_to(
            hat_ref.at[mine_v * slabs + place], cross_recv.at[source],
            cross_send_sem.at[place], cross_recv_sem.at[source], "gx", target,
        )

    def back_copy(place, target):
        return copy_to(
            cross_out.at[target], gathered.at[mine_v * slabs + place],
            back_send_sem.at[target], back_recv_sem.at[place], "gx", target,
        )

    def send_cross(chunk):
        for member in range(piece):
            target = source_of(chunk, member)
            place = chunk * piece + member

            @pl.when(target != mine_x)
            def _():
                cross_copy(place, mine_x, target).start()

            @pl.when(target == mine_x)
            def _():
                cross_recv[mine_x] = hat_ref[mine_v * slabs + place]

    def over_others(action):
        def one(offset, carry):
            action(at("gx", offset))
            return carry

        lax.fori_loop(1, slabs, one, 0)

    def solve_row():
        shape = (nx, half)
        y_mode = jnp.full(shape, 0, jnp.int32) + (mine_v * slabs + mine_x)
        x_mode = lax.broadcasted_iota(jnp.int32, shape, 0)
        lane = lax.broadcasted_iota(jnp.int32, shape, 1)
        ends = (y_mode == 0) | (y_mode * 2 == ny)
        upper = y_mode * 2 > ny
        edge = lane == 0
        z_first = jnp.where(edge & upper, half, lane)
        z_second = jnp.where(edge & (upper | ends), half, lane)
        normal_sets = [
            unit_normals(x_mode, y_mode, z_mode, (nx, ny, nz)) for z_mode in (z_first, z_second)
        ]
        over_others(lambda source: cross_copy(0, source, source).wait_recv())
        parts = []
        for comp in range(6):
            modes = table_left(forward_ref, cross_recv[:, comp].reshape(2 * nx, half))
            parts.append([modes[i * nx : (i + 1) * nx] for i in range(4)])
        stresses = []
        for part in range(2):
            total = None
            for source in range(2):
                strain = [parts[comp][2 * source + part] for comp in range(6)]
                for normals in normal_sets[source]:
                    value = green_stress(strain, normals)
                    total = value if total is None else [a + b for a, b in zip(total, value)]
            stresses.append([0.5 * value for value in total])
        for comp in range(6):
            lines = table_left(inverse_ref, jnp.concatenate([stresses[0][comp], stresses[1][comp]]))
            cross_out[:, comp] = lines.reshape(slabs, 2 * width, half)
        over_others(lambda target: back_copy(my_place, target).start())
        gathered[mine] = cross_out[mine_x]

    def gather_copy(right, group, chunk):
        way = 0 if right else 1
        place = gathered.at[rows_of(group, chunk)]
        return copy(
            place, place, gather_send_sem.at[way, group, chunk],
            gather_recv_sem.at[way, group, chunk], "vert", 1 if right else last,
        )

    def send_gather(chunk):
        for member in range(piece):
            source = source_of(chunk, member)

            @pl.when(source != mine_x)
            def _():
                back_copy(chunk * piece + member, source).wait_recv()

        for right, able in ((True, has_right), (False, has_left)):

            @pl.when(able)
            def _():
                gather_copy(right, mine_v, chunk).start()

    def relay_gather(stage, chunk):
        for right, able, exists, group in (
            (True, has_right, mine_v >= stage, mine_v - stage),
            (False, has_left, mine_v + stage <= last, mine_v + stage),
        ):

            @pl.when(exists)
            def _():
                gather_copy(right, group, chunk).wait_recv()

                @pl.when(able)
                def _():
                    gather_copy(right, group, chunk).start()

    def square_copy(right, src=None):
        way = 0 if right else 1
        return copy(
            square_out.at[way] if src is None else src, square_recv.at[way],
            square_send_sem.at[way], square_recv_sem.at[way], "vert", 1 if right else last,
        )

    def square_hop(hop):
        for right in (True, False):
            way = 0 if right else 1

            @pl.when(mine_v == (hop if right else last - hop))
            def _():
                if hop == 0:
                    square_copy(right, square_ref).start()
                else:
                    square_copy(right).wait_recv()
                    square_out[way] = square_ref[...] + square_recv[way]
                    square_copy(right).start()

    def react(number, carry):
        orient = orient_ref[number]
        kappa = [kappa_ref[dim, orient] for dim in range(3)]
        for plane in range(width):
            value = phase_ref[number, plane]
            low = low_halo[number] if plane == 0 else phase_ref[number, plane - 1]
            high = high_halo[number] if plane == width - 1 else phase_ref[number, plane + 1]
            twice = 2.0 * value
            laplace = kappa[0] * (low + high - twice)
            laplace = laplace + kappa[1] * (
                pltpu.roll(value, 1, 0) + pltpu.roll(value, ny - 1, 0) - twice
            )
            laplace = laplace + kappa[2] * (
                pltpu.roll(value, 1, 1) + pltpu.roll(value, nz - 1, 1) - twice
            )
            square = value * value
            chemical = twice - 6.0 * square + 4.0 * square * value
            chemical = chemical - 2.0 * CROSS_COUPLING * value * square
            base_ref[number, plane] = value - TIME_STEP * (chemical - laplace)
        return carry

    for right in (True, False):

        @pl.when(way_of(right)[3])
        def _():
            def one(chunk, carry):
                for turn in range(last):
                    sum_copy(right, turn, chunk).start()
                return carry

            lax.fori_loop(0, chunks, one, 0)

    square_hop(0)
    lower = mine_v * 2 < groups
    gather_lag = SOLVE_LAG + 2
    slots = chunks + gather_lag + last
    share = -(-count // (slots - gather_lag))

    def slot(number, carry):
        @pl.when(number < chunks)
        def _():
            @pl.when(lower)
            def _():
                pass_sums(True, number)

            @pl.when(jnp.logical_not(lower))
            def _():
                pass_sums(False, number)

        @pl.when((number >= 1) & (number <= chunks))
        def _():
            @pl.when(lower)
            def _():
                pass_sums(False, number - 1)

            @pl.when(jnp.logical_not(lower))
            def _():
                pass_sums(True, number - 1)

            end_sums(number - 1)
            send_cross(number - 1)

        @pl.when(number == my_chunk + SOLVE_LAG)
        def _():
            solve_row()

        @pl.when((number >= gather_lag) & (number < gather_lag + chunks))
        def _():
            send_gather(number - gather_lag)

        for stage in range(1, groups):

            @pl.when((number >= gather_lag + stage) & (number < gather_lag + stage + chunks))
            def _():
                relay_gather(stage, number - gather_lag - stage)

        for hop in range(1, last):

            @pl.when(number == chunks - 1 + 2 * hop)
            def _():
                square_hop(hop)

        @pl.when(number == gather_lag)
        def _():
            for item in halo_copies:
                item.wait_recv()

        @pl.when(number >= gather_lag)
        def _():
            begin = (number - gather_lag) * share
            lax.fori_loop(
                jnp.minimum(begin, count), jnp.minimum(begin + share, count), react, 0
            )

        return carry

    lax.fori_loop(0, slots, slot, 0)
    for right, at_last in ((True, mine_v == last), (False, mine_v == 0)):

        @pl.when(at_last)
        def _():
            square_copy(right).wait_recv()

    square_total[...] = square_ref[...]

    @pl.when(has_left)
    def _():
        square_total[...] = square_total[...] + square_recv[0]

    @pl.when(has_right)
    def _():
        square_total[...] = square_total[...] + square_recv[1]

    for item in halo_copies:
        item.wait_send()

    def end_cross(place, carry):
        target = source_of(place // piece, lax.rem(place, piece))

        @pl.when(target != mine_x)
        def _():
            cross_copy(place, mine_x, target).wait_send()

        return carry

    lax.fori_loop(0, slabs, end_cross, 0)
    over_others(lambda target: back_copy(my_place, target).wait_send())

    def end_chunk(chunk, carry):
        for right, able in ((True, has_right), (False, has_left)):
            for turn in range(last):

                @pl.when(sends_sum(right, turn))
                def _():
                    sum_copy(right, turn, chunk).wait_send()

            for stage in range(groups):
                group = mine_v - stage if right else mine_v + stage
                exists = able & ((mine_v >= stage) if right else (mine_v + stage <= last))

                @pl.when(exists)
                def _():
                    gather_copy(right, group, chunk).wait_send()

        return carry

    lax.fori_loop(0, chunks, end_chunk, 0)
    for right, able in ((True, has_right), (False, has_left)):

        @pl.when(able)
        def _():
            square_copy(right).wait_send()


def update_kernel(
    family_ref, eps_ref, hat_ref, phase_ref, base_ref, square_ref, y_ref, z_ref,
    next_ref, stress_ref, lines_ref,
):
    count, _, ny, nz = next_ref.shape
    width = square_ref.shape[0]
    plane = pl.program_id(0)
    half = nz // 2
    size = 2 * width * ny

    @pl.when(plane == 0)
    def _():
        first_column = first_lane((size, half))

        def transform_pair(pair, carry):
            modes = [hat_ref[:, pl.ds(2 * pair + side, 1)].reshape(size, half) for side in range(2)]
            both = table_left(y_ref, jnp.concatenate(modes, axis=1))
            for side in range(2):
                lanes = slice(side * half, (side + 1) * half)
                picked = jnp.where(first_column, both[size:, lanes], both[:size, lanes])
                lines = jnp.concatenate([picked[: size // 2], picked[size // 2 :]], axis=1)
                lines_ref[pl.ds(2 * pair + side, 1)] = lines.reshape(1, width, ny, nz)
            return carry

        lax.fori_loop(0, 3, transform_pair, 0)

    lines = lines_ref[:, pl.ds(plane, 1)].reshape(6 * ny, nz)
    stress_ref[...] = table_right(lines, z_ref).reshape(6, 1, ny, nz)
    step = 16

    def finish(index, carry):
        rows = pl.ds(pl.multiple_of(index * step, step), step)
        stress = [stress_ref[comp, 0, rows, :] for comp in range(6)]
        shared = (-2.0 * TIME_STEP * CROSS_COUPLING) * square_ref[plane, rows, :]
        for number in range(count):
            family = family_ref[number]
            total = shared
            for comp in range(6):
                factor = eps_ref[comp, family] * (2.0 * TIME_STEP * (1.0 if comp < 3 else 2.0))
                total = total + factor * stress[comp]
            value = phase_ref[number, plane, rows, :]
            next_ref[number, 0, rows, :] = base_ref[number, plane, rows, :] + value * total
        return carry

    lax.fori_loop(0, ny // step, finish, 0)


def body(phase_field, kappa_table, eps_table, orient_index, family_index):
    slabs = lax.axis_size("gx")
    groups = lax.axis_size("vert")
    count, width, ny, nz = phase_field.shape
    half = nz // 2
    whole_rows = slabs * groups == ny and slabs % 2 == 0 and groups >= 2
    if not whole_rows or width * 2 != 8 or half % 128 or ny % 32:
        return general_body(phase_field, kappa_table, eps_table, orient_index, family_index)
    f32 = jnp.float32
    chunks = slabs // 2
    places = np.arange(slabs)
    order = np.concatenate([
        group * slabs + places // 2 + chunks * (places % 2) for group in range(groups)
    ])
    y_forward, y_inverse = (split_table(table) for table in y_tables(ny, width, order))
    z_forward, z_inverse = (split_table(table) for table in z_tables(nz))
    x_forward, x_inverse = (split_table(table) for table in x_tables(slabs, width))
    tile = (6, 2 * width, half)
    dma = pltpu.SemaphoreType.DMA
    halo = (count, ny, nz)
    squares = (width, ny, nz)
    tables = (z_forward, y_forward, x_forward, x_inverse)
    in_place = functools.partial(pltpu.with_memory_space_constraint, memory_space=pltpu.HBM)
    small = [in_place(item) for item in (family_index, orient_index, eps_table.T, kappa_table.T)]
    hat, base, phase, square = pl.pallas_call(
        transform_kernel,
        out_shape=(
            pltpu.VMEM((ny, *tile), f32),
            pltpu.VMEM(phase_field.shape, f32),
            pltpu.VMEM(phase_field.shape, f32),
            pltpu.VMEM(squares, f32),
        ),
        in_specs=[SMEM_SPEC] * 4 + [HBM_SPEC] * 5,
        out_specs=(VMEM_SPEC,) * 4,
        scratch_shapes=[
            *[pltpu.VMEM(table.shape, table.dtype) for table in tables],
            pltpu.VMEM((6, *squares), f32),
            pltpu.VMEM((ny, *tile), f32),
            *[pltpu.VMEM((groups - 1, slabs, *tile), f32) for _ in range(2)],
            *[pltpu.VMEM((slabs, *tile), f32) for _ in range(2)],
            pltpu.VMEM(halo, f32), pltpu.VMEM(halo, f32),
            pltpu.VMEM(squares, f32),
            pltpu.VMEM((2, *squares), f32), pltpu.VMEM((2, *squares), f32),
            dma((width,)), dma((len(tables),)),
            dma((2, groups - 1, chunks)), dma((2, groups - 1, chunks)),
            dma((slabs,)), dma((slabs,)),
            dma((slabs,)), dma((slabs,)),
            dma((2, groups, chunks)), dma((2, groups, chunks)),
            dma((2,)), dma((2,)),
            dma((2,)), dma((2,)),
        ],
        compiler_params=pltpu.CompilerParams(
            vmem_limit_bytes=VMEM_LIMIT, collective_id=0, has_side_effects=True
        ),
        name="transform",
    )(*small, in_place(phase_field), *[in_place(table) for table in tables])
    phase_next, stress = pl.pallas_call(
        update_kernel,
        grid=(width,),
        out_shape=(
            jax.ShapeDtypeStruct(phase_field.shape, f32),
            jax.ShapeDtypeStruct((6, width, ny, nz), f32),
        ),
        in_specs=[SMEM_SPEC] * 2 + [VMEM_SPEC] * 6,
        out_specs=(
            pl.BlockSpec((count, 1, ny, nz), lambda i: (0, i, 0, 0)),
            pl.BlockSpec((6, 1, ny, nz), lambda i: (0, i, 0, 0)),
        ),
        scratch_shapes=[pltpu.VMEM((6, width, ny, nz), f32)],
        compiler_params=pltpu.CompilerParams(vmem_limit_bytes=VMEM_LIMIT),
        name="update",
    )(small[0], small[2], hat, phase, base, square, y_inverse, z_inverse)
    return (phase_next, stress)


def solution(mesh):
    return jax.shard_map(
        body,
        mesh=mesh,
        in_specs=(P("vert", "gx", None, None), P(), P(), P("vert"), P("vert")),
        out_specs=(P("vert", "gx", None, None), P(None, "gx", None, None)),
        check_vma=False,
    )
```

```python
import functools
import math

import jax
import jax.numpy as jnp
import ml_dtypes
import numpy as np
from jax import lax
from jax.experimental import pallas as pl
from jax.experimental.pallas import tpu as pltpu
from jax.sharding import PartitionSpec as P

LAME_LAMBDA = 1.5
SHEAR_MOD = 1.0
TIME_STEP = 0.1
CROSS_COUPLING = 0.02
HIGHEST = lax.Precision.HIGHEST
TENSOR_SLOTS = ((0, 5, 4), (5, 1, 3), (4, 3, 2))
VOIGT_PAIRS = ((0, 0), (1, 1), (2, 2), (1, 2), (0, 2), (0, 1))
PAIRED_FORMS = {1: "pcxyz,pxqk->qckyz", 2: "pcxyz,pyqk->qcxkz", 3: "pcxyz,pzqk->qcxyk"}


def with_halo(block, sides, width):
    for axis, dim in sides:
        count = lax.axis_size(axis)
        forward = [(i, i + 1) for i in range(count - 1)]
        forward.append((count - 1, 0))
        backward = [(target, source) for source, target in forward]
        low = lax.ppermute(
            lax.slice_in_dim(block, block.shape[dim] - width, None, axis=dim), axis, forward
        )
        high = lax.ppermute(lax.slice_in_dim(block, 0, width, axis=dim), axis, backward)
        block = jnp.concatenate([low, block, high], axis=dim)
    return block


def signed_wave(first_row, row_count, full_count):
    positions = first_row + jnp.arange(row_count, dtype=jnp.int32)
    shifted = jnp.where(positions * 2 >= full_count, positions - full_count, positions)
    return shifted.astype(jnp.float32) / full_count


def wave_normals(x_wave, y_wave, z_wave):
    x_grid = x_wave[:, None, None]
    y_grid = y_wave[None, :, None]
    z_grid = z_wave[None, None, :]
    length_sq = x_grid * x_grid + y_grid * y_grid + z_grid * z_grid
    positive = length_sq > 0
    safe_length = jnp.where(positive, length_sq, 1.0)
    inverse_len = jnp.where(positive, lax.rsqrt(safe_length), 0.0)
    return [x_grid * inverse_len, y_grid * inverse_len, z_grid * inverse_len]


def green_stress(strain, normals):
    trace_strain = strain[0] + strain[1] + strain[2]
    stiffened = [
        (
            LAME_LAMBDA * trace_strain + 2.0 * SHEAR_MOD * strain[number]
            if number < 3
            else 2.0 * SHEAR_MOD * strain[number]
        )
        for number in range(6)
    ]
    traction = [
        sum(
            (
                stiffened[TENSOR_SLOTS[row_axis][col_axis]] * normals[col_axis]
                for col_axis in range(3)
            )
        )
        for row_axis in range(3)
    ]
    normal_part = normals[0] * traction[0] + normals[1] * traction[1] + normals[2] * traction[2]
    coupling = (LAME_LAMBDA + SHEAR_MOD) / (LAME_LAMBDA + 2.0 * SHEAR_MOD)
    shifted = [
        (traction[row_axis] - normals[row_axis] * normal_part * coupling) / SHEAR_MOD
        for row_axis in range(3)
    ]
    excess = [
        0.5
        * (
            normals[VOIGT_PAIRS[number][0]] * shifted[VOIGT_PAIRS[number][1]]
            + normals[VOIGT_PAIRS[number][1]] * shifted[VOIGT_PAIRS[number][0]]
        )
        - strain[number]
        for number in range(6)
    ]
    trace_excess = excess[0] + excess[1] + excess[2]
    result = [
        (
            LAME_LAMBDA * trace_excess + 2.0 * SHEAR_MOD * excess[number]
            if number < 3
            else 2.0 * SHEAR_MOD * excess[number]
        )
        for number in range(6)
    ]
    return result


def reaction_update(variant, laplace, driving, square_sum):
    chemical = 2.0 * variant - 6.0 * variant * variant + 4.0 * variant * variant * variant
    chemical = chemical + 2.0 * CROSS_COUPLING * variant * (square_sum - variant * variant)
    chemical = chemical - 2.0 * variant * driving - laplace
    return variant - TIME_STEP * chemical


def dft_tables(length):
    positions = jnp.arange(length, dtype=jnp.int32)
    products = positions[:, None] * positions[None, :] % length
    angles = products.astype(jnp.float32) * (2.0 * math.pi / length)
    return (jnp.cos(angles), jnp.sin(angles))


def paired_table(length, inverse):
    cosine_table, sine_table = dft_tables(length)
    cross_term = sine_table if inverse else -sine_table
    from_real = jnp.stack([cosine_table, cross_term], axis=1)
    from_imag = jnp.stack([-cross_term, cosine_table], axis=1)
    table = jnp.stack([from_real, from_imag])
    if inverse:
        table = table * (1.0 / length)
    return table


def transform(real_part, imag_part, axis_dim, inverse):
    length = real_part.shape[axis_dim]
    table = paired_table(length, inverse)
    if imag_part is None:
        pattern = PAIRED_FORMS[axis_dim].replace("p", "")
        result = jnp.einsum(pattern, real_part, table[0], precision=HIGHEST)
        return (result[0], result[1])
    stacked = jnp.stack([real_part, imag_part])
    result = jnp.einsum(PAIRED_FORMS[axis_dim], stacked, table, precision=HIGHEST)
    return (result[0], result[1])


def transform_real(real_part, imag_part, axis_dim):
    length = real_part.shape[axis_dim]
    table = paired_table(length, True)[:, :, 0, :]
    pattern = PAIRED_FORMS[axis_dim].replace("q", "")
    stacked = jnp.stack([real_part, imag_part])
    return jnp.einsum(pattern, stacked, table, precision=HIGHEST)


def forward_x(halves):
    return transform(halves[0], halves[1], 1, False)


def forward_y(halves):
    return transform(halves[0], halves[1], 2, False)


def backward_x(halves):
    return transform(halves[0], halves[1], 1, True)


def backward_z(halves):
    return transform_real(halves[0], halves[1], 3)


def general_body(phase_field, kappa_table, eps_table, orient_index, family_index):
    slab_count = lax.axis_size("gx")
    count_var, slab_width, width_y, width_z = phase_field.shape
    total_x = slab_width * slab_count
    family_hot = (
        family_index[:, None] == jnp.arange(eps_table.shape[0], dtype=jnp.int32)[None, :]
    ).astype(jnp.float32)
    orient_hot = (
        orient_index[:, None] == jnp.arange(kappa_table.shape[0], dtype=jnp.int32)[None, :]
    ).astype(jnp.float32)
    eps_var = jnp.dot(family_hot, eps_table, precision=HIGHEST)
    kappa_var = jnp.dot(orient_hot, kappa_table, precision=HIGHEST)
    padded = with_halo(phase_field, (("gx", 1),), 1)
    squared = phase_field * phase_field
    eigen_sum = jnp.einsum("vk,vxyz->kxyz", eps_var, squared, precision=HIGHEST)
    local_square = jnp.sum(squared, axis=0)
    eigen_sum = lax.psum_scatter(eigen_sum, "vert", scatter_dimension=2, tiled=True)
    square_sum = lax.psum(local_square, "vert")
    real_part, imag_part = transform(eigen_sum, None, 3, False)
    real_part, imag_part = forward_x(
        (
            lax.all_to_all(real_part, "gx", split_axis=3, concat_axis=1, tiled=True),
            lax.all_to_all(imag_part, "gx", split_axis=3, concat_axis=1, tiled=True),
        )
    )
    real_part, imag_part = forward_y(
        (
            lax.all_to_all(real_part, "vert", split_axis=1, concat_axis=2, tiled=True),
            lax.all_to_all(imag_part, "vert", split_axis=1, concat_axis=2, tiled=True),
        )
    )
    x_start = lax.axis_index("vert") * real_part.shape[1]
    z_start = lax.axis_index("gx") * real_part.shape[3]
    normals = wave_normals(
        signed_wave(x_start, real_part.shape[1], total_x),
        signed_wave(0, width_y, width_y),
        signed_wave(z_start, real_part.shape[3], width_z),
    )
    real_part = jnp.stack(green_stress(real_part, normals))
    imag_part = jnp.stack(green_stress(imag_part, normals))
    real_part, imag_part = transform(real_part, imag_part, 2, True)
    real_part, imag_part = backward_x(
        (
            lax.all_to_all(real_part, "vert", split_axis=2, concat_axis=1, tiled=True),
            lax.all_to_all(imag_part, "vert", split_axis=2, concat_axis=1, tiled=True),
        )
    )
    stress = backward_z(
        (
            lax.all_to_all(real_part, "gx", split_axis=1, concat_axis=3, tiled=True),
            lax.all_to_all(imag_part, "gx", split_axis=1, concat_axis=3, tiled=True),
        )
    )
    stress = lax.all_gather(stress, "vert", axis=2, tiled=True)
    weights = jnp.array([1.0, 1.0, 1.0, 2.0, 2.0, 2.0], jnp.float32)
    driving = jnp.einsum("vk,kxyz->vxyz", eps_var * weights[None, :], stress, precision=HIGHEST)
    kappa_x = kappa_var[:, 0][:, None, None, None]
    kappa_y = kappa_var[:, 1][:, None, None, None]
    kappa_z = kappa_var[:, 2][:, None, None, None]
    laplace = kappa_x * (padded[:, 2:] + padded[:, :-2] - 2.0 * phase_field)
    laplace = laplace + kappa_y * (
        jnp.roll(phase_field, 1, 2) + jnp.roll(phase_field, -1, 2) - 2.0 * phase_field
    )
    laplace = laplace + kappa_z * (
        jnp.roll(phase_field, 1, 3) + jnp.roll(phase_field, -1, 3) - 2.0 * phase_field
    )
    phase_next = reaction_update(phase_field, laplace, driving, square_sum[None])
    return (phase_next, stress)


MESH = pl.DeviceIdType.MESH
VMEM_SPEC = pl.BlockSpec(memory_space=pltpu.VMEM)
SMEM_SPEC = pl.BlockSpec(memory_space=pltpu.SMEM)
HBM_SPEC = pl.BlockSpec(memory_space=pltpu.HBM)
VMEM_LIMIT = 20 * 1024 * 1024
SUM_LAG = 2
SOLVE_LAG = 3
GATHER_LAG = 5
SQUARE_SLOTS = (0, 1, 3)
REACT_SLOT = 4
SPREAD = 4


def split_table(table):
    high = table.astype(np.float32).astype(ml_dtypes.bfloat16)
    low = (table - high.astype(np.float64)).astype(np.float32).astype(ml_dtypes.bfloat16)
    return jnp.asarray(np.stack([high, low]))


def stacked_table(table):
    high, low = split_table(table)
    return jnp.concatenate([high, high, low], axis=1)


def trig(length):
    positions = np.arange(length)
    angles = (positions[:, None] * positions[None, :] % length) * (2.0 * np.pi / length)
    return np.cos(angles), np.sin(angles)


def z_tables(length):
    half = length // 2
    cosine, sine = trig(length)
    forward = np.concatenate([cosine[:, : half + 1], -sine[:, 1:half]], axis=1)
    weight = np.full(length, 2.0)
    weight[[0, half]] = 1.0
    inverse = forward.T * weight[:, None] / length
    return forward, inverse


def y_tables(length, width, order):
    half = length // 2
    cosine, sine = trig(length)
    eye = np.eye(width)
    full = np.array([[cosine, sine], [-sine, cosine]])
    edge = np.zeros_like(full)
    low, high, ends = slice(1, half), slice(half + 1, length), [0, half]
    edge[0, 0, low], edge[1, 0, low] = cosine[low], -sine[low]
    edge[0, 1, high], edge[1, 1, high] = cosine[high], -sine[high]
    edge[0, 0, ends], edge[1, 1, ends] = cosine[ends], cosine[ends]
    weight = np.full(length, 2.0)
    weight[ends] = 1.0
    forward, inverse = [], []
    size = 2 * width * length
    for table, scale in ((full, np.ones(length)), (edge, weight)):
        grid = np.einsum("abky,xw->kaxbwy", table, eye)[order]
        forward.append(grid.reshape(size, size))
        grid = np.einsum("abky,xw,k->bwykax", table, eye, scale / length)[:, :, :, order]
        inverse.append(grid.reshape(size, size))
    return np.concatenate(forward), np.concatenate(inverse)


def x_tables(slabs, width):
    length = slabs * width
    cosine, sine = (part.reshape(length, slabs, width) for part in trig(length))
    zero = np.zeros_like(cosine)
    from_real = np.stack([np.stack([cosine, zero], 2), np.stack([-sine, zero], 2)])
    from_imag = np.stack([np.stack([zero, sine], 2), np.stack([zero, cosine], 2)])
    rows = np.stack([from_real, from_imag])
    forward = rows.reshape(4 * length, 2 * length)
    inverse = (rows[0] + rows[1]).reshape(2 * length, 2 * length).T / length
    return forward, inverse


def halves(value):
    high = value.astype(jnp.bfloat16)
    return high, (value - high.astype(jnp.float32)).astype(jnp.bfloat16)


def mm(left, right):
    return jnp.dot(left, right, preferred_element_type=jnp.float32)


def table_right(value, table_ref):
    high, low = halves(value)
    return mm(high, table_ref[0]) + (mm(low, table_ref[0]) + mm(high, table_ref[1]))


def stack_rows(value):
    high, low = halves(value)
    return jnp.concatenate([high, low, high])


def table_product(table_ref, high, low):
    return mm(table_ref[0], high) + (mm(table_ref[0], low) + mm(table_ref[1], high))


def lane_is(shape, number):
    return lax.broadcasted_iota(jnp.int32, shape, len(shape) - 1) == number


def to_lane(value, number):
    return pltpu.roll(value, number, 1) if number else value


def from_lane(value, number):
    return pltpu.roll(value, value.shape[1] - number, 1) if number else value


def first_lane(shape):
    return lax.broadcasted_iota(jnp.int32, shape, len(shape) - 1) == 0


def signed(position, full):
    return jnp.where(position * 2 >= full, position - full, position)


def unit_normals(x_mode, y_mode, z_mode, sizes):
    pair = []
    for flip in (False, True):
        waves = []
        for mode, full in zip((x_mode, y_mode, z_mode), sizes):
            wave = signed(mode, full)
            if flip:
                wave = jnp.where(mode * 2 == full, -wave, wave)
            waves.append(wave.astype(jnp.float32) * (1.0 / full))
        length_sq = waves[0] * waves[0] + waves[1] * waves[1] + waves[2] * waves[2]
        positive = length_sq > 0
        inverse = jnp.where(positive, lax.rsqrt(jnp.where(positive, length_sq, 1.0)), 0.0)
        pair.append([wave * inverse for wave in waves])
    return pair


def transform_kernel(
    family_ref, orient_ref, eps_ref, kappa_ref, phase_hbm, z_hbm, y_hbm, forward_hbm, inverse_hbm,
    gathered, base_ref, phase_ref, square_total,
    z_ref, y_ref, forward_ref, inverse_ref,
    eigen_ref, line_high, line_low, end_high, end_low, hat_ref, right_recv, left_recv, cross_recv, cross_out, low_halo, high_halo,
    square_ref, square_recv, square_out,
    plane_sem, table_sem, sum_send_sem, sum_recv_sem, cross_send_sem, cross_recv_sem,
    back_send_sem, back_recv_sem, gather_send_sem, gather_recv_sem, spread_send_sem,
    square_send_sem, square_recv_sem, halo_send_sem, halo_recv_sem,
):
    slabs = lax.axis_size("gx")
    groups = lax.axis_size("vert")
    mine_x = lax.axis_index("gx")
    mine_v = lax.axis_index("vert")
    count, width, ny, nz = phase_ref.shape
    nx = slabs * width
    half = nz // 2
    last = groups - 1
    chunks = sum_send_sem.shape[2]
    piece = slabs // chunks
    relayed = max(chunks - SPREAD, 0)
    at_end = (mine_v == 0) | (mine_v == last)
    step = 32

    def at(axis, offset):
        if axis == "gx":
            return lax.rem(mine_x + offset, slabs)
        return lax.rem(mine_v + offset, groups)

    def copy_to(src, dst, send_sem, recv_sem, axis, place):
        return pltpu.make_async_remote_copy(
            src_ref=src, dst_ref=dst, send_sem=send_sem, recv_sem=recv_sem,
            device_id={axis: place}, device_id_type=MESH,
        )

    def copy(src, dst, send_sem, recv_sem, axis, offset):
        return copy_to(src, dst, send_sem, recv_sem, axis, at(axis, offset))

    plane_copies = [
        pltpu.make_async_copy(phase_hbm.at[:, plane], phase_ref.at[:, plane], plane_sem.at[plane])
        for plane in range(width)
    ]
    table_copies = [
        pltpu.make_async_copy(src, dst, table_sem.at[index])
        for index, (src, dst) in enumerate((
            (z_hbm, z_ref), (y_hbm, y_ref), (forward_hbm, forward_ref), (inverse_hbm, inverse_ref),
        ))
    ]
    for item in table_copies[:1] + plane_copies + table_copies[1:]:
        item.start()

    has_left = mine_v > 0
    has_right = mine_v < last
    barrier = pltpu.get_barrier_semaphore()
    for offset in range(1, slabs):
        pl.semaphore_signal(barrier, inc=1, device_id={"gx": at("gx", offset)}, device_id_type=MESH)

    for offset in range(1, groups):
        pl.semaphore_signal(
            barrier, inc=1, device_id={"vert": at("vert", offset)}, device_id_type=MESH
        )

    table_copies[0].wait()
    lane_shape = (ny, half)
    for plane in range(width):
        plane_copies[plane].wait()
        sums = [jnp.zeros((ny, nz), jnp.float32) for _ in range(7)]
        for number in range(count):
            value = phase_ref[number, plane]
            value = value * value
            family = family_ref[number]
            for comp in range(6):
                sums[comp] = sums[comp] + eps_ref[comp, family] * value
            sums[6] = sums[6] + value
        for comp in range(6):
            eigen_ref[comp] = sums[comp]
        square_ref[plane] = sums[6]
        lines = table_right(eigen_ref[...].reshape(6 * ny, nz), z_ref)
        for part in range(2):
            rows = pl.ds((part * width + plane) * ny, ny)
            ends = jnp.zeros(lane_shape, jnp.float32)
            for comp in range(6):
                block = lines[comp * ny : (comp + 1) * ny, part * half : (part + 1) * half]
                lanes = pl.ds(comp % 2 * half, half)
                line_high[comp // 2, rows, lanes], line_low[comp // 2, rows, lanes] = halves(block)
                ends = jnp.where(lane_is(lane_shape, comp), to_lane(block, comp), ends)
            end_high[rows, :], end_low[rows, :] = halves(ends)

    pl.semaphore_wait(barrier, slabs + groups - 2)
    halo_copies = [
        copy(phase_ref.at[:, width - 1], low_halo, halo_send_sem.at[0], halo_recv_sem.at[0], "gx", 1),
        copy(phase_ref.at[:, 0], high_halo, halo_send_sem.at[1], halo_recv_sem.at[1], "gx", slabs - 1),
    ]
    def square_copy(right, src=None):
        way = 0 if right else 1
        return copy(
            square_out.at[way] if src is None else src, square_recv.at[way],
            square_send_sem.at[way], square_recv_sem.at[way], "vert", 1 if right else last,
        )

    def square_hop(hop):
        for right in (True, False):
            way = 0 if right else 1

            @pl.when(mine_v == (hop if right else last - hop))
            def _():
                if hop == 0:
                    square_copy(right, square_ref).start()
                else:
                    square_copy(right).wait_recv()
                    square_out[way] = square_ref[...] + square_recv[way]
                    square_copy(right).start()

    square_hop(0)
    for item in halo_copies:
        item.start()
    for item in table_copies[1:]:
        item.wait()
    size = 2 * width * ny
    first = first_lane((size, half))
    full_table, edge_table = (y_ref.at[:, pl.ds(index * size, size)] for index in range(2))

    end_modes = table_product(edge_table, end_high[...], end_low[...])
    for pair in range(3):
        modes = table_product(full_table, line_high[pair], line_low[pair])
        for side in range(2):
            comp = 2 * pair + side
            lanes = slice(side * half, (side + 1) * half)
            picked = jnp.where(first, from_lane(end_modes, comp), modes[:, lanes])
            hat_ref[:, comp] = picked.reshape(ny, 2 * width, half)

    def way_of(right):
        if right:
            return right_recv, 0, 1, mine_v == 0
        return left_recv, 1, last, mine_v == last

    def rows_of(group, chunk):
        return pl.ds(group * slabs + chunk * piece, piece)

    def sum_copy(right, turn, chunk):
        recv, way, offset, _ = way_of(right)
        owner = last - turn if right else turn
        return copy(
            hat_ref.at[rows_of(owner, chunk)], recv.at[turn, pl.ds(chunk * piece, piece)],
            sum_send_sem.at[way, turn, chunk], sum_recv_sem.at[way, turn, chunk], "vert", offset,
        )

    def sends_sum(right, turn):
        return mine_v < last - turn if right else mine_v > turn

    def add_sum(right, turn, chunk):
        owner = last - turn if right else turn
        rows = rows_of(owner, chunk)
        sum_copy(right, turn, chunk).wait_recv()
        hat_ref[rows] = hat_ref[rows] + way_of(right)[0][turn, pl.ds(chunk * piece, piece)]

    def during(number, begin, length, action):
        @pl.when((number >= begin) & (number < begin + length))
        def _():
            action(number - begin)

    def pass_sums(right, number):
        at_end = way_of(right)[3]
        for turn in range(last):

            def one(chunk):
                @pl.when(jnp.logical_not(at_end) & sends_sum(right, turn))
                def _():
                    add_sum(right, turn, chunk)
                    sum_copy(right, turn, chunk).start()

            during(number, turn, chunks, one)

    def end_sums(chunk):
        @pl.when(has_left)
        def _():
            add_sum(True, last - mine_v, chunk)

        @pl.when(has_right)
        def _():
            add_sum(False, mine_v, chunk)

    def source_of(chunk, member):
        return chunk + member * chunks

    my_chunk = lax.rem(mine_x, chunks)
    my_place = my_chunk * piece + mine_x // chunks
    mine = mine_v * slabs + my_place

    def cross_copy(place, source, target):
        return copy_to(
            hat_ref.at[mine_v * slabs + place], cross_recv.at[source],
            cross_send_sem.at[place], cross_recv_sem.at[source], "gx", target,
        )

    def back_copy(place, target):
        return copy_to(
            cross_out.at[target], gathered.at[mine_v * slabs + place],
            back_send_sem.at[target], back_recv_sem.at[place], "gx", target,
        )

    def send_cross(chunk):
        for member in range(piece):
            target = source_of(chunk, member)
            place = chunk * piece + member

            @pl.when(target != mine_x)
            def _():
                cross_copy(place, mine_x, target).start()

            @pl.when(target == mine_x)
            def _():
                cross_recv[mine_x] = hat_ref[mine_v * slabs + place]

    def over_others(action):
        def one(offset, carry):
            action(at("gx", offset))
            return carry

        lax.fori_loop(1, slabs, one, 0)

    def solve_row():
        shape = (nx, half)
        y_mode = jnp.full(shape, 0, jnp.int32) + (mine_v * slabs + mine_x)
        x_mode = lax.broadcasted_iota(jnp.int32, shape, 0)
        lane = lax.broadcasted_iota(jnp.int32, shape, 1)
        ends = (y_mode == 0) | (y_mode * 2 == ny)
        upper = y_mode * 2 > ny
        edge = lane == 0
        z_first = jnp.where(edge & upper, half, lane)
        z_second = jnp.where(edge & (upper | ends), half, lane)
        normal_sets = [
            unit_normals(x_mode, y_mode, z_mode, (nx, ny, nz)) for z_mode in (z_first, z_second)
        ]
        over_others(lambda source: cross_copy(0, source, source).wait_recv())
        lines = jnp.concatenate(
            [cross_recv[:, comp].reshape(2 * nx, half) for comp in range(6)], axis=1
        )
        modes = mm(forward_ref[...], stack_rows(lines))
        parts = [
            [modes[i * nx : (i + 1) * nx, comp * half : (comp + 1) * half] for i in range(4)]
            for comp in range(6)
        ]
        stresses = []
        for part in range(2):
            total = None
            for source in range(2):
                strain = [parts[comp][2 * source + part] for comp in range(6)]
                for normals in normal_sets[source]:
                    value = green_stress(strain, normals)
                    total = value if total is None else [a + b for a, b in zip(total, value)]
            stresses.append([0.5 * value for value in total])
        modes = jnp.concatenate([jnp.concatenate(part, axis=1) for part in stresses])
        lines = mm(inverse_ref[...], stack_rows(modes))
        for comp in range(6):
            block = lines[:, comp * half : (comp + 1) * half]
            cross_out[:, comp] = block.reshape(slabs, 2 * width, half)
        over_others(lambda target: back_copy(my_place, target).start())
        gathered[mine] = cross_out[mine_x]

    def gather_copy(right, group, chunk):
        way = 0 if right else 1
        place = gathered.at[rows_of(group, chunk)]
        return copy(
            place, place, gather_send_sem.at[way, group, chunk],
            gather_recv_sem.at[way, group, chunk], "vert", 1 if right else last,
        )

    def spread_copy(right, target, chunk):
        place = gathered.at[rows_of(mine_v, chunk)]
        return copy_to(
            place, place, spread_send_sem.at[target, chunk - relayed],
            gather_recv_sem.at[0 if right else 1, mine_v, chunk], "vert", target,
        )

    def over_targets(chunk, action):
        for distance in reversed(range(1, groups)):
            for right in (True, False):
                target = mine_v + distance if right else mine_v - distance

                @pl.when(target <= last if right else target >= 0)
                def _():
                    action(spread_copy(right, target, chunk))

    def send_gather(chunk):
        for member in range(piece):
            source = source_of(chunk, member)

            @pl.when(source != mine_x)
            def _():
                back_copy(chunk * piece + member, source).wait_recv()

        spread = at_end & (chunk >= relayed)

        @pl.when(jnp.logical_not(spread))
        def _():
            for right, able in ((True, has_right), (False, has_left)):

                @pl.when(able)
                def _():
                    gather_copy(right, mine_v, chunk).start()

        @pl.when(spread)
        def _():
            over_targets(chunk, lambda item: item.start())

    def end_spread(chunk, carry):
        for right, exists, group in ((True, has_left, 0), (False, has_right, last)):

            @pl.when(exists)
            def _():
                gather_copy(right, group, chunk).wait_recv()

        return carry

    def relay_gather(stage, chunk):
        for right, able, exists, group in (
            (True, has_right, mine_v >= stage, mine_v - stage),
            (False, has_left, mine_v + stage <= last, mine_v + stage),
        ):

            first_group = mine_v == stage if right else mine_v + stage == last

            @pl.when(exists & jnp.logical_not(first_group & (chunk >= relayed)))
            def _():
                gather_copy(right, group, chunk).wait_recv()

                @pl.when(able)
                def _():
                    gather_copy(right, group, chunk).start()

    def react(number, carry):
        orient = orient_ref[number]
        kappa = [kappa_ref[dim, orient] for dim in range(3)]
        for plane in range(width):
            value = phase_ref[number, plane]
            low = low_halo[number] if plane == 0 else phase_ref[number, plane - 1]
            high = high_halo[number] if plane == width - 1 else phase_ref[number, plane + 1]
            twice = 2.0 * value
            laplace = kappa[0] * (low + high - twice)
            laplace = laplace + kappa[1] * (
                pltpu.roll(value, 1, 0) + pltpu.roll(value, ny - 1, 0) - twice
            )
            laplace = laplace + kappa[2] * (
                pltpu.roll(value, 1, 1) + pltpu.roll(value, nz - 1, 1) - twice
            )
            square = value * value
            chemical = twice - 6.0 * square + 4.0 * square * value
            chemical = chemical - 2.0 * CROSS_COUPLING * value * square
            base_ref[number, plane] = value - TIME_STEP * (chemical - laplace)
        return carry

    for right in (True, False):

        @pl.when(way_of(right)[3])
        def _():
            def one(number, carry):
                for turn in range(last):
                    during(number, turn, chunks, lambda chunk: sum_copy(right, turn, chunk).start())
                return carry

            lax.fori_loop(0, chunks + last - 1, one, 0)

    lower = mine_v * 2 < groups
    share = 4
    slots = max(
        chunks + GATHER_LAG + last, REACT_SLOT - (-count // share), max(SQUARE_SLOTS) + groups
    )

    def slot(number, carry):
        for right in (True, False):

            @pl.when(lower if right else jnp.logical_not(lower))
            def _():
                pass_sums(right, number)
                pass_sums(not right, number - 1)

        def own(chunk):
            end_sums(chunk)
            send_cross(chunk)

        during(number, SUM_LAG, chunks, own)

        during(number, GATHER_LAG, chunks, send_gather)

        @pl.when(number == my_chunk + SOLVE_LAG)
        def _():
            solve_row()

        for stage in range(1, groups):
            during(number, GATHER_LAG + stage, chunks, lambda chunk: relay_gather(stage, chunk))
        for hop in range(1, last):

            @pl.when(number == SQUARE_SLOTS[min(hop, 2)] + max(hop - 2, 0))
            def _():
                square_hop(hop)

        @pl.when(number == REACT_SLOT)
        def _():
            for item in halo_copies:
                item.wait_recv()

        def react_share(index):
            begin = index * share
            lax.fori_loop(
                jnp.minimum(begin, count), jnp.minimum(begin + share, count), react, 0
            )

        during(number, REACT_SLOT, -(-count // share), react_share)
        return carry

    lax.fori_loop(0, slots, slot, 0)
    lax.fori_loop(relayed, chunks, end_spread, 0)
    for right, at_last in ((True, mine_v == last), (False, mine_v == 0)):

        @pl.when(at_last)
        def _():
            square_copy(right).wait_recv()

    square_total[...] = square_ref[...]

    @pl.when(has_left)
    def _():
        square_total[...] = square_total[...] + square_recv[0]

    @pl.when(has_right)
    def _():
        square_total[...] = square_total[...] + square_recv[1]

    for item in halo_copies:
        item.wait_send()

    def end_cross(place, carry):
        target = source_of(place // piece, lax.rem(place, piece))

        @pl.when(target != mine_x)
        def _():
            cross_copy(place, mine_x, target).wait_send()

        return carry

    lax.fori_loop(0, slabs, end_cross, 0)
    over_others(lambda target: back_copy(my_place, target).wait_send())

    def end_chunk(chunk, carry):
        for right, able in ((True, has_right), (False, has_left)):
            for turn in range(last):

                @pl.when(sends_sum(right, turn))
                def _():
                    sum_copy(right, turn, chunk).wait_send()

            for stage in range(groups):
                group = mine_v - stage if right else mine_v + stage
                exists = able & ((mine_v >= stage) if right else (mine_v + stage <= last))

                first_group = group == (0 if right else last)

                @pl.when(exists & jnp.logical_not(first_group & (chunk >= relayed)))
                def _():
                    gather_copy(right, group, chunk).wait_send()

        @pl.when(at_end & (chunk >= relayed))
        def _():
            over_targets(chunk, lambda item: item.wait_send())

        return carry

    lax.fori_loop(0, chunks, end_chunk, 0)
    for right, able in ((True, has_right), (False, has_left)):

        @pl.when(able)
        def _():
            square_copy(right).wait_send()


def update_kernel(
    family_ref, eps_ref, hat_ref, phase_ref, base_ref, square_ref, y_ref, z_ref,
    next_ref, stress_ref, lines_ref,
):
    count, _, ny, nz = next_ref.shape
    width = square_ref.shape[0]
    plane = pl.program_id(0)
    half = nz // 2
    size = 2 * width * ny

    @pl.when(plane == 0)
    def _():
        shape = (size, half)
        first = first_lane(shape)
        ends = jnp.zeros(shape, jnp.float32)
        for comp in range(6):
            block = hat_ref[:, comp].reshape(shape)
            ends = jnp.where(lane_is(shape, comp), to_lane(block, comp), ends)
        full_table, edge_table = (y_ref.at[:, pl.ds(index * size, size)] for index in range(2))
        end_lines = table_product(edge_table, *halves(ends))
        for pair in range(3):
            modes = [hat_ref[:, 2 * pair + side].reshape(shape) for side in range(2)]
            both = table_product(full_table, *halves(jnp.concatenate(modes, axis=1)))
            for side in range(2):
                comp = 2 * pair + side
                lanes = slice(side * half, (side + 1) * half)
                picked = jnp.where(first, from_lane(end_lines, comp), both[:, lanes])
                lines = jnp.concatenate([picked[: size // 2], picked[size // 2 :]], axis=1)
                lines_ref[comp] = lines.reshape(width, ny, nz)

    lines = lines_ref[:, pl.ds(plane, 1)].reshape(6 * ny, nz)
    stress_ref[...] = table_right(lines, z_ref).reshape(6, 1, ny, nz)
    step = 16

    def finish(index, carry):
        rows = pl.ds(pl.multiple_of(index * step, step), step)
        stress = [stress_ref[comp, 0, rows, :] for comp in range(6)]
        shared = (-2.0 * TIME_STEP * CROSS_COUPLING) * square_ref[plane, rows, :]
        for number in range(count):
            family = family_ref[number]
            total = shared
            for comp in range(6):
                factor = eps_ref[comp, family] * (2.0 * TIME_STEP * (1.0 if comp < 3 else 2.0))
                total = total + factor * stress[comp]
            value = phase_ref[number, plane, rows, :]
            next_ref[number, 0, rows, :] = base_ref[number, plane, rows, :] + value * total
        return carry

    lax.fori_loop(0, ny // step, finish, 0)


def body(phase_field, kappa_table, eps_table, orient_index, family_index):
    slabs = lax.axis_size("gx")
    groups = lax.axis_size("vert")
    count, width, ny, nz = phase_field.shape
    half = nz // 2
    whole_rows = slabs * groups == ny and slabs % 2 == 0 and groups >= 2
    if not whole_rows or width * 2 != 8 or half % 128 or ny % 32:
        return general_body(phase_field, kappa_table, eps_table, orient_index, family_index)
    f32 = jnp.float32
    chunks = slabs // 2
    places = np.arange(slabs)
    order = np.concatenate([
        group * slabs + places // 2 + chunks * (places % 2) for group in range(groups)
    ])
    y_forward, y_inverse = (split_table(table) for table in y_tables(ny, width, order))
    z_forward, z_inverse = (split_table(table) for table in z_tables(nz))
    x_forward, x_inverse = (stacked_table(table) for table in x_tables(slabs, width))
    tile = (6, 2 * width, half)
    dma = pltpu.SemaphoreType.DMA
    halo = (count, ny, nz)
    squares = (width, ny, nz)
    tables = (z_forward, y_forward, x_forward, x_inverse)
    in_place = functools.partial(pltpu.with_memory_space_constraint, memory_space=pltpu.HBM)
    small = [in_place(item) for item in (family_index, orient_index, eps_table.T, kappa_table.T)]
    hat, base, phase, square = pl.pallas_call(
        transform_kernel,
        out_shape=(
            pltpu.VMEM((ny, *tile), f32),
            pltpu.VMEM(phase_field.shape, f32),
            pltpu.VMEM(phase_field.shape, f32),
            pltpu.VMEM(squares, f32),
        ),
        in_specs=[SMEM_SPEC] * 4 + [HBM_SPEC] * 5,
        out_specs=(VMEM_SPEC,) * 4,
        scratch_shapes=[
            *[pltpu.VMEM(table.shape, table.dtype) for table in tables],
            pltpu.VMEM((6, ny, nz), f32),
            *[pltpu.VMEM((3, 2 * width * ny, nz), jnp.bfloat16) for _ in range(2)],
            *[pltpu.VMEM((2 * width * ny, half), jnp.bfloat16) for _ in range(2)],
            pltpu.VMEM((ny, *tile), f32),
            *[pltpu.VMEM((groups - 1, slabs, *tile), f32) for _ in range(2)],
            *[pltpu.VMEM((slabs, *tile), f32) for _ in range(2)],
            pltpu.VMEM(halo, f32), pltpu.VMEM(halo, f32),
            pltpu.VMEM(squares, f32),
            pltpu.VMEM((2, *squares), f32), pltpu.VMEM((2, *squares), f32),
            dma((width,)), dma((len(tables),)),
            dma((2, groups - 1, chunks)), dma((2, groups - 1, chunks)),
            dma((slabs,)), dma((slabs,)),
            dma((slabs,)), dma((slabs,)),
            dma((2, groups, chunks)), dma((2, groups, chunks)), dma((groups, max(min(SPREAD, chunks), 1))),
            dma((2,)), dma((2,)),
            dma((2,)), dma((2,)),
        ],
        compiler_params=pltpu.CompilerParams(
            vmem_limit_bytes=VMEM_LIMIT, collective_id=0, has_side_effects=True
        ),
        name="transform",
    )(*small, in_place(phase_field), *[in_place(table) for table in tables])
    phase_next, stress = pl.pallas_call(
        update_kernel,
        grid=(width,),
        out_shape=(
            jax.ShapeDtypeStruct(phase_field.shape, f32),
            jax.ShapeDtypeStruct((6, width, ny, nz), f32),
        ),
        in_specs=[SMEM_SPEC] * 2 + [VMEM_SPEC] * 6,
        out_specs=(
            pl.BlockSpec((count, 1, ny, nz), lambda i: (0, i, 0, 0)),
            pl.BlockSpec((6, 1, ny, nz), lambda i: (0, i, 0, 0)),
        ),
        scratch_shapes=[pltpu.VMEM((6, width, ny, nz), f32)],
        compiler_params=pltpu.CompilerParams(vmem_limit_bytes=VMEM_LIMIT),
        name="update",
    )(small[0], small[2], hat, phase, base, square, y_inverse, z_inverse)
    return (phase_next, stress)


def solution(mesh):
    return jax.shard_map(
        body,
        mesh=mesh,
        in_specs=(P("vert", "gx", None, None), P(), P(), P("vert"), P("vert")),
        out_specs=(P("vert", "gx", None, None), P(None, "gx", None, None)),
        check_vma=False,
    )
```

```python
import functools
import math

import jax
import jax.numpy as jnp
import ml_dtypes
import numpy as np
from jax import lax
from jax.experimental import pallas as pl
from jax.experimental.pallas import tpu as pltpu
from jax.sharding import PartitionSpec as P

LAME_LAMBDA = 1.5
SHEAR_MOD = 1.0
TIME_STEP = 0.1
CROSS_COUPLING = 0.02
HIGHEST = lax.Precision.HIGHEST
TENSOR_SLOTS = ((0, 5, 4), (5, 1, 3), (4, 3, 2))
VOIGT_PAIRS = ((0, 0), (1, 1), (2, 2), (1, 2), (0, 2), (0, 1))
PAIRED_FORMS = {1: "pcxyz,pxqk->qckyz", 2: "pcxyz,pyqk->qcxkz", 3: "pcxyz,pzqk->qcxyk"}


def with_halo(block, sides, width):
    for axis, dim in sides:
        count = lax.axis_size(axis)
        forward = [(i, i + 1) for i in range(count - 1)]
        forward.append((count - 1, 0))
        backward = [(target, source) for source, target in forward]
        low = lax.ppermute(
            lax.slice_in_dim(block, block.shape[dim] - width, None, axis=dim), axis, forward
        )
        high = lax.ppermute(lax.slice_in_dim(block, 0, width, axis=dim), axis, backward)
        block = jnp.concatenate([low, block, high], axis=dim)
    return block


def signed_wave(first_row, row_count, full_count):
    positions = first_row + jnp.arange(row_count, dtype=jnp.int32)
    shifted = jnp.where(positions * 2 >= full_count, positions - full_count, positions)
    return shifted.astype(jnp.float32) / full_count


def wave_normals(x_wave, y_wave, z_wave):
    x_grid = x_wave[:, None, None]
    y_grid = y_wave[None, :, None]
    z_grid = z_wave[None, None, :]
    length_sq = x_grid * x_grid + y_grid * y_grid + z_grid * z_grid
    positive = length_sq > 0
    safe_length = jnp.where(positive, length_sq, 1.0)
    inverse_len = jnp.where(positive, lax.rsqrt(safe_length), 0.0)
    return [x_grid * inverse_len, y_grid * inverse_len, z_grid * inverse_len]


def green_stress(strain, normals):
    trace_strain = strain[0] + strain[1] + strain[2]
    stiffened = [
        (
            LAME_LAMBDA * trace_strain + 2.0 * SHEAR_MOD * strain[number]
            if number < 3
            else 2.0 * SHEAR_MOD * strain[number]
        )
        for number in range(6)
    ]
    traction = [
        sum(
            (
                stiffened[TENSOR_SLOTS[row_axis][col_axis]] * normals[col_axis]
                for col_axis in range(3)
            )
        )
        for row_axis in range(3)
    ]
    normal_part = normals[0] * traction[0] + normals[1] * traction[1] + normals[2] * traction[2]
    coupling = (LAME_LAMBDA + SHEAR_MOD) / (LAME_LAMBDA + 2.0 * SHEAR_MOD)
    shifted = [
        (traction[row_axis] - normals[row_axis] * normal_part * coupling) / SHEAR_MOD
        for row_axis in range(3)
    ]
    excess = [
        0.5
        * (
            normals[VOIGT_PAIRS[number][0]] * shifted[VOIGT_PAIRS[number][1]]
            + normals[VOIGT_PAIRS[number][1]] * shifted[VOIGT_PAIRS[number][0]]
        )
        - strain[number]
        for number in range(6)
    ]
    trace_excess = excess[0] + excess[1] + excess[2]
    result = [
        (
            LAME_LAMBDA * trace_excess + 2.0 * SHEAR_MOD * excess[number]
            if number < 3
            else 2.0 * SHEAR_MOD * excess[number]
        )
        for number in range(6)
    ]
    return result


def reaction_update(variant, laplace, driving, square_sum):
    chemical = 2.0 * variant - 6.0 * variant * variant + 4.0 * variant * variant * variant
    chemical = chemical + 2.0 * CROSS_COUPLING * variant * (square_sum - variant * variant)
    chemical = chemical - 2.0 * variant * driving - laplace
    return variant - TIME_STEP * chemical


def dft_tables(length):
    positions = jnp.arange(length, dtype=jnp.int32)
    products = positions[:, None] * positions[None, :] % length
    angles = products.astype(jnp.float32) * (2.0 * math.pi / length)
    return (jnp.cos(angles), jnp.sin(angles))


def paired_table(length, inverse):
    cosine_table, sine_table = dft_tables(length)
    cross_term = sine_table if inverse else -sine_table
    from_real = jnp.stack([cosine_table, cross_term], axis=1)
    from_imag = jnp.stack([-cross_term, cosine_table], axis=1)
    table = jnp.stack([from_real, from_imag])
    if inverse:
        table = table * (1.0 / length)
    return table


def transform(real_part, imag_part, axis_dim, inverse):
    length = real_part.shape[axis_dim]
    table = paired_table(length, inverse)
    if imag_part is None:
        pattern = PAIRED_FORMS[axis_dim].replace("p", "")
        result = jnp.einsum(pattern, real_part, table[0], precision=HIGHEST)
        return (result[0], result[1])
    stacked = jnp.stack([real_part, imag_part])
    result = jnp.einsum(PAIRED_FORMS[axis_dim], stacked, table, precision=HIGHEST)
    return (result[0], result[1])


def transform_real(real_part, imag_part, axis_dim):
    length = real_part.shape[axis_dim]
    table = paired_table(length, True)[:, :, 0, :]
    pattern = PAIRED_FORMS[axis_dim].replace("q", "")
    stacked = jnp.stack([real_part, imag_part])
    return jnp.einsum(pattern, stacked, table, precision=HIGHEST)


def forward_x(halves):
    return transform(halves[0], halves[1], 1, False)


def forward_y(halves):
    return transform(halves[0], halves[1], 2, False)


def backward_x(halves):
    return transform(halves[0], halves[1], 1, True)


def backward_z(halves):
    return transform_real(halves[0], halves[1], 3)


def general_body(phase_field, kappa_table, eps_table, orient_index, family_index):
    slab_count = lax.axis_size("gx")
    count_var, slab_width, width_y, width_z = phase_field.shape
    total_x = slab_width * slab_count
    family_hot = (
        family_index[:, None] == jnp.arange(eps_table.shape[0], dtype=jnp.int32)[None, :]
    ).astype(jnp.float32)
    orient_hot = (
        orient_index[:, None] == jnp.arange(kappa_table.shape[0], dtype=jnp.int32)[None, :]
    ).astype(jnp.float32)
    eps_var = jnp.dot(family_hot, eps_table, precision=HIGHEST)
    kappa_var = jnp.dot(orient_hot, kappa_table, precision=HIGHEST)
    padded = with_halo(phase_field, (("gx", 1),), 1)
    squared = phase_field * phase_field
    eigen_sum = jnp.einsum("vk,vxyz->kxyz", eps_var, squared, precision=HIGHEST)
    local_square = jnp.sum(squared, axis=0)
    eigen_sum = lax.psum_scatter(eigen_sum, "vert", scatter_dimension=2, tiled=True)
    square_sum = lax.psum(local_square, "vert")
    real_part, imag_part = transform(eigen_sum, None, 3, False)
    real_part, imag_part = forward_x(
        (
            lax.all_to_all(real_part, "gx", split_axis=3, concat_axis=1, tiled=True),
            lax.all_to_all(imag_part, "gx", split_axis=3, concat_axis=1, tiled=True),
        )
    )
    real_part, imag_part = forward_y(
        (
            lax.all_to_all(real_part, "vert", split_axis=1, concat_axis=2, tiled=True),
            lax.all_to_all(imag_part, "vert", split_axis=1, concat_axis=2, tiled=True),
        )
    )
    x_start = lax.axis_index("vert") * real_part.shape[1]
    z_start = lax.axis_index("gx") * real_part.shape[3]
    normals = wave_normals(
        signed_wave(x_start, real_part.shape[1], total_x),
        signed_wave(0, width_y, width_y),
        signed_wave(z_start, real_part.shape[3], width_z),
    )
    real_part = jnp.stack(green_stress(real_part, normals))
    imag_part = jnp.stack(green_stress(imag_part, normals))
    real_part, imag_part = transform(real_part, imag_part, 2, True)
    real_part, imag_part = backward_x(
        (
            lax.all_to_all(real_part, "vert", split_axis=2, concat_axis=1, tiled=True),
            lax.all_to_all(imag_part, "vert", split_axis=2, concat_axis=1, tiled=True),
        )
    )
    stress = backward_z(
        (
            lax.all_to_all(real_part, "gx", split_axis=1, concat_axis=3, tiled=True),
            lax.all_to_all(imag_part, "gx", split_axis=1, concat_axis=3, tiled=True),
        )
    )
    stress = lax.all_gather(stress, "vert", axis=2, tiled=True)
    weights = jnp.array([1.0, 1.0, 1.0, 2.0, 2.0, 2.0], jnp.float32)
    driving = jnp.einsum("vk,kxyz->vxyz", eps_var * weights[None, :], stress, precision=HIGHEST)
    kappa_x = kappa_var[:, 0][:, None, None, None]
    kappa_y = kappa_var[:, 1][:, None, None, None]
    kappa_z = kappa_var[:, 2][:, None, None, None]
    laplace = kappa_x * (padded[:, 2:] + padded[:, :-2] - 2.0 * phase_field)
    laplace = laplace + kappa_y * (
        jnp.roll(phase_field, 1, 2) + jnp.roll(phase_field, -1, 2) - 2.0 * phase_field
    )
    laplace = laplace + kappa_z * (
        jnp.roll(phase_field, 1, 3) + jnp.roll(phase_field, -1, 3) - 2.0 * phase_field
    )
    phase_next = reaction_update(phase_field, laplace, driving, square_sum[None])
    return (phase_next, stress)


MESH = pl.DeviceIdType.MESH
VMEM_SPEC = pl.BlockSpec(memory_space=pltpu.VMEM)
SMEM_SPEC = pl.BlockSpec(memory_space=pltpu.SMEM)
HBM_SPEC = pl.BlockSpec(memory_space=pltpu.HBM)
VMEM_LIMIT = 20 * 1024 * 1024
SUM_LAG = 2
SOLVE_LAG = 3
GATHER_LAG = 5
SQUARE_SLOT = 0
SQUARE_LAG = 1
SQUARE_SPAN = 1
STEP = 16
BARRIER_PLANE = 1
REACT_SLOT = 4
SPREAD = 4


def split_table(table):
    high = table.astype(np.float32).astype(ml_dtypes.bfloat16)
    low = (table - high.astype(np.float64)).astype(np.float32).astype(ml_dtypes.bfloat16)
    return jnp.asarray(np.stack([high, low]))


def stacked_table(table):
    high, low = split_table(table)
    return jnp.concatenate([high, high, low], axis=1)


def trig(length):
    positions = np.arange(length)
    angles = (positions[:, None] * positions[None, :] % length) * (2.0 * np.pi / length)
    return np.cos(angles), np.sin(angles)


def z_tables(length):
    half = length // 2
    cosine, sine = trig(length)
    forward = np.concatenate([cosine[:, : half + 1], -sine[:, 1:half]], axis=1)
    weight = np.full(length, 2.0)
    weight[[0, half]] = 1.0
    inverse = forward.T * weight[:, None] / length
    return forward, inverse


def y_tables(length, width, order):
    half = length // 2
    cosine, sine = trig(length)
    eye = np.eye(width)
    full = np.array([[cosine, sine], [-sine, cosine]])
    edge = np.zeros_like(full)
    low, high, ends = slice(1, half), slice(half + 1, length), [0, half]
    edge[0, 0, low], edge[1, 0, low] = cosine[low], -sine[low]
    edge[0, 1, high], edge[1, 1, high] = cosine[high], -sine[high]
    edge[0, 0, ends], edge[1, 1, ends] = cosine[ends], cosine[ends]
    weight = np.full(length, 2.0)
    weight[ends] = 1.0
    forward, inverse = [], []
    size = 2 * width * length
    for table, scale in ((full, np.ones(length)), (edge, weight)):
        grid = np.einsum("abky,xw->kaxbwy", table, eye)[order]
        forward.append(grid.reshape(size, size))
        grid = np.einsum("abky,xw,k->bwykax", table, eye, scale / length)[:, :, :, order]
        inverse.append(grid.reshape(size, size))
    return np.concatenate(forward), np.concatenate(inverse)


def x_tables(slabs, width):
    length = slabs * width
    cosine, sine = (part.reshape(length, slabs, width) for part in trig(length))
    zero = np.zeros_like(cosine)
    from_real = np.stack([np.stack([cosine, zero], 2), np.stack([-sine, zero], 2)])
    from_imag = np.stack([np.stack([zero, sine], 2), np.stack([zero, cosine], 2)])
    rows = np.stack([from_real, from_imag])
    forward = rows.reshape(4 * length, 2 * length)
    inverse = (rows[0] + rows[1]).reshape(2 * length, 2 * length).T / length
    return forward, inverse


def halves(value):
    high = value.astype(jnp.bfloat16)
    return high, (value - high.astype(jnp.float32)).astype(jnp.bfloat16)


def mm(left, right):
    return jnp.dot(left, right, preferred_element_type=jnp.float32)


def table_right(value, table_ref):
    high, low = halves(value)
    return mm(high, table_ref[0]) + (mm(low, table_ref[0]) + mm(high, table_ref[1]))


def stack_rows(value):
    high, low = halves(value)
    return jnp.concatenate([high, low, high])


def table_product(table_ref, high, low):
    return mm(table_ref[0], high) + (mm(table_ref[0], low) + mm(table_ref[1], high))


def lane_is(shape, number):
    return lax.broadcasted_iota(jnp.int32, shape, len(shape) - 1) == number


def to_lane(value, number):
    return pltpu.roll(value, number, 1) if number else value


def from_lane(value, number):
    return pltpu.roll(value, value.shape[1] - number, 1) if number else value


def first_lane(shape):
    return lax.broadcasted_iota(jnp.int32, shape, len(shape) - 1) == 0


def signed(position, full):
    return jnp.where(position * 2 >= full, position - full, position)


def unit_normals(x_mode, y_mode, z_mode, sizes):
    pair = []
    for flip in (False, True):
        waves = []
        for mode, full in zip((x_mode, y_mode, z_mode), sizes):
            wave = signed(mode, full)
            if flip:
                wave = jnp.where(mode * 2 == full, -wave, wave)
            waves.append(wave.astype(jnp.float32) * (1.0 / full))
        length_sq = waves[0] * waves[0] + waves[1] * waves[1] + waves[2] * waves[2]
        positive = length_sq > 0
        inverse = jnp.where(positive, lax.rsqrt(jnp.where(positive, length_sq, 1.0)), 0.0)
        pair.append([wave * inverse for wave in waves])
    return pair


def transform_kernel(
    family_ref, orient_ref, eps_ref, kappa_ref, phase_hbm, z_hbm, y_hbm, forward_hbm, inverse_hbm,
    gathered, base_ref, phase_ref, square_total,
    z_ref, y_ref, forward_ref, inverse_ref,
    eigen_ref, line_high, line_low, end_high, end_low, hat_ref, right_recv, left_recv, cross_recv, cross_out, low_halo, high_halo,
    square_ref, square_recv, square_out,
    plane_sem, table_sem, sum_send_sem, sum_recv_sem, cross_send_sem, cross_recv_sem,
    back_send_sem, back_recv_sem, gather_send_sem, gather_recv_sem, spread_send_sem,
    square_send_sem, square_recv_sem, halo_send_sem, halo_recv_sem,
):
    slabs = lax.axis_size("gx")
    groups = lax.axis_size("vert")
    mine_x = lax.axis_index("gx")
    mine_v = lax.axis_index("vert")
    count, width, ny, nz = phase_ref.shape
    nx = slabs * width
    half = nz // 2
    last = groups - 1
    chunks = sum_send_sem.shape[2]
    piece = slabs // chunks
    relayed = max(chunks - SPREAD, 0)
    at_end = (mine_v == 0) | (mine_v == last)
    step = 32

    def at(axis, offset):
        if axis == "gx":
            return lax.rem(mine_x + offset, slabs)
        return lax.rem(mine_v + offset, groups)

    def copy_to(src, dst, send_sem, recv_sem, axis, place):
        return pltpu.make_async_remote_copy(
            src_ref=src, dst_ref=dst, send_sem=send_sem, recv_sem=recv_sem,
            device_id={axis: place}, device_id_type=MESH,
        )

    def copy(src, dst, send_sem, recv_sem, axis, offset):
        return copy_to(src, dst, send_sem, recv_sem, axis, at(axis, offset))

    plane_copies = [
        pltpu.make_async_copy(phase_hbm.at[:, plane], phase_ref.at[:, plane], plane_sem.at[plane])
        for plane in range(width)
    ]
    table_copies = [
        pltpu.make_async_copy(src, dst, table_sem.at[index])
        for index, (src, dst) in enumerate((
            (z_hbm, z_ref), (y_hbm, y_ref), (forward_hbm, forward_ref), (inverse_hbm, inverse_ref),
        ))
    ]
    plane_order = [0, width - 1] + list(range(1, width - 1))
    for item in table_copies[:1] + [plane_copies[plane] for plane in plane_order] + table_copies[1:]:
        item.start()

    has_left = mine_v > 0
    has_right = mine_v < last
    barrier = pltpu.get_barrier_semaphore()
    for offset in range(1, slabs):
        pl.semaphore_signal(barrier, inc=1, device_id={"gx": at("gx", offset)}, device_id_type=MESH)

    for offset in range(1, groups):
        pl.semaphore_signal(
            barrier, inc=1, device_id={"vert": at("vert", offset)}, device_id_type=MESH
        )

    def square_copy(right, plane, src=None):
        way = 0 if right else 1
        return copy(
            (square_out.at[way] if src is None else src).at[plane], square_recv.at[way, plane],
            square_send_sem.at[way, plane], square_recv_sem.at[way, plane],
            "vert", 1 if right else last,
        )

    def square_hop(hop, planes):
        for right in (True, False):
            way = 0 if right else 1

            @pl.when(mine_v == (hop if right else last - hop))
            def _():
                for plane in planes:
                    if hop == 0:
                        square_copy(right, plane, square_ref).start()
                    else:
                        square_copy(right, plane).wait_recv()
                        square_out[way, plane] = square_ref[plane] + square_recv[way, plane]
                        square_copy(right, plane).start()

    halo_copies = [
        copy(phase_ref.at[:, width - 1], low_halo, halo_send_sem.at[0], halo_recv_sem.at[0], "gx", 1),
        copy(phase_ref.at[:, 0], high_halo, halo_send_sem.at[1], halo_recv_sem.at[1], "gx", slabs - 1),
    ]
    table_copies[0].wait()
    lane_shape = (ny, half)
    for turn, plane in enumerate(plane_order):
        plane_copies[plane].wait()
        for begin in range(0, ny, STEP):
            rows = pl.ds(begin, STEP)
            sums = [jnp.zeros((STEP, nz), jnp.float32) for _ in range(7)]
            for number in range(count):
                value = phase_ref[number, plane, rows]
                value = value * value
                family = family_ref[number]
                for comp in range(6):
                    sums[comp] = sums[comp] + eps_ref[comp, family] * value
                sums[6] = sums[6] + value
            for comp in range(6):
                eigen_ref[comp, rows] = sums[comp]
            square_ref[plane, rows] = sums[6]
        if turn == BARRIER_PLANE:
            pl.semaphore_wait(barrier, slabs + groups - 2)
        if turn >= BARRIER_PLANE:
            square_hop(0, plane_order[: turn + 1] if turn == BARRIER_PLANE else [plane])
        if turn == max(BARRIER_PLANE, 1):
            for item in halo_copies:
                item.start()
        lines = table_right(eigen_ref[...].reshape(6 * ny, nz), z_ref)
        for part in range(2):
            rows = pl.ds((part * width + plane) * ny, ny)
            ends = jnp.zeros(lane_shape, jnp.float32)
            for comp in range(6):
                block = lines[comp * ny : (comp + 1) * ny, part * half : (part + 1) * half]
                lanes = pl.ds(comp % 2 * half, half)
                line_high[comp // 2, rows, lanes], line_low[comp // 2, rows, lanes] = halves(block)
                ends = jnp.where(lane_is(lane_shape, comp), to_lane(block, comp), ends)
            end_high[rows, :], end_low[rows, :] = halves(ends)

    for item in table_copies[1:]:
        item.wait()
    size = 2 * width * ny
    first = first_lane((size, half))
    full_table, edge_table = (y_ref.at[:, pl.ds(index * size, size)] for index in range(2))

    end_modes = table_product(edge_table, end_high[...], end_low[...])
    for pair in range(3):
        modes = table_product(full_table, line_high[pair], line_low[pair])
        for side in range(2):
            comp = 2 * pair + side
            lanes = slice(side * half, (side + 1) * half)
            picked = jnp.where(first, from_lane(end_modes, comp), modes[:, lanes])
            hat_ref[:, comp] = picked.reshape(ny, 2 * width, half)

    def way_of(right):
        if right:
            return right_recv, 0, 1, mine_v == 0
        return left_recv, 1, last, mine_v == last

    def rows_of(group, chunk):
        return pl.ds(group * slabs + chunk * piece, piece)

    def sum_copy(right, turn, chunk):
        recv, way, offset, _ = way_of(right)
        owner = last - turn if right else turn
        return copy(
            hat_ref.at[rows_of(owner, chunk)], recv.at[turn, pl.ds(chunk * piece, piece)],
            sum_send_sem.at[way, turn, chunk], sum_recv_sem.at[way, turn, chunk], "vert", offset,
        )

    def sends_sum(right, turn):
        return mine_v < last - turn if right else mine_v > turn

    def add_sum(right, turn, chunk):
        owner = last - turn if right else turn
        rows = rows_of(owner, chunk)
        sum_copy(right, turn, chunk).wait_recv()
        hat_ref[rows] = hat_ref[rows] + way_of(right)[0][turn, pl.ds(chunk * piece, piece)]

    def during(number, begin, length, action):
        @pl.when((number >= begin) & (number < begin + length))
        def _():
            action(number - begin)

    def pass_sums(right, number):
        at_end = way_of(right)[3]
        for turn in range(last):

            def one(chunk):
                @pl.when(jnp.logical_not(at_end) & sends_sum(right, turn))
                def _():
                    add_sum(right, turn, chunk)
                    sum_copy(right, turn, chunk).start()

            during(number, turn, chunks, one)

    def end_sums(chunk):
        @pl.when(has_left)
        def _():
            add_sum(True, last - mine_v, chunk)

        @pl.when(has_right)
        def _():
            add_sum(False, mine_v, chunk)

    def source_of(chunk, member):
        return chunk + member * chunks

    my_chunk = lax.rem(mine_x, chunks)
    my_place = my_chunk * piece + mine_x // chunks
    mine = mine_v * slabs + my_place

    def cross_copy(place, source, target):
        return copy_to(
            hat_ref.at[mine_v * slabs + place], cross_recv.at[source],
            cross_send_sem.at[place], cross_recv_sem.at[source], "gx", target,
        )

    def back_copy(place, target):
        return copy_to(
            cross_out.at[target], gathered.at[mine_v * slabs + place],
            back_send_sem.at[target], back_recv_sem.at[place], "gx", target,
        )

    def send_cross(chunk):
        for member in range(piece):
            target = source_of(chunk, member)
            place = chunk * piece + member

            @pl.when(target != mine_x)
            def _():
                cross_copy(place, mine_x, target).start()

            @pl.when(target == mine_x)
            def _():
                cross_recv[mine_x] = hat_ref[mine_v * slabs + place]

    def over_others(action):
        def one(offset, carry):
            action(at("gx", offset))
            return carry

        lax.fori_loop(1, slabs, one, 0)

    def solve_row():
        shape = (nx, half)
        y_mode = jnp.full(shape, 0, jnp.int32) + (mine_v * slabs + mine_x)
        x_mode = lax.broadcasted_iota(jnp.int32, shape, 0)
        lane = lax.broadcasted_iota(jnp.int32, shape, 1)
        ends = (y_mode == 0) | (y_mode * 2 == ny)
        upper = y_mode * 2 > ny
        edge = lane == 0
        z_first = jnp.where(edge & upper, half, lane)
        z_second = jnp.where(edge & (upper | ends), half, lane)
        normal_sets = [
            unit_normals(x_mode, y_mode, z_mode, (nx, ny, nz)) for z_mode in (z_first, z_second)
        ]
        over_others(lambda source: cross_copy(0, source, source).wait_recv())
        lines = jnp.concatenate(
            [cross_recv[:, comp].reshape(2 * nx, half) for comp in range(6)], axis=1
        )
        modes = mm(forward_ref[...], stack_rows(lines))
        parts = [
            [modes[i * nx : (i + 1) * nx, comp * half : (comp + 1) * half] for i in range(4)]
            for comp in range(6)
        ]
        stresses = []
        for part in range(2):
            total = None
            for source in range(2):
                strain = [parts[comp][2 * source + part] for comp in range(6)]
                for normals in normal_sets[source]:
                    value = green_stress(strain, normals)
                    total = value if total is None else [a + b for a, b in zip(total, value)]
            stresses.append([0.5 * value for value in total])
        modes = jnp.concatenate([jnp.concatenate(part, axis=1) for part in stresses])
        lines = mm(inverse_ref[...], stack_rows(modes))
        for comp in range(6):
            block = lines[:, comp * half : (comp + 1) * half]
            cross_out[:, comp] = block.reshape(slabs, 2 * width, half)
        over_others(lambda target: back_copy(my_place, target).start())
        gathered[mine] = cross_out[mine_x]

    def gather_copy(right, group, chunk):
        way = 0 if right else 1
        place = gathered.at[rows_of(group, chunk)]
        return copy(
            place, place, gather_send_sem.at[way, group, chunk],
            gather_recv_sem.at[way, group, chunk], "vert", 1 if right else last,
        )

    def spread_copy(right, target, chunk):
        place = gathered.at[rows_of(mine_v, chunk)]
        return copy_to(
            place, place, spread_send_sem.at[target, chunk - relayed],
            gather_recv_sem.at[0 if right else 1, mine_v, chunk], "vert", target,
        )

    def over_targets(chunk, action):
        for distance in reversed(range(1, groups)):
            for right in (True, False):
                target = mine_v + distance if right else mine_v - distance

                @pl.when(target <= last if right else target >= 0)
                def _():
                    action(spread_copy(right, target, chunk))

    def send_gather(chunk):
        for member in range(piece):
            source = source_of(chunk, member)

            @pl.when(source != mine_x)
            def _():
                back_copy(chunk * piece + member, source).wait_recv()

        spread = at_end & (chunk >= relayed)

        @pl.when(jnp.logical_not(spread))
        def _():
            for right, able in ((True, has_right), (False, has_left)):

                @pl.when(able)
                def _():
                    gather_copy(right, mine_v, chunk).start()

        @pl.when(spread)
        def _():
            over_targets(chunk, lambda item: item.start())

    def end_spread(chunk, carry):
        for right, exists, group in ((True, has_left, 0), (False, has_right, last)):

            @pl.when(exists)
            def _():
                gather_copy(right, group, chunk).wait_recv()

        return carry

    def relay_gather(stage, chunk):
        for right, able, exists, group in (
            (True, has_right, mine_v >= stage, mine_v - stage),
            (False, has_left, mine_v + stage <= last, mine_v + stage),
        ):

            first_group = mine_v == stage if right else mine_v + stage == last

            @pl.when(exists & jnp.logical_not(first_group & (chunk >= relayed)))
            def _():
                gather_copy(right, group, chunk).wait_recv()

                @pl.when(able)
                def _():
                    gather_copy(right, group, chunk).start()

    def react(number, carry):
        orient = orient_ref[number]
        kappa = [kappa_ref[dim, orient] for dim in range(3)]
        for plane in range(width):
            value = phase_ref[number, plane]
            low = low_halo[number] if plane == 0 else phase_ref[number, plane - 1]
            high = high_halo[number] if plane == width - 1 else phase_ref[number, plane + 1]
            twice = 2.0 * value
            laplace = kappa[0] * (low + high - twice)
            laplace = laplace + kappa[1] * (
                pltpu.roll(value, 1, 0) + pltpu.roll(value, ny - 1, 0) - twice
            )
            laplace = laplace + kappa[2] * (
                pltpu.roll(value, 1, 1) + pltpu.roll(value, nz - 1, 1) - twice
            )
            square = value * value
            chemical = twice - 6.0 * square + 4.0 * square * value
            chemical = chemical - 2.0 * CROSS_COUPLING * value * square
            base_ref[number, plane] = value - TIME_STEP * (chemical - laplace)
        return carry

    for right in (True, False):

        @pl.when(way_of(right)[3])
        def _():
            def one(number, carry):
                for turn in range(last):
                    during(number, turn, chunks, lambda chunk: sum_copy(right, turn, chunk).start())
                return carry

            lax.fori_loop(0, chunks + last - 1, one, 0)

    lower = mine_v * 2 < groups
    share = 4
    slots = max(
        chunks + GATHER_LAG + last, REACT_SLOT - (-count // share), SQUARE_SLOT + SQUARE_LAG * groups + width
    )

    def slot(number, carry):
        for right in (True, False):

            @pl.when(lower if right else jnp.logical_not(lower))
            def _():
                pass_sums(right, number)
                pass_sums(not right, number - 1)

        def own(chunk):
            end_sums(chunk)
            send_cross(chunk)

        during(number, SUM_LAG, chunks, own)

        during(number, GATHER_LAG, chunks, send_gather)

        @pl.when(number == my_chunk + SOLVE_LAG)
        def _():
            solve_row()

        for stage in range(1, groups):
            during(number, GATHER_LAG + stage, chunks, lambda chunk: relay_gather(stage, chunk))
        for hop in range(1, last):
            for index in range(0, width, SQUARE_SPAN):

                @pl.when(number == SQUARE_SLOT + SQUARE_LAG * (hop - 1) + index // SQUARE_SPAN)
                def _():
                    square_hop(hop, plane_order[index : index + SQUARE_SPAN])

        @pl.when(number == REACT_SLOT)
        def _():
            for item in halo_copies:
                item.wait_recv()

        def react_share(index):
            begin = index * share
            lax.fori_loop(
                jnp.minimum(begin, count), jnp.minimum(begin + share, count), react, 0
            )

        during(number, REACT_SLOT, -(-count // share), react_share)
        return carry

    lax.fori_loop(0, slots, slot, 0)
    lax.fori_loop(relayed, chunks, end_spread, 0)
    for right, at_last in ((True, mine_v == last), (False, mine_v == 0)):

        @pl.when(at_last)
        def _():
            for plane in range(width):
                square_copy(right, plane).wait_recv()

    square_total[...] = square_ref[...]

    @pl.when(has_left)
    def _():
        square_total[...] = square_total[...] + square_recv[0]

    @pl.when(has_right)
    def _():
        square_total[...] = square_total[...] + square_recv[1]

    for item in halo_copies:
        item.wait_send()

    def end_cross(place, carry):
        target = source_of(place // piece, lax.rem(place, piece))

        @pl.when(target != mine_x)
        def _():
            cross_copy(place, mine_x, target).wait_send()

        return carry

    lax.fori_loop(0, slabs, end_cross, 0)
    over_others(lambda target: back_copy(my_place, target).wait_send())

    def end_chunk(chunk, carry):
        for right, able in ((True, has_right), (False, has_left)):
            for turn in range(last):

                @pl.when(sends_sum(right, turn))
                def _():
                    sum_copy(right, turn, chunk).wait_send()

            for stage in range(groups):
                group = mine_v - stage if right else mine_v + stage
                exists = able & ((mine_v >= stage) if right else (mine_v + stage <= last))

                first_group = group == (0 if right else last)

                @pl.when(exists & jnp.logical_not(first_group & (chunk >= relayed)))
                def _():
                    gather_copy(right, group, chunk).wait_send()

        @pl.when(at_end & (chunk >= relayed))
        def _():
            over_targets(chunk, lambda item: item.wait_send())

        return carry

    lax.fori_loop(0, chunks, end_chunk, 0)
    for right, able in ((True, has_right), (False, has_left)):

        @pl.when(able)
        def _():
            for plane in range(width):
                square_copy(right, plane).wait_send()


def update_kernel(
    family_ref, eps_ref, hat_ref, phase_ref, base_ref, square_ref, y_ref, z_ref,
    next_ref, stress_ref, lines_ref,
):
    count, _, ny, nz = next_ref.shape
    width = square_ref.shape[0]
    plane = pl.program_id(0)
    half = nz // 2
    size = 2 * width * ny

    @pl.when(plane == 0)
    def _():
        shape = (size, half)
        first = first_lane(shape)
        ends = jnp.zeros(shape, jnp.float32)
        for comp in range(6):
            block = hat_ref[:, comp].reshape(shape)
            ends = jnp.where(lane_is(shape, comp), to_lane(block, comp), ends)
        full_table, edge_table = (y_ref.at[:, pl.ds(index * size, size)] for index in range(2))
        end_lines = table_product(edge_table, *halves(ends))
        for pair in range(3):
            modes = [hat_ref[:, 2 * pair + side].reshape(shape) for side in range(2)]
            both = table_product(full_table, *halves(jnp.concatenate(modes, axis=1)))
            for side in range(2):
                comp = 2 * pair + side
                lanes = slice(side * half, (side + 1) * half)
                picked = jnp.where(first, from_lane(end_lines, comp), both[:, lanes])
                lines = jnp.concatenate([picked[: size // 2], picked[size // 2 :]], axis=1)
                lines_ref[comp] = lines.reshape(width, ny, nz)

    lines = lines_ref[:, pl.ds(plane, 1)].reshape(6 * ny, nz)
    stress_ref[...] = table_right(lines, z_ref).reshape(6, 1, ny, nz)
    step = 16

    def finish(index, carry):
        rows = pl.ds(pl.multiple_of(index * step, step), step)
        stress = [stress_ref[comp, 0, rows, :] for comp in range(6)]
        shared = (-2.0 * TIME_STEP * CROSS_COUPLING) * square_ref[plane, rows, :]
        for number in range(count):
            family = family_ref[number]
            total = shared
            for comp in range(6):
                factor = eps_ref[comp, family] * (2.0 * TIME_STEP * (1.0 if comp < 3 else 2.0))
                total = total + factor * stress[comp]
            value = phase_ref[number, plane, rows, :]
            next_ref[number, 0, rows, :] = base_ref[number, plane, rows, :] + value * total
        return carry

    lax.fori_loop(0, ny // step, finish, 0)


def body(phase_field, kappa_table, eps_table, orient_index, family_index):
    slabs = lax.axis_size("gx")
    groups = lax.axis_size("vert")
    count, width, ny, nz = phase_field.shape
    half = nz // 2
    whole_rows = slabs * groups == ny and slabs % 2 == 0 and groups >= 2
    if not whole_rows or width * 2 != 8 or half % 128 or ny % 32:
        return general_body(phase_field, kappa_table, eps_table, orient_index, family_index)
    f32 = jnp.float32
    chunks = slabs // 2
    places = np.arange(slabs)
    order = np.concatenate([
        group * slabs + places // 2 + chunks * (places % 2) for group in range(groups)
    ])
    y_forward, y_inverse = (split_table(table) for table in y_tables(ny, width, order))
    z_forward, z_inverse = (split_table(table) for table in z_tables(nz))
    x_forward, x_inverse = (stacked_table(table) for table in x_tables(slabs, width))
    tile = (6, 2 * width, half)
    dma = pltpu.SemaphoreType.DMA
    halo = (count, ny, nz)
    squares = (width, ny, nz)
    tables = (z_forward, y_forward, x_forward, x_inverse)
    in_place = functools.partial(pltpu.with_memory_space_constraint, memory_space=pltpu.HBM)
    small = [in_place(item) for item in (family_index, orient_index, eps_table.T, kappa_table.T)]
    hat, base, phase, square = pl.pallas_call(
        transform_kernel,
        out_shape=(
            pltpu.VMEM((ny, *tile), f32),
            pltpu.VMEM(phase_field.shape, f32),
            pltpu.VMEM(phase_field.shape, f32),
            pltpu.VMEM(squares, f32),
        ),
        in_specs=[SMEM_SPEC] * 4 + [HBM_SPEC] * 5,
        out_specs=(VMEM_SPEC,) * 4,
        scratch_shapes=[
            *[pltpu.VMEM(table.shape, table.dtype) for table in tables],
            pltpu.VMEM((6, ny, nz), f32),
            *[pltpu.VMEM((3, 2 * width * ny, nz), jnp.bfloat16) for _ in range(2)],
            *[pltpu.VMEM((2 * width * ny, half), jnp.bfloat16) for _ in range(2)],
            pltpu.VMEM((ny, *tile), f32),
            *[pltpu.VMEM((groups - 1, slabs, *tile), f32) for _ in range(2)],
            *[pltpu.VMEM((slabs, *tile), f32) for _ in range(2)],
            pltpu.VMEM(halo, f32), pltpu.VMEM(halo, f32),
            pltpu.VMEM(squares, f32),
            pltpu.VMEM((2, *squares), f32), pltpu.VMEM((2, *squares), f32),
            dma((width,)), dma((len(tables),)),
            dma((2, groups - 1, chunks)), dma((2, groups - 1, chunks)),
            dma((slabs,)), dma((slabs,)),
            dma((slabs,)), dma((slabs,)),
            dma((2, groups, chunks)), dma((2, groups, chunks)), dma((groups, max(min(SPREAD, chunks), 1))),
            dma((2, width)), dma((2, width)),
            dma((2,)), dma((2,)),
        ],
        compiler_params=pltpu.CompilerParams(
            vmem_limit_bytes=VMEM_LIMIT, collective_id=0, has_side_effects=True
        ),
        name="transform",
    )(*small, in_place(phase_field), *[in_place(table) for table in tables])
    phase_next, stress = pl.pallas_call(
        update_kernel,
        grid=(width,),
        out_shape=(
            jax.ShapeDtypeStruct(phase_field.shape, f32),
            jax.ShapeDtypeStruct((6, width, ny, nz), f32),
        ),
        in_specs=[SMEM_SPEC] * 2 + [VMEM_SPEC] * 6,
        out_specs=(
            pl.BlockSpec((count, 1, ny, nz), lambda i: (0, i, 0, 0)),
            pl.BlockSpec((6, 1, ny, nz), lambda i: (0, i, 0, 0)),
        ),
        scratch_shapes=[pltpu.VMEM((6, width, ny, nz), f32)],
        compiler_params=pltpu.CompilerParams(vmem_limit_bytes=VMEM_LIMIT),
        name="update",
    )(small[0], small[2], hat, phase, base, square, y_inverse, z_inverse)
    return (phase_next, stress)


def solution(mesh):
    return jax.shard_map(
        body,
        mesh=mesh,
        in_specs=(P("vert", "gx", None, None), P(), P(), P("vert"), P("vert")),
        out_specs=(P("vert", "gx", None, None), P(None, "gx", None, None)),
        check_vma=False,
    )
```

```python
import functools
import math

import jax
import jax.numpy as jnp
import ml_dtypes
import numpy as np
from jax import lax
from jax.experimental import pallas as pl
from jax.experimental.pallas import tpu as pltpu
from jax.sharding import PartitionSpec as P

LAME_LAMBDA = 1.5
SHEAR_MOD = 1.0
TIME_STEP = 0.1
CROSS_COUPLING = 0.02
HIGHEST = lax.Precision.HIGHEST
TENSOR_SLOTS = ((0, 5, 4), (5, 1, 3), (4, 3, 2))
VOIGT_PAIRS = ((0, 0), (1, 1), (2, 2), (1, 2), (0, 2), (0, 1))
PAIRED_FORMS = {1: "pcxyz,pxqk->qckyz", 2: "pcxyz,pyqk->qcxkz", 3: "pcxyz,pzqk->qcxyk"}


def with_halo(block, sides, width):
    for axis, dim in sides:
        count = lax.axis_size(axis)
        forward = [(i, i + 1) for i in range(count - 1)]
        forward.append((count - 1, 0))
        backward = [(target, source) for source, target in forward]
        low = lax.ppermute(
            lax.slice_in_dim(block, block.shape[dim] - width, None, axis=dim), axis, forward
        )
        high = lax.ppermute(lax.slice_in_dim(block, 0, width, axis=dim), axis, backward)
        block = jnp.concatenate([low, block, high], axis=dim)
    return block


def signed_wave(first_row, row_count, full_count):
    positions = first_row + jnp.arange(row_count, dtype=jnp.int32)
    shifted = jnp.where(positions * 2 >= full_count, positions - full_count, positions)
    return shifted.astype(jnp.float32) / full_count


def wave_normals(x_wave, y_wave, z_wave):
    x_grid = x_wave[:, None, None]
    y_grid = y_wave[None, :, None]
    z_grid = z_wave[None, None, :]
    length_sq = x_grid * x_grid + y_grid * y_grid + z_grid * z_grid
    positive = length_sq > 0
    safe_length = jnp.where(positive, length_sq, 1.0)
    inverse_len = jnp.where(positive, lax.rsqrt(safe_length), 0.0)
    return [x_grid * inverse_len, y_grid * inverse_len, z_grid * inverse_len]


def green_stress(strain, normals):
    trace_strain = strain[0] + strain[1] + strain[2]
    stiffened = [
        (
            LAME_LAMBDA * trace_strain + 2.0 * SHEAR_MOD * strain[number]
            if number < 3
            else 2.0 * SHEAR_MOD * strain[number]
        )
        for number in range(6)
    ]
    traction = [
        sum(
            (
                stiffened[TENSOR_SLOTS[row_axis][col_axis]] * normals[col_axis]
                for col_axis in range(3)
            )
        )
        for row_axis in range(3)
    ]
    normal_part = normals[0] * traction[0] + normals[1] * traction[1] + normals[2] * traction[2]
    coupling = (LAME_LAMBDA + SHEAR_MOD) / (LAME_LAMBDA + 2.0 * SHEAR_MOD)
    shifted = [
        (traction[row_axis] - normals[row_axis] * normal_part * coupling) / SHEAR_MOD
        for row_axis in range(3)
    ]
    excess = [
        0.5
        * (
            normals[VOIGT_PAIRS[number][0]] * shifted[VOIGT_PAIRS[number][1]]
            + normals[VOIGT_PAIRS[number][1]] * shifted[VOIGT_PAIRS[number][0]]
        )
        - strain[number]
        for number in range(6)
    ]
    trace_excess = excess[0] + excess[1] + excess[2]
    result = [
        (
            LAME_LAMBDA * trace_excess + 2.0 * SHEAR_MOD * excess[number]
            if number < 3
            else 2.0 * SHEAR_MOD * excess[number]
        )
        for number in range(6)
    ]
    return result


def reaction_update(variant, laplace, driving, square_sum):
    chemical = 2.0 * variant - 6.0 * variant * variant + 4.0 * variant * variant * variant
    chemical = chemical + 2.0 * CROSS_COUPLING * variant * (square_sum - variant * variant)
    chemical = chemical - 2.0 * variant * driving - laplace
    return variant - TIME_STEP * chemical


def dft_tables(length):
    positions = jnp.arange(length, dtype=jnp.int32)
    products = positions[:, None] * positions[None, :] % length
    angles = products.astype(jnp.float32) * (2.0 * math.pi / length)
    return (jnp.cos(angles), jnp.sin(angles))


def paired_table(length, inverse):
    cosine_table, sine_table = dft_tables(length)
    cross_term = sine_table if inverse else -sine_table
    from_real = jnp.stack([cosine_table, cross_term], axis=1)
    from_imag = jnp.stack([-cross_term, cosine_table], axis=1)
    table = jnp.stack([from_real, from_imag])
    if inverse:
        table = table * (1.0 / length)
    return table


def transform(real_part, imag_part, axis_dim, inverse):
    length = real_part.shape[axis_dim]
    table = paired_table(length, inverse)
    if imag_part is None:
        pattern = PAIRED_FORMS[axis_dim].replace("p", "")
        result = jnp.einsum(pattern, real_part, table[0], precision=HIGHEST)
        return (result[0], result[1])
    stacked = jnp.stack([real_part, imag_part])
    result = jnp.einsum(PAIRED_FORMS[axis_dim], stacked, table, precision=HIGHEST)
    return (result[0], result[1])


def transform_real(real_part, imag_part, axis_dim):
    length = real_part.shape[axis_dim]
    table = paired_table(length, True)[:, :, 0, :]
    pattern = PAIRED_FORMS[axis_dim].replace("q", "")
    stacked = jnp.stack([real_part, imag_part])
    return jnp.einsum(pattern, stacked, table, precision=HIGHEST)


def forward_x(halves):
    return transform(halves[0], halves[1], 1, False)


def forward_y(halves):
    return transform(halves[0], halves[1], 2, False)


def backward_x(halves):
    return transform(halves[0], halves[1], 1, True)


def backward_z(halves):
    return transform_real(halves[0], halves[1], 3)


def general_body(phase_field, kappa_table, eps_table, orient_index, family_index):
    slab_count = lax.axis_size("gx")
    count_var, slab_width, width_y, width_z = phase_field.shape
    total_x = slab_width * slab_count
    family_hot = (
        family_index[:, None] == jnp.arange(eps_table.shape[0], dtype=jnp.int32)[None, :]
    ).astype(jnp.float32)
    orient_hot = (
        orient_index[:, None] == jnp.arange(kappa_table.shape[0], dtype=jnp.int32)[None, :]
    ).astype(jnp.float32)
    eps_var = jnp.dot(family_hot, eps_table, precision=HIGHEST)
    kappa_var = jnp.dot(orient_hot, kappa_table, precision=HIGHEST)
    padded = with_halo(phase_field, (("gx", 1),), 1)
    squared = phase_field * phase_field
    eigen_sum = jnp.einsum("vk,vxyz->kxyz", eps_var, squared, precision=HIGHEST)
    local_square = jnp.sum(squared, axis=0)
    eigen_sum = lax.psum_scatter(eigen_sum, "vert", scatter_dimension=2, tiled=True)
    square_sum = lax.psum(local_square, "vert")
    real_part, imag_part = transform(eigen_sum, None, 3, False)
    real_part, imag_part = forward_x(
        (
            lax.all_to_all(real_part, "gx", split_axis=3, concat_axis=1, tiled=True),
            lax.all_to_all(imag_part, "gx", split_axis=3, concat_axis=1, tiled=True),
        )
    )
    real_part, imag_part = forward_y(
        (
            lax.all_to_all(real_part, "vert", split_axis=1, concat_axis=2, tiled=True),
            lax.all_to_all(imag_part, "vert", split_axis=1, concat_axis=2, tiled=True),
        )
    )
    x_start = lax.axis_index("vert") * real_part.shape[1]
    z_start = lax.axis_index("gx") * real_part.shape[3]
    normals = wave_normals(
        signed_wave(x_start, real_part.shape[1], total_x),
        signed_wave(0, width_y, width_y),
        signed_wave(z_start, real_part.shape[3], width_z),
    )
    real_part = jnp.stack(green_stress(real_part, normals))
    imag_part = jnp.stack(green_stress(imag_part, normals))
    real_part, imag_part = transform(real_part, imag_part, 2, True)
    real_part, imag_part = backward_x(
        (
            lax.all_to_all(real_part, "vert", split_axis=2, concat_axis=1, tiled=True),
            lax.all_to_all(imag_part, "vert", split_axis=2, concat_axis=1, tiled=True),
        )
    )
    stress = backward_z(
        (
            lax.all_to_all(real_part, "gx", split_axis=1, concat_axis=3, tiled=True),
            lax.all_to_all(imag_part, "gx", split_axis=1, concat_axis=3, tiled=True),
        )
    )
    stress = lax.all_gather(stress, "vert", axis=2, tiled=True)
    weights = jnp.array([1.0, 1.0, 1.0, 2.0, 2.0, 2.0], jnp.float32)
    driving = jnp.einsum("vk,kxyz->vxyz", eps_var * weights[None, :], stress, precision=HIGHEST)
    kappa_x = kappa_var[:, 0][:, None, None, None]
    kappa_y = kappa_var[:, 1][:, None, None, None]
    kappa_z = kappa_var[:, 2][:, None, None, None]
    laplace = kappa_x * (padded[:, 2:] + padded[:, :-2] - 2.0 * phase_field)
    laplace = laplace + kappa_y * (
        jnp.roll(phase_field, 1, 2) + jnp.roll(phase_field, -1, 2) - 2.0 * phase_field
    )
    laplace = laplace + kappa_z * (
        jnp.roll(phase_field, 1, 3) + jnp.roll(phase_field, -1, 3) - 2.0 * phase_field
    )
    phase_next = reaction_update(phase_field, laplace, driving, square_sum[None])
    return (phase_next, stress)


MESH = pl.DeviceIdType.MESH
VMEM_SPEC = pl.BlockSpec(memory_space=pltpu.VMEM)
SMEM_SPEC = pl.BlockSpec(memory_space=pltpu.SMEM)
HBM_SPEC = pl.BlockSpec(memory_space=pltpu.HBM)
VMEM_LIMIT = 20 * 1024 * 1024
SUM_LAG = 2
SOLVE_LAG = 3
GATHER_LAG = 5
SQUARE_SLOT = 1
SQUARE_LAG = 1
SQUARE_SPAN = 1
STEP = 16
BARRIER_PLANE = 1
REACT_SLOT = 5
SPREAD = 4


def split_table(table):
    high = table.astype(np.float32).astype(ml_dtypes.bfloat16)
    low = (table - high.astype(np.float64)).astype(np.float32).astype(ml_dtypes.bfloat16)
    return jnp.asarray(np.stack([high, low]))


def stacked_table(table):
    high, low = split_table(table)
    return jnp.concatenate([high, high, low], axis=1)


def trig(length):
    positions = np.arange(length)
    angles = (positions[:, None] * positions[None, :] % length) * (2.0 * np.pi / length)
    return np.cos(angles), np.sin(angles)


def z_tables(length):
    half = length // 2
    cosine, sine = trig(length)
    forward = np.concatenate([cosine[:, : half + 1], -sine[:, 1:half]], axis=1)
    weight = np.full(length, 2.0)
    weight[[0, half]] = 1.0
    inverse = forward.T * weight[:, None] / length
    return forward, inverse


def y_tables(length, width, order):
    half = length // 2
    cosine, sine = trig(length)
    eye = np.eye(width)
    full = np.array([[cosine, sine], [-sine, cosine]])
    edge = np.zeros_like(full)
    low, high, ends = slice(1, half), slice(half + 1, length), [0, half]
    edge[0, 0, low], edge[1, 0, low] = cosine[low], -sine[low]
    edge[0, 1, high], edge[1, 1, high] = cosine[high], -sine[high]
    edge[0, 0, ends], edge[1, 1, ends] = cosine[ends], cosine[ends]
    weight = np.full(length, 2.0)
    weight[ends] = 1.0
    forward, inverse = [], []
    size = 2 * width * length
    for table, scale in ((full, np.ones(length)), (edge, weight)):
        grid = np.einsum("abky,xw->kaxbwy", table, eye)[order]
        forward.append(grid.reshape(size, size))
        grid = np.einsum("abky,xw,k->bwykax", table, eye, scale / length)[:, :, :, order]
        inverse.append(grid.reshape(size, size))
    return np.concatenate(forward), np.concatenate(inverse)


def x_tables(slabs, width):
    length = slabs * width
    cosine, sine = (part.reshape(length, slabs, width) for part in trig(length))
    zero = np.zeros_like(cosine)
    from_real = np.stack([np.stack([cosine, zero], 2), np.stack([-sine, zero], 2)])
    from_imag = np.stack([np.stack([zero, sine], 2), np.stack([zero, cosine], 2)])
    rows = np.stack([from_real, from_imag])
    forward = rows.reshape(4 * length, 2 * length)
    inverse = (rows[0] + rows[1]).reshape(2 * length, 2 * length).T / length
    return forward, inverse


def halves(value):
    high = value.astype(jnp.bfloat16)
    return high, (value - high.astype(jnp.float32)).astype(jnp.bfloat16)


def mm(left, right):
    return jnp.dot(left, right, preferred_element_type=jnp.float32)


def table_right(value, table_ref):
    high, low = halves(value)
    return mm(high, table_ref[0]) + (mm(low, table_ref[0]) + mm(high, table_ref[1]))


def stack_rows(value):
    high, low = halves(value)
    return jnp.concatenate([high, low, high])


def table_product(table_ref, high, low):
    return mm(table_ref[0], high) + (mm(table_ref[0], low) + mm(table_ref[1], high))


def lane_is(shape, number):
    return lax.broadcasted_iota(jnp.int32, shape, len(shape) - 1) == number


def to_lane(value, number):
    return pltpu.roll(value, number, 1) if number else value


def from_lane(value, number):
    return pltpu.roll(value, value.shape[1] - number, 1) if number else value


def first_lane(shape):
    return lax.broadcasted_iota(jnp.int32, shape, len(shape) - 1) == 0


def signed(position, full):
    return jnp.where(position * 2 >= full, position - full, position)


def unit_normals(x_mode, y_mode, z_mode, sizes):
    pair = []
    for flip in (False, True):
        waves = []
        for mode, full in zip((x_mode, y_mode, z_mode), sizes):
            wave = signed(mode, full)
            if flip:
                wave = jnp.where(mode * 2 == full, -wave, wave)
            waves.append(wave.astype(jnp.float32) * (1.0 / full))
        length_sq = waves[0] * waves[0] + waves[1] * waves[1] + waves[2] * waves[2]
        positive = length_sq > 0
        inverse = jnp.where(positive, lax.rsqrt(jnp.where(positive, length_sq, 1.0)), 0.0)
        pair.append([wave * inverse for wave in waves])
    return pair


def transform_kernel(
    family_ref, orient_ref, eps_ref, kappa_ref, phase_hbm, z_hbm, y_hbm, forward_hbm, inverse_hbm,
    gathered, base_ref, phase_ref, square_total,
    z_ref, y_ref, forward_ref, inverse_ref,
    eigen_ref, line_high, line_low, end_high, end_low, hat_ref, right_recv, left_recv, cross_recv, cross_out, low_halo, high_halo,
    square_ref, square_recv, square_out,
    plane_sem, table_sem, sum_send_sem, sum_recv_sem, cross_send_sem, cross_recv_sem,
    back_send_sem, back_recv_sem, gather_send_sem, gather_recv_sem, spread_send_sem,
    square_send_sem, square_recv_sem, halo_send_sem, halo_recv_sem,
):
    slabs = lax.axis_size("gx")
    groups = lax.axis_size("vert")
    mine_x = lax.axis_index("gx")
    mine_v = lax.axis_index("vert")
    count, width, ny, nz = phase_ref.shape
    nx = slabs * width
    half = nz // 2
    last = groups - 1
    chunks = sum_send_sem.shape[2]
    piece = slabs // chunks
    relayed = max(chunks - SPREAD, 0)
    at_end = (mine_v == 0) | (mine_v == last)
    step = 32

    def at(axis, offset):
        if axis == "gx":
            return lax.rem(mine_x + offset, slabs)
        return lax.rem(mine_v + offset, groups)

    def copy_to(src, dst, send_sem, recv_sem, axis, place):
        return pltpu.make_async_remote_copy(
            src_ref=src, dst_ref=dst, send_sem=send_sem, recv_sem=recv_sem,
            device_id={axis: place}, device_id_type=MESH,
        )

    def copy(src, dst, send_sem, recv_sem, axis, offset):
        return copy_to(src, dst, send_sem, recv_sem, axis, at(axis, offset))

    plane_copies = [
        pltpu.make_async_copy(phase_hbm.at[:, plane], phase_ref.at[:, plane], plane_sem.at[plane])
        for plane in range(width)
    ]
    table_copies = [
        pltpu.make_async_copy(src, dst, table_sem.at[index])
        for index, (src, dst) in enumerate((
            (z_hbm, z_ref), (y_hbm, y_ref), (forward_hbm, forward_ref), (inverse_hbm, inverse_ref),
        ))
    ]
    plane_order = [0, width - 1] + list(range(1, width - 1))
    for item in table_copies[:1] + [plane_copies[plane] for plane in plane_order] + table_copies[1:]:
        item.start()

    has_left = mine_v > 0
    has_right = mine_v < last
    barrier = pltpu.get_barrier_semaphore()
    for offset in range(1, slabs):
        pl.semaphore_signal(barrier, inc=1, device_id={"gx": at("gx", offset)}, device_id_type=MESH)

    for offset in range(1, groups):
        pl.semaphore_signal(
            barrier, inc=1, device_id={"vert": at("vert", offset)}, device_id_type=MESH
        )

    def square_copy(right, plane, src=None):
        way = 0 if right else 1
        return copy(
            (square_out.at[way] if src is None else src).at[plane], square_recv.at[way, plane],
            square_send_sem.at[way, plane], square_recv_sem.at[way, plane],
            "vert", 1 if right else last,
        )

    def square_hop(hop, planes):
        for right in (True, False):
            way = 0 if right else 1

            @pl.when(mine_v == (hop if right else last - hop))
            def _():
                for plane in planes:
                    if hop == 0:
                        square_copy(right, plane, square_ref).start()
                    else:
                        square_copy(right, plane).wait_recv()
                        square_out[way, plane] = square_ref[plane] + square_recv[way, plane]
                        square_copy(right, plane).start()

    halo_copies = [
        copy(phase_ref.at[:, width - 1], low_halo, halo_send_sem.at[0], halo_recv_sem.at[0], "gx", 1),
        copy(phase_ref.at[:, 0], high_halo, halo_send_sem.at[1], halo_recv_sem.at[1], "gx", slabs - 1),
    ]
    table_copies[0].wait()
    lane_shape = (ny, half)
    for turn, plane in enumerate(plane_order):
        plane_copies[plane].wait()
        for begin in range(0, ny, STEP):
            rows = pl.ds(begin, STEP)
            sums = [jnp.zeros((STEP, nz), jnp.float32) for _ in range(7)]
            for number in range(count):
                value = phase_ref[number, plane, rows]
                value = value * value
                family = family_ref[number]
                for comp in range(6):
                    sums[comp] = sums[comp] + eps_ref[comp, family] * value
                sums[6] = sums[6] + value
            for comp in range(6):
                eigen_ref[comp, rows] = sums[comp]
            square_ref[plane, rows] = sums[6]
        if turn == BARRIER_PLANE:
            pl.semaphore_wait(barrier, slabs + groups - 2)
        if turn >= BARRIER_PLANE:
            square_hop(0, plane_order[: turn + 1] if turn == BARRIER_PLANE else [plane])
        if turn == max(BARRIER_PLANE, 1):
            for item in halo_copies:
                item.start()
        lines = table_right(eigen_ref[...].reshape(6 * ny, nz), z_ref)
        for part in range(2):
            rows = pl.ds((part * width + plane) * ny, ny)
            ends = jnp.zeros(lane_shape, jnp.float32)
            for comp in range(6):
                block = lines[comp * ny : (comp + 1) * ny, part * half : (part + 1) * half]
                lanes = pl.ds(comp % 2 * half, half)
                line_high[comp // 2, rows, lanes], line_low[comp // 2, rows, lanes] = halves(block)
                ends = jnp.where(lane_is(lane_shape, comp), to_lane(block, comp), ends)
            end_high[rows, :], end_low[rows, :] = halves(ends)

    for item in table_copies[1:]:
        item.wait()
    size = 2 * width * ny
    first = first_lane((size, half))
    full_table, edge_table = (y_ref.at[:, pl.ds(index * size, size)] for index in range(2))

    end_modes = table_product(edge_table, end_high[...], end_low[...])
    for pair in range(3):
        modes = table_product(full_table, line_high[pair], line_low[pair])
        for side in range(2):
            comp = 2 * pair + side
            lanes = slice(side * half, (side + 1) * half)
            picked = jnp.where(first, from_lane(end_modes, comp), modes[:, lanes])
            hat_ref[:, comp] = picked.reshape(ny, 2 * width, half)

    def way_of(right):
        if right:
            return right_recv, 0, 1, mine_v == 0
        return left_recv, 1, last, mine_v == last

    def rows_of(group, chunk):
        return pl.ds(group * slabs + chunk * piece, piece)

    def sum_copy(right, turn, chunk):
        recv, way, offset, _ = way_of(right)
        owner = last - turn if right else turn
        return copy(
            hat_ref.at[rows_of(owner, chunk)], recv.at[turn, pl.ds(chunk * piece, piece)],
            sum_send_sem.at[way, turn, chunk], sum_recv_sem.at[way, turn, chunk], "vert", offset,
        )

    def sends_sum(right, turn):
        return mine_v < last - turn if right else mine_v > turn

    def add_sum(right, turn, chunk):
        owner = last - turn if right else turn
        rows = rows_of(owner, chunk)
        sum_copy(right, turn, chunk).wait_recv()
        hat_ref[rows] = hat_ref[rows] + way_of(right)[0][turn, pl.ds(chunk * piece, piece)]

    def during(number, begin, length, action):
        @pl.when((number >= begin) & (number < begin + length))
        def _():
            action(number - begin)

    def pass_sums(right, number):
        at_end = way_of(right)[3]
        for turn in range(last):

            def one(chunk):
                @pl.when(jnp.logical_not(at_end) & sends_sum(right, turn))
                def _():
                    add_sum(right, turn, chunk)
                    sum_copy(right, turn, chunk).start()

            during(number, turn, chunks, one)

    def end_sums(chunk):
        @pl.when(has_left)
        def _():
            add_sum(True, last - mine_v, chunk)

        @pl.when(has_right)
        def _():
            add_sum(False, mine_v, chunk)

    def source_of(chunk, member):
        return chunk + member * chunks

    my_chunk = lax.rem(mine_x, chunks)
    my_place = my_chunk * piece + mine_x // chunks
    mine = mine_v * slabs + my_place

    def cross_copy(place, source, target):
        return copy_to(
            hat_ref.at[mine_v * slabs + place], cross_recv.at[source],
            cross_send_sem.at[place], cross_recv_sem.at[source], "gx", target,
        )

    def back_copy(place, target):
        return copy_to(
            cross_out.at[target], gathered.at[mine_v * slabs + place],
            back_send_sem.at[target], back_recv_sem.at[place], "gx", target,
        )

    def send_cross(chunk):
        for member in range(piece):
            target = source_of(chunk, member)
            place = chunk * piece + member

            @pl.when(target != mine_x)
            def _():
                cross_copy(place, mine_x, target).start()

            @pl.when(target == mine_x)
            def _():
                cross_recv[mine_x] = hat_ref[mine_v * slabs + place]

    def over_others(action):
        def one(offset, carry):
            action(at("gx", offset))
            return carry

        lax.fori_loop(1, slabs, one, 0)

    def solve_row():
        shape = (nx, half)
        y_mode = jnp.full(shape, 0, jnp.int32) + (mine_v * slabs + mine_x)
        x_mode = lax.broadcasted_iota(jnp.int32, shape, 0)
        lane = lax.broadcasted_iota(jnp.int32, shape, 1)
        ends = (y_mode == 0) | (y_mode * 2 == ny)
        upper = y_mode * 2 > ny
        edge = lane == 0
        z_first = jnp.where(edge & upper, half, lane)
        z_second = jnp.where(edge & (upper | ends), half, lane)
        normal_sets = [
            unit_normals(x_mode, y_mode, z_mode, (nx, ny, nz)) for z_mode in (z_first, z_second)
        ]
        over_others(lambda source: cross_copy(0, source, source).wait_recv())
        lines = jnp.concatenate(
            [cross_recv[:, comp].reshape(2 * nx, half) for comp in range(6)], axis=1
        )
        modes = mm(forward_ref[...], stack_rows(lines))
        parts = [
            [modes[i * nx : (i + 1) * nx, comp * half : (comp + 1) * half] for i in range(4)]
            for comp in range(6)
        ]
        stresses = []
        for part in range(2):
            total = None
            for source in range(2):
                strain = [parts[comp][2 * source + part] for comp in range(6)]
                for normals in normal_sets[source]:
                    value = green_stress(strain, normals)
                    total = value if total is None else [a + b for a, b in zip(total, value)]
            stresses.append([0.5 * value for value in total])
        modes = jnp.concatenate([jnp.concatenate(part, axis=1) for part in stresses])
        lines = mm(inverse_ref[...], stack_rows(modes))
        for comp in range(6):
            block = lines[:, comp * half : (comp + 1) * half]
            cross_out[:, comp] = block.reshape(slabs, 2 * width, half)
        over_others(lambda target: back_copy(my_place, target).start())
        gathered[mine] = cross_out[mine_x]

    def gather_copy(right, group, chunk):
        way = 0 if right else 1
        place = gathered.at[rows_of(group, chunk)]
        return copy(
            place, place, gather_send_sem.at[way, group, chunk],
            gather_recv_sem.at[way, group, chunk], "vert", 1 if right else last,
        )

    def spread_copy(right, target, chunk):
        place = gathered.at[rows_of(mine_v, chunk)]
        return copy_to(
            place, place, spread_send_sem.at[target, chunk - relayed],
            gather_recv_sem.at[0 if right else 1, mine_v, chunk], "vert", target,
        )

    def over_targets(chunk, action):
        for distance in reversed(range(1, groups)):
            for right in (True, False):
                target = mine_v + distance if right else mine_v - distance

                @pl.when(target <= last if right else target >= 0)
                def _():
                    action(spread_copy(right, target, chunk))

    def send_gather(chunk):
        for member in range(piece):
            source = source_of(chunk, member)

            @pl.when(source != mine_x)
            def _():
                back_copy(chunk * piece + member, source).wait_recv()

        spread = at_end & (chunk >= relayed)

        @pl.when(jnp.logical_not(spread))
        def _():
            for right, able in ((True, has_right), (False, has_left)):

                @pl.when(able)
                def _():
                    gather_copy(right, mine_v, chunk).start()

        @pl.when(spread)
        def _():
            over_targets(chunk, lambda item: item.start())

    def end_spread(chunk, carry):
        for right, exists, group in ((True, has_left, 0), (False, has_right, last)):

            @pl.when(exists)
            def _():
                gather_copy(right, group, chunk).wait_recv()

        return carry

    def relay_gather(stage, chunk):
        for right, able, exists, group in (
            (True, has_right, mine_v >= stage, mine_v - stage),
            (False, has_left, mine_v + stage <= last, mine_v + stage),
        ):

            first_group = mine_v == stage if right else mine_v + stage == last

            @pl.when(exists & jnp.logical_not(first_group & (chunk >= relayed)))
            def _():
                gather_copy(right, group, chunk).wait_recv()

                @pl.when(able)
                def _():
                    gather_copy(right, group, chunk).start()

    def react(number, carry):
        orient = orient_ref[number]
        kappa = [kappa_ref[dim, orient] for dim in range(3)]
        for plane in range(width):
            value = phase_ref[number, plane]
            low = low_halo[number] if plane == 0 else phase_ref[number, plane - 1]
            high = high_halo[number] if plane == width - 1 else phase_ref[number, plane + 1]
            twice = 2.0 * value
            laplace = kappa[0] * (low + high - twice)
            laplace = laplace + kappa[1] * (
                pltpu.roll(value, 1, 0) + pltpu.roll(value, ny - 1, 0) - twice
            )
            laplace = laplace + kappa[2] * (
                pltpu.roll(value, 1, 1) + pltpu.roll(value, nz - 1, 1) - twice
            )
            square = value * value
            chemical = twice - 6.0 * square + 4.0 * square * value
            chemical = chemical - 2.0 * CROSS_COUPLING * value * square
            base_ref[number, plane] = value - TIME_STEP * (chemical - laplace)
        return carry

    for right in (True, False):

        @pl.when(way_of(right)[3])
        def _():
            def one(number, carry):
                for turn in range(last):
                    during(number, turn, chunks, lambda chunk: sum_copy(right, turn, chunk).start())
                return carry

            lax.fori_loop(0, chunks + last - 1, one, 0)

    lower = mine_v * 2 < groups
    share = 4
    slots = max(
        chunks + GATHER_LAG + last, REACT_SLOT - (-count // share), SQUARE_SLOT + SQUARE_LAG * groups + width
    )

    def slot(number, carry):
        for right in (True, False):

            @pl.when(lower if right else jnp.logical_not(lower))
            def _():
                pass_sums(right, number)
                pass_sums(not right, number - 1)

        def own(chunk):
            end_sums(chunk)
            send_cross(chunk)

        during(number, SUM_LAG, chunks, own)

        during(number, GATHER_LAG, chunks, send_gather)

        @pl.when(number == my_chunk + SOLVE_LAG)
        def _():
            solve_row()

        for stage in range(1, groups):
            during(number, GATHER_LAG + stage, chunks, lambda chunk: relay_gather(stage, chunk))
        for hop in range(1, last):
            for index in range(0, width, SQUARE_SPAN):

                @pl.when(number == SQUARE_SLOT + SQUARE_LAG * (hop - 1) + index // SQUARE_SPAN)
                def _():
                    square_hop(hop, plane_order[index : index + SQUARE_SPAN])

        @pl.when(number == REACT_SLOT)
        def _():
            for item in halo_copies:
                item.wait_recv()

        def react_share(index):
            begin = index * share
            lax.fori_loop(
                jnp.minimum(begin, count), jnp.minimum(begin + share, count), react, 0
            )

        during(number, REACT_SLOT, -(-count // share), react_share)
        return carry

    lax.fori_loop(0, slots, slot, 0)
    lax.fori_loop(relayed, chunks, end_spread, 0)
    for right, at_last in ((True, mine_v == last), (False, mine_v == 0)):

        @pl.when(at_last)
        def _():
            for plane in range(width):
                square_copy(right, plane).wait_recv()

    square_total[...] = square_ref[...]

    @pl.when(has_left)
    def _():
        square_total[...] = square_total[...] + square_recv[0]

    @pl.when(has_right)
    def _():
        square_total[...] = square_total[...] + square_recv[1]

    for item in halo_copies:
        item.wait_send()

    def end_cross(place, carry):
        target = source_of(place // piece, lax.rem(place, piece))

        @pl.when(target != mine_x)
        def _():
            cross_copy(place, mine_x, target).wait_send()

        return carry

    lax.fori_loop(0, slabs, end_cross, 0)
    over_others(lambda target: back_copy(my_place, target).wait_send())

    def end_chunk(chunk, carry):
        for right, able in ((True, has_right), (False, has_left)):
            for turn in range(last):

                @pl.when(sends_sum(right, turn))
                def _():
                    sum_copy(right, turn, chunk).wait_send()

            for stage in range(groups):
                group = mine_v - stage if right else mine_v + stage
                exists = able & ((mine_v >= stage) if right else (mine_v + stage <= last))

                first_group = group == (0 if right else last)

                @pl.when(exists & jnp.logical_not(first_group & (chunk >= relayed)))
                def _():
                    gather_copy(right, group, chunk).wait_send()

        @pl.when(at_end & (chunk >= relayed))
        def _():
            over_targets(chunk, lambda item: item.wait_send())

        return carry

    lax.fori_loop(0, chunks, end_chunk, 0)
    for right, able in ((True, has_right), (False, has_left)):

        @pl.when(able)
        def _():
            for plane in range(width):
                square_copy(right, plane).wait_send()


def update_kernel(
    family_ref, eps_ref, hat_ref, phase_ref, base_ref, square_ref, y_ref, z_ref,
    next_ref, stress_ref, lines_ref,
):
    count, _, ny, nz = next_ref.shape
    width = square_ref.shape[0]
    plane = pl.program_id(0)
    half = nz // 2
    size = 2 * width * ny

    @pl.when(plane == 0)
    def _():
        shape = (size, half)
        first = first_lane(shape)
        ends = jnp.zeros(shape, jnp.float32)
        for comp in range(6):
            block = hat_ref[:, comp].reshape(shape)
            ends = jnp.where(lane_is(shape, comp), to_lane(block, comp), ends)
        full_table, edge_table = (y_ref.at[:, pl.ds(index * size, size)] for index in range(2))
        end_lines = table_product(edge_table, *halves(ends))
        for pair in range(3):
            modes = [hat_ref[:, 2 * pair + side].reshape(shape) for side in range(2)]
            both = table_product(full_table, *halves(jnp.concatenate(modes, axis=1)))
            for side in range(2):
                comp = 2 * pair + side
                lanes = slice(side * half, (side + 1) * half)
                picked = jnp.where(first, from_lane(end_lines, comp), both[:, lanes])
                lines = jnp.concatenate([picked[: size // 2], picked[size // 2 :]], axis=1)
                lines_ref[comp] = lines.reshape(width, ny, nz)

    lines = lines_ref[:, pl.ds(plane, 1)].reshape(6 * ny, nz)
    stress_ref[...] = table_right(lines, z_ref).reshape(6, 1, ny, nz)
    step = 16

    def finish(index, carry):
        rows = pl.ds(pl.multiple_of(index * step, step), step)
        stress = [stress_ref[comp, 0, rows, :] for comp in range(6)]
        shared = (-2.0 * TIME_STEP * CROSS_COUPLING) * square_ref[plane, rows, :]
        for number in range(count):
            family = family_ref[number]
            total = shared
            for comp in range(6):
                factor = eps_ref[comp, family] * (2.0 * TIME_STEP * (1.0 if comp < 3 else 2.0))
                total = total + factor * stress[comp]
            value = phase_ref[number, plane, rows, :]
            next_ref[number, 0, rows, :] = base_ref[number, plane, rows, :] + value * total
        return carry

    lax.fori_loop(0, ny // step, finish, 0)


def body(phase_field, kappa_table, eps_table, orient_index, family_index):
    slabs = lax.axis_size("gx")
    groups = lax.axis_size("vert")
    count, width, ny, nz = phase_field.shape
    half = nz // 2
    whole_rows = slabs * groups == ny and slabs % 2 == 0 and groups >= 2
    if not whole_rows or width * 2 != 8 or half % 128 or ny % 32:
        return general_body(phase_field, kappa_table, eps_table, orient_index, family_index)
    f32 = jnp.float32
    chunks = slabs // 2
    places = np.arange(slabs)
    order = np.concatenate([
        group * slabs + places // 2 + chunks * (places % 2) for group in range(groups)
    ])
    y_forward, y_inverse = (split_table(table) for table in y_tables(ny, width, order))
    z_forward, z_inverse = (split_table(table) for table in z_tables(nz))
    x_forward, x_inverse = (stacked_table(table) for table in x_tables(slabs, width))
    tile = (6, 2 * width, half)
    dma = pltpu.SemaphoreType.DMA
    halo = (count, ny, nz)
    squares = (width, ny, nz)
    tables = (z_forward, y_forward, x_forward, x_inverse)
    in_place = functools.partial(pltpu.with_memory_space_constraint, memory_space=pltpu.HBM)
    small = [in_place(item) for item in (family_index, orient_index, eps_table.T, kappa_table.T)]
    hat, base, phase, square = pl.pallas_call(
        transform_kernel,
        out_shape=(
            pltpu.VMEM((ny, *tile), f32),
            pltpu.VMEM(phase_field.shape, f32),
            pltpu.VMEM(phase_field.shape, f32),
            pltpu.VMEM(squares, f32),
        ),
        in_specs=[SMEM_SPEC] * 4 + [HBM_SPEC] * 5,
        out_specs=(VMEM_SPEC,) * 4,
        scratch_shapes=[
            *[pltpu.VMEM(table.shape, table.dtype) for table in tables],
            pltpu.VMEM((6, ny, nz), f32),
            *[pltpu.VMEM((3, 2 * width * ny, nz), jnp.bfloat16) for _ in range(2)],
            *[pltpu.VMEM((2 * width * ny, half), jnp.bfloat16) for _ in range(2)],
            pltpu.VMEM((ny, *tile), f32),
            *[pltpu.VMEM((groups - 1, slabs, *tile), f32) for _ in range(2)],
            *[pltpu.VMEM((slabs, *tile), f32) for _ in range(2)],
            pltpu.VMEM(halo, f32), pltpu.VMEM(halo, f32),
            pltpu.VMEM(squares, f32),
            pltpu.VMEM((2, *squares), f32), pltpu.VMEM((2, *squares), f32),
            dma((width,)), dma((len(tables),)),
            dma((2, groups - 1, chunks)), dma((2, groups - 1, chunks)),
            dma((slabs,)), dma((slabs,)),
            dma((slabs,)), dma((slabs,)),
            dma((2, groups, chunks)), dma((2, groups, chunks)), dma((groups, max(min(SPREAD, chunks), 1))),
            dma((2, width)), dma((2, width)),
            dma((2,)), dma((2,)),
        ],
        compiler_params=pltpu.CompilerParams(
            vmem_limit_bytes=VMEM_LIMIT, collective_id=0, has_side_effects=True
        ),
        name="transform",
    )(*small, in_place(phase_field), *[in_place(table) for table in tables])
    phase_next, stress = pl.pallas_call(
        update_kernel,
        grid=(width,),
        out_shape=(
            jax.ShapeDtypeStruct(phase_field.shape, f32),
            jax.ShapeDtypeStruct((6, width, ny, nz), f32),
        ),
        in_specs=[SMEM_SPEC] * 2 + [VMEM_SPEC] * 6,
        out_specs=(
            pl.BlockSpec((count, 1, ny, nz), lambda i: (0, i, 0, 0)),
            pl.BlockSpec((6, 1, ny, nz), lambda i: (0, i, 0, 0)),
        ),
        scratch_shapes=[pltpu.VMEM((6, width, ny, nz), f32)],
        compiler_params=pltpu.CompilerParams(vmem_limit_bytes=VMEM_LIMIT),
        name="update",
    )(small[0], small[2], hat, phase, base, square, y_inverse, z_inverse)
    return (phase_next, stress)


def solution(mesh):
    return jax.shard_map(
        body,
        mesh=mesh,
        in_specs=(P("vert", "gx", None, None), P(), P(), P("vert"), P("vert")),
        out_specs=(P("vert", "gx", None, None), P(None, "gx", None, None)),
        check_vma=False,
    )
```

```python
import functools
import math

import jax
import jax.numpy as jnp
import ml_dtypes
import numpy as np
from jax import lax
from jax.experimental import pallas as pl
from jax.experimental.pallas import tpu as pltpu
from jax.sharding import PartitionSpec as P

LAME_LAMBDA = 1.5
SHEAR_MOD = 1.0
TIME_STEP = 0.1
CROSS_COUPLING = 0.02
HIGHEST = lax.Precision.HIGHEST
TENSOR_SLOTS = ((0, 5, 4), (5, 1, 3), (4, 3, 2))
VOIGT_PAIRS = ((0, 0), (1, 1), (2, 2), (1, 2), (0, 2), (0, 1))
PAIRED_FORMS = {1: "pcxyz,pxqk->qckyz", 2: "pcxyz,pyqk->qcxkz", 3: "pcxyz,pzqk->qcxyk"}


def with_halo(block, sides, width):
    for axis, dim in sides:
        count = lax.axis_size(axis)
        forward = [(i, i + 1) for i in range(count - 1)]
        forward.append((count - 1, 0))
        backward = [(target, source) for source, target in forward]
        low = lax.ppermute(
            lax.slice_in_dim(block, block.shape[dim] - width, None, axis=dim), axis, forward
        )
        high = lax.ppermute(lax.slice_in_dim(block, 0, width, axis=dim), axis, backward)
        block = jnp.concatenate([low, block, high], axis=dim)
    return block


def signed_wave(first_row, row_count, full_count):
    positions = first_row + jnp.arange(row_count, dtype=jnp.int32)
    shifted = jnp.where(positions * 2 >= full_count, positions - full_count, positions)
    return shifted.astype(jnp.float32) / full_count


def wave_normals(x_wave, y_wave, z_wave):
    x_grid = x_wave[:, None, None]
    y_grid = y_wave[None, :, None]
    z_grid = z_wave[None, None, :]
    length_sq = x_grid * x_grid + y_grid * y_grid + z_grid * z_grid
    positive = length_sq > 0
    safe_length = jnp.where(positive, length_sq, 1.0)
    inverse_len = jnp.where(positive, lax.rsqrt(safe_length), 0.0)
    return [x_grid * inverse_len, y_grid * inverse_len, z_grid * inverse_len]


def green_stress(strain, normals):
    trace_strain = strain[0] + strain[1] + strain[2]
    stiffened = [
        (
            LAME_LAMBDA * trace_strain + 2.0 * SHEAR_MOD * strain[number]
            if number < 3
            else 2.0 * SHEAR_MOD * strain[number]
        )
        for number in range(6)
    ]
    traction = [
        sum(
            (
                stiffened[TENSOR_SLOTS[row_axis][col_axis]] * normals[col_axis]
                for col_axis in range(3)
            )
        )
        for row_axis in range(3)
    ]
    normal_part = normals[0] * traction[0] + normals[1] * traction[1] + normals[2] * traction[2]
    coupling = (LAME_LAMBDA + SHEAR_MOD) / (LAME_LAMBDA + 2.0 * SHEAR_MOD)
    shifted = [
        (traction[row_axis] - normals[row_axis] * normal_part * coupling) / SHEAR_MOD
        for row_axis in range(3)
    ]
    excess = [
        0.5
        * (
            normals[VOIGT_PAIRS[number][0]] * shifted[VOIGT_PAIRS[number][1]]
            + normals[VOIGT_PAIRS[number][1]] * shifted[VOIGT_PAIRS[number][0]]
        )
        - strain[number]
        for number in range(6)
    ]
    trace_excess = excess[0] + excess[1] + excess[2]
    result = [
        (
            LAME_LAMBDA * trace_excess + 2.0 * SHEAR_MOD * excess[number]
            if number < 3
            else 2.0 * SHEAR_MOD * excess[number]
        )
        for number in range(6)
    ]
    return result


def reaction_update(variant, laplace, driving, square_sum):
    chemical = 2.0 * variant - 6.0 * variant * variant + 4.0 * variant * variant * variant
    chemical = chemical + 2.0 * CROSS_COUPLING * variant * (square_sum - variant * variant)
    chemical = chemical - 2.0 * variant * driving - laplace
    return variant - TIME_STEP * chemical


def dft_tables(length):
    positions = jnp.arange(length, dtype=jnp.int32)
    products = positions[:, None] * positions[None, :] % length
    angles = products.astype(jnp.float32) * (2.0 * math.pi / length)
    return (jnp.cos(angles), jnp.sin(angles))


def paired_table(length, inverse):
    cosine_table, sine_table = dft_tables(length)
    cross_term = sine_table if inverse else -sine_table
    from_real = jnp.stack([cosine_table, cross_term], axis=1)
    from_imag = jnp.stack([-cross_term, cosine_table], axis=1)
    table = jnp.stack([from_real, from_imag])
    if inverse:
        table = table * (1.0 / length)
    return table


def transform(real_part, imag_part, axis_dim, inverse):
    length = real_part.shape[axis_dim]
    table = paired_table(length, inverse)
    if imag_part is None:
        pattern = PAIRED_FORMS[axis_dim].replace("p", "")
        result = jnp.einsum(pattern, real_part, table[0], precision=HIGHEST)
        return (result[0], result[1])
    stacked = jnp.stack([real_part, imag_part])
    result = jnp.einsum(PAIRED_FORMS[axis_dim], stacked, table, precision=HIGHEST)
    return (result[0], result[1])


def transform_real(real_part, imag_part, axis_dim):
    length = real_part.shape[axis_dim]
    table = paired_table(length, True)[:, :, 0, :]
    pattern = PAIRED_FORMS[axis_dim].replace("q", "")
    stacked = jnp.stack([real_part, imag_part])
    return jnp.einsum(pattern, stacked, table, precision=HIGHEST)


def forward_x(halves):
    return transform(halves[0], halves[1], 1, False)


def forward_y(halves):
    return transform(halves[0], halves[1], 2, False)


def backward_x(halves):
    return transform(halves[0], halves[1], 1, True)


def backward_z(halves):
    return transform_real(halves[0], halves[1], 3)


def general_body(phase_field, kappa_table, eps_table, orient_index, family_index):
    slab_count = lax.axis_size("gx")
    count_var, slab_width, width_y, width_z = phase_field.shape
    total_x = slab_width * slab_count
    family_hot = (
        family_index[:, None] == jnp.arange(eps_table.shape[0], dtype=jnp.int32)[None, :]
    ).astype(jnp.float32)
    orient_hot = (
        orient_index[:, None] == jnp.arange(kappa_table.shape[0], dtype=jnp.int32)[None, :]
    ).astype(jnp.float32)
    eps_var = jnp.dot(family_hot, eps_table, precision=HIGHEST)
    kappa_var = jnp.dot(orient_hot, kappa_table, precision=HIGHEST)
    padded = with_halo(phase_field, (("gx", 1),), 1)
    squared = phase_field * phase_field
    eigen_sum = jnp.einsum("vk,vxyz->kxyz", eps_var, squared, precision=HIGHEST)
    local_square = jnp.sum(squared, axis=0)
    eigen_sum = lax.psum_scatter(eigen_sum, "vert", scatter_dimension=2, tiled=True)
    square_sum = lax.psum(local_square, "vert")
    real_part, imag_part = transform(eigen_sum, None, 3, False)
    real_part, imag_part = forward_x(
        (
            lax.all_to_all(real_part, "gx", split_axis=3, concat_axis=1, tiled=True),
            lax.all_to_all(imag_part, "gx", split_axis=3, concat_axis=1, tiled=True),
        )
    )
    real_part, imag_part = forward_y(
        (
            lax.all_to_all(real_part, "vert", split_axis=1, concat_axis=2, tiled=True),
            lax.all_to_all(imag_part, "vert", split_axis=1, concat_axis=2, tiled=True),
        )
    )
    x_start = lax.axis_index("vert") * real_part.shape[1]
    z_start = lax.axis_index("gx") * real_part.shape[3]
    normals = wave_normals(
        signed_wave(x_start, real_part.shape[1], total_x),
        signed_wave(0, width_y, width_y),
        signed_wave(z_start, real_part.shape[3], width_z),
    )
    real_part = jnp.stack(green_stress(real_part, normals))
    imag_part = jnp.stack(green_stress(imag_part, normals))
    real_part, imag_part = transform(real_part, imag_part, 2, True)
    real_part, imag_part = backward_x(
        (
            lax.all_to_all(real_part, "vert", split_axis=2, concat_axis=1, tiled=True),
            lax.all_to_all(imag_part, "vert", split_axis=2, concat_axis=1, tiled=True),
        )
    )
    stress = backward_z(
        (
            lax.all_to_all(real_part, "gx", split_axis=1, concat_axis=3, tiled=True),
            lax.all_to_all(imag_part, "gx", split_axis=1, concat_axis=3, tiled=True),
        )
    )
    stress = lax.all_gather(stress, "vert", axis=2, tiled=True)
    weights = jnp.array([1.0, 1.0, 1.0, 2.0, 2.0, 2.0], jnp.float32)
    driving = jnp.einsum("vk,kxyz->vxyz", eps_var * weights[None, :], stress, precision=HIGHEST)
    kappa_x = kappa_var[:, 0][:, None, None, None]
    kappa_y = kappa_var[:, 1][:, None, None, None]
    kappa_z = kappa_var[:, 2][:, None, None, None]
    laplace = kappa_x * (padded[:, 2:] + padded[:, :-2] - 2.0 * phase_field)
    laplace = laplace + kappa_y * (
        jnp.roll(phase_field, 1, 2) + jnp.roll(phase_field, -1, 2) - 2.0 * phase_field
    )
    laplace = laplace + kappa_z * (
        jnp.roll(phase_field, 1, 3) + jnp.roll(phase_field, -1, 3) - 2.0 * phase_field
    )
    phase_next = reaction_update(phase_field, laplace, driving, square_sum[None])
    return (phase_next, stress)


MESH = pl.DeviceIdType.MESH
VMEM_SPEC = pl.BlockSpec(memory_space=pltpu.VMEM)
SMEM_SPEC = pl.BlockSpec(memory_space=pltpu.SMEM)
HBM_SPEC = pl.BlockSpec(memory_space=pltpu.HBM)
VMEM_LIMIT = 20 * 1024 * 1024
SUM_LAG = 2
SOLVE_LAG = 3
GATHER_LAG = 5
SQUARE_SLOT = 1
SQUARE_LAG = 1
SQUARE_SPAN = 1
STEP = 16
BARRIER_PLANE = 1
REACT_SLOT = 5
SPREAD = 4


def split_table(table):
    high = table.astype(np.float32).astype(ml_dtypes.bfloat16)
    low = (table - high.astype(np.float64)).astype(np.float32).astype(ml_dtypes.bfloat16)
    return jnp.asarray(np.stack([high, low]))


def stacked_table(table):
    high, low = split_table(table)
    return jnp.concatenate([high, high, low], axis=1)


def trig(length):
    positions = np.arange(length)
    angles = (positions[:, None] * positions[None, :] % length) * (2.0 * np.pi / length)
    return np.cos(angles), np.sin(angles)


def z_tables(length):
    half = length // 2
    cosine, sine = trig(length)
    forward = np.concatenate([cosine[:, : half + 1], -sine[:, 1:half]], axis=1)
    weight = np.full(length, 2.0)
    weight[[0, half]] = 1.0
    inverse = forward.T * weight[:, None] / length
    return forward, inverse


def y_tables(length, width, order):
    half = length // 2
    cosine, sine = trig(length)
    eye = np.eye(width)
    full = np.array([[cosine, sine], [-sine, cosine]])
    edge = np.zeros_like(full)
    low, high, ends = slice(1, half), slice(half + 1, length), [0, half]
    edge[0, 0, low], edge[1, 0, low] = cosine[low], -sine[low]
    edge[0, 1, high], edge[1, 1, high] = cosine[high], -sine[high]
    edge[0, 0, ends], edge[1, 1, ends] = cosine[ends], cosine[ends]
    weight = np.full(length, 2.0)
    weight[ends] = 1.0
    forward, inverse = [], []
    size = 2 * width * length
    for table, scale in ((full, np.ones(length)), (edge, weight)):
        grid = np.einsum("abky,xw->kaxbwy", table, eye)[order]
        forward.append(grid.reshape(size, size))
        grid = np.einsum("abky,xw,k->bwykax", table, eye, scale / length)[:, :, :, order]
        inverse.append(grid.reshape(size, size))
    return np.concatenate(forward), np.concatenate(inverse)


def x_tables(slabs, width):
    length = slabs * width
    cosine, sine = (part.reshape(length, slabs, width) for part in trig(length))
    zero = np.zeros_like(cosine)
    from_real = np.stack([np.stack([cosine, zero], 2), np.stack([-sine, zero], 2)])
    from_imag = np.stack([np.stack([zero, sine], 2), np.stack([zero, cosine], 2)])
    rows = np.stack([from_real, from_imag])
    forward = rows.reshape(4 * length, 2 * length)
    inverse = (rows[0] + rows[1]).reshape(2 * length, 2 * length).T / length
    return forward, inverse


def halves(value):
    high = value.astype(jnp.bfloat16)
    return high, (value - high.astype(jnp.float32)).astype(jnp.bfloat16)


def mm(left, right):
    return jnp.dot(left, right, preferred_element_type=jnp.float32)


def table_right(value, table_ref):
    high, low = halves(value)
    return mm(high, table_ref[0]) + (mm(low, table_ref[0]) + mm(high, table_ref[1]))


def stack_rows(value):
    high, low = halves(value)
    return jnp.concatenate([high, low, high])


def table_product(table_ref, high, low):
    return mm(table_ref[0], high) + (mm(table_ref[0], low) + mm(table_ref[1], high))


def lane_is(shape, number):
    return lax.broadcasted_iota(jnp.int32, shape, len(shape) - 1) == number


def to_lane(value, number):
    return pltpu.roll(value, number, 1) if number else value


def from_lane(value, number):
    return pltpu.roll(value, value.shape[1] - number, 1) if number else value


def first_lane(shape):
    return lax.broadcasted_iota(jnp.int32, shape, len(shape) - 1) == 0


def signed(position, full):
    return jnp.where(position * 2 >= full, position - full, position)


def unit_normals(x_mode, y_mode, z_mode, sizes):
    pair = []
    for flip in (False, True):
        waves = []
        for mode, full in zip((x_mode, y_mode, z_mode), sizes):
            wave = signed(mode, full)
            if flip:
                wave = jnp.where(mode * 2 == full, -wave, wave)
            waves.append(wave.astype(jnp.float32) * (1.0 / full))
        length_sq = waves[0] * waves[0] + waves[1] * waves[1] + waves[2] * waves[2]
        positive = length_sq > 0
        inverse = jnp.where(positive, lax.rsqrt(jnp.where(positive, length_sq, 1.0)), 0.0)
        pair.append([wave * inverse for wave in waves])
    return pair


def transform_kernel(
    family_ref, orient_ref, eps_ref, kappa_ref, phase_hbm, z_hbm, y_hbm, forward_hbm, inverse_hbm,
    gathered, base_ref, phase_ref, square_total,
    z_ref, y_ref, forward_ref, inverse_ref,
    eigen_ref, line_high, line_low, end_high, end_low, hat_ref, right_recv, left_recv, cross_recv, cross_out, low_halo, high_halo,
    square_ref, square_recv, square_out,
    plane_sem, table_sem, sum_send_sem, sum_recv_sem, cross_send_sem, cross_recv_sem,
    back_send_sem, back_recv_sem, gather_send_sem, gather_recv_sem, spread_send_sem,
    square_send_sem, square_recv_sem, halo_send_sem, halo_recv_sem,
):
    slabs = lax.axis_size("gx")
    groups = lax.axis_size("vert")
    mine_x = lax.axis_index("gx")
    mine_v = lax.axis_index("vert")
    count, width, ny, nz = phase_ref.shape
    nx = slabs * width
    half = nz // 2
    last = groups - 1
    chunks = sum_send_sem.shape[2]
    piece = slabs // chunks
    relayed = max(chunks - SPREAD, 0)
    at_end = (mine_v == 0) | (mine_v == last)
    step = 32

    def at(axis, offset):
        if axis == "gx":
            return lax.rem(mine_x + offset, slabs)
        return lax.rem(mine_v + offset, groups)

    def copy_to(src, dst, send_sem, recv_sem, axis, place):
        return pltpu.make_async_remote_copy(
            src_ref=src, dst_ref=dst, send_sem=send_sem, recv_sem=recv_sem,
            device_id={axis: place}, device_id_type=MESH,
        )

    def copy(src, dst, send_sem, recv_sem, axis, offset):
        return copy_to(src, dst, send_sem, recv_sem, axis, at(axis, offset))

    plane_copies = [
        pltpu.make_async_copy(phase_hbm.at[:, plane], phase_ref.at[:, plane], plane_sem.at[plane])
        for plane in range(width)
    ]
    table_copies = [
        pltpu.make_async_copy(src, dst, table_sem.at[index])
        for index, (src, dst) in enumerate((
            (z_hbm, z_ref), (y_hbm, y_ref), (forward_hbm, forward_ref), (inverse_hbm, inverse_ref),
        ))
    ]
    plane_order = [0, width - 1] + list(range(1, width - 1))
    for item in table_copies[:1] + [plane_copies[plane] for plane in plane_order] + table_copies[1:]:
        item.start()

    has_left = mine_v > 0
    has_right = mine_v < last
    barrier = pltpu.get_barrier_semaphore()
    for offset in range(1, slabs):
        pl.semaphore_signal(barrier, inc=1, device_id={"gx": at("gx", offset)}, device_id_type=MESH)

    for offset in range(1, groups):
        pl.semaphore_signal(
            barrier, inc=1, device_id={"vert": at("vert", offset)}, device_id_type=MESH
        )

    def square_copy(right, plane, src=None):
        way = 0 if right else 1
        return copy(
            (square_out.at[way] if src is None else src).at[plane], square_recv.at[way, plane],
            square_send_sem.at[way, plane], square_recv_sem.at[way, plane],
            "vert", 1 if right else last,
        )

    def square_hop(hop, planes):
        for right in (True, False):
            way = 0 if right else 1

            @pl.when(mine_v == (hop if right else last - hop))
            def _():
                for plane in planes:
                    if hop == 0:
                        square_copy(right, plane, square_ref).start()
                    else:
                        square_copy(right, plane).wait_recv()
                        square_out[way, plane] = square_ref[plane] + square_recv[way, plane]
                        square_copy(right, plane).start()

    halo_copies = [
        copy(phase_ref.at[:, width - 1], low_halo, halo_send_sem.at[0], halo_recv_sem.at[0], "gx", 1),
        copy(phase_ref.at[:, 0], high_halo, halo_send_sem.at[1], halo_recv_sem.at[1], "gx", slabs - 1),
    ]
    table_copies[0].wait()
    lane_shape = (ny, half)
    for turn, plane in enumerate(plane_order):
        plane_copies[plane].wait()
        for begin in range(0, ny, STEP):
            rows = pl.ds(begin, STEP)
            sums = [jnp.zeros((STEP, nz), jnp.float32) for _ in range(7)]
            for number in range(count):
                value = phase_ref[number, plane, rows]
                value = value * value
                family = family_ref[number]
                for comp in range(6):
                    sums[comp] = sums[comp] + eps_ref[comp, family] * value
                sums[6] = sums[6] + value
            for comp in range(6):
                eigen_ref[comp, rows] = sums[comp]
            square_ref[plane, rows] = sums[6]
        if turn == BARRIER_PLANE:
            pl.semaphore_wait(barrier, slabs + groups - 2)
        if turn >= BARRIER_PLANE:
            square_hop(0, plane_order[: turn + 1] if turn == BARRIER_PLANE else [plane])
        if turn == max(BARRIER_PLANE, 1):
            for item in halo_copies:
                item.start()
        lines = table_right(eigen_ref[...].reshape(6 * ny, nz), z_ref)
        for part in range(2):
            rows = pl.ds((part * width + plane) * ny, ny)
            ends = jnp.zeros(lane_shape, jnp.float32)
            for comp in range(6):
                block = lines[comp * ny : (comp + 1) * ny, part * half : (part + 1) * half]
                lanes = pl.ds(comp % 2 * half, half)
                line_high[comp // 2, rows, lanes], line_low[comp // 2, rows, lanes] = halves(block)
                ends = jnp.where(lane_is(lane_shape, comp), to_lane(block, comp), ends)
            end_high[rows, :], end_low[rows, :] = halves(ends)

    for item in table_copies[1:]:
        item.wait()
    size = 2 * width * ny
    first = first_lane((size, half))
    full_table, edge_table = (y_ref.at[:, pl.ds(index * size, size)] for index in range(2))

    end_modes = table_product(edge_table, end_high[...], end_low[...])
    for pair in range(3):
        modes = table_product(full_table, line_high[pair], line_low[pair])
        for side in range(2):
            comp = 2 * pair + side
            lanes = slice(side * half, (side + 1) * half)
            picked = jnp.where(first, from_lane(end_modes, comp), modes[:, lanes])
            hat_ref[:, comp] = picked.reshape(ny, 2 * width, half)

    def way_of(right):
        if right:
            return right_recv, 0, 1, mine_v == 0
        return left_recv, 1, last, mine_v == last

    def rows_of(group, chunk):
        return pl.ds(group * slabs + chunk * piece, piece)

    def sum_copy(right, turn, chunk):
        recv, way, offset, _ = way_of(right)
        owner = last - turn if right else turn
        return copy(
            hat_ref.at[rows_of(owner, chunk)], recv.at[turn, pl.ds(chunk * piece, piece)],
            sum_send_sem.at[way, turn, chunk], sum_recv_sem.at[way, turn, chunk], "vert", offset,
        )

    def sends_sum(right, turn):
        return mine_v < last - turn if right else mine_v > turn

    def add_sum(right, turn, chunk):
        owner = last - turn if right else turn
        rows = rows_of(owner, chunk)
        sum_copy(right, turn, chunk).wait_recv()
        hat_ref[rows] = hat_ref[rows] + way_of(right)[0][turn, pl.ds(chunk * piece, piece)]

    def during(number, begin, length, action):
        @pl.when((number >= begin) & (number < begin + length))
        def _():
            action(number - begin)

    def pass_sums(right, number):
        at_end = way_of(right)[3]
        for turn in range(last):

            def one(chunk):
                @pl.when(jnp.logical_not(at_end) & sends_sum(right, turn))
                def _():
                    add_sum(right, turn, chunk)
                    sum_copy(right, turn, chunk).start()

            during(number, turn, chunks, one)

    def end_sums(chunk):
        @pl.when(has_left)
        def _():
            add_sum(True, last - mine_v, chunk)

        @pl.when(has_right)
        def _():
            add_sum(False, mine_v, chunk)

    def source_of(chunk, member):
        return chunk + member * chunks

    my_chunk = lax.rem(mine_x, chunks)
    my_place = my_chunk * piece + mine_x // chunks
    mine = mine_v * slabs + my_place

    def cross_copy(place, source, target):
        return copy_to(
            hat_ref.at[mine_v * slabs + place], cross_recv.at[source],
            cross_send_sem.at[place], cross_recv_sem.at[source], "gx", target,
        )

    def back_copy(place, target):
        return copy_to(
            cross_out.at[target], gathered.at[mine_v * slabs + place],
            back_send_sem.at[target], back_recv_sem.at[place], "gx", target,
        )

    def send_cross(chunk):
        for member in range(piece):
            target = source_of(chunk, member)
            place = chunk * piece + member

            @pl.when(target != mine_x)
            def _():
                cross_copy(place, mine_x, target).start()

            @pl.when(target == mine_x)
            def _():
                cross_recv[mine_x] = hat_ref[mine_v * slabs + place]

    def over_others(action):
        def one(offset, carry):
            action(at("gx", offset))
            return carry

        lax.fori_loop(1, slabs, one, 0)

    def solve_row():
        shape = (nx, half)
        y_mode = jnp.full(shape, 0, jnp.int32) + (mine_v * slabs + mine_x)
        x_mode = lax.broadcasted_iota(jnp.int32, shape, 0)
        lane = lax.broadcasted_iota(jnp.int32, shape, 1)
        ends = (y_mode == 0) | (y_mode * 2 == ny)
        upper = y_mode * 2 > ny
        edge = lane == 0
        z_first = jnp.where(edge & upper, half, lane)
        z_second = jnp.where(edge & (upper | ends), half, lane)
        normal_sets = [
            unit_normals(x_mode, y_mode, z_mode, (nx, ny, nz)) for z_mode in (z_first, z_second)
        ]
        over_others(lambda source: cross_copy(0, source, source).wait_recv())
        lines = jnp.concatenate(
            [cross_recv[:, comp].reshape(2 * nx, half) for comp in range(6)], axis=1
        )
        modes = mm(forward_ref[...], stack_rows(lines))
        parts = [
            [modes[i * nx : (i + 1) * nx, comp * half : (comp + 1) * half] for i in range(4)]
            for comp in range(6)
        ]
        stresses = []
        for part in range(2):
            total = None
            for source in range(2):
                strain = [parts[comp][2 * source + part] for comp in range(6)]
                for normals in normal_sets[source]:
                    value = green_stress(strain, normals)
                    total = value if total is None else [a + b for a, b in zip(total, value)]
            stresses.append([0.5 * value for value in total])
        modes = jnp.concatenate([jnp.concatenate(part, axis=1) for part in stresses])
        lines = mm(inverse_ref[...], stack_rows(modes))
        for comp in range(6):
            block = lines[:, comp * half : (comp + 1) * half]
            cross_out[:, comp] = block.reshape(slabs, 2 * width, half)
        over_others(lambda target: back_copy(my_place, target).start())
        gathered[mine] = cross_out[mine_x]

    def gather_copy(right, group, chunk):
        way = 0 if right else 1
        place = gathered.at[rows_of(group, chunk)]
        return copy(
            place, place, gather_send_sem.at[way, group, chunk],
            gather_recv_sem.at[way, group, chunk], "vert", 1 if right else last,
        )

    def spread_copy(right, target, chunk):
        place = gathered.at[rows_of(mine_v, chunk)]
        return copy_to(
            place, place, spread_send_sem.at[target, chunk - relayed],
            gather_recv_sem.at[0 if right else 1, mine_v, chunk], "vert", target,
        )

    def over_targets(chunk, action):
        for distance in reversed(range(1, groups)):
            for right in (True, False):
                target = mine_v + distance if right else mine_v - distance

                @pl.when(target <= last if right else target >= 0)
                def _():
                    action(spread_copy(right, target, chunk))

    def send_gather(chunk):
        for member in range(piece):
            source = source_of(chunk, member)

            @pl.when(source != mine_x)
            def _():
                back_copy(chunk * piece + member, source).wait_recv()

        spread = (at_end & (chunk >= relayed)) | (chunk == chunks - 1)

        @pl.when(jnp.logical_not(spread))
        def _():
            for right, able in ((True, has_right), (False, has_left)):

                @pl.when(able)
                def _():
                    gather_copy(right, mine_v, chunk).start()

        @pl.when(spread)
        def _():
            over_targets(chunk, lambda item: item.start())

    def end_spread(chunk, carry):
        for right, exists, group in ((True, has_left, 0), (False, has_right, last)):

            @pl.when(exists)
            def _():
                gather_copy(right, group, chunk).wait_recv()

            for middle in range(1, last):

                @pl.when((chunk == chunks - 1) & (mine_v > middle if right else mine_v < middle))
                def _():
                    gather_copy(right, middle, chunk).wait_recv()

        return carry

    def relay_gather(stage, chunk):
        for right, able, exists, group in (
            (True, has_right, mine_v >= stage, mine_v - stage),
            (False, has_left, mine_v + stage <= last, mine_v + stage),
        ):

            first_group = mine_v == stage if right else mine_v + stage == last

            @pl.when(exists & (chunk < chunks - 1) & jnp.logical_not(first_group & (chunk >= relayed)))
            def _():
                gather_copy(right, group, chunk).wait_recv()

                @pl.when(able)
                def _():
                    gather_copy(right, group, chunk).start()

    def react(number, carry):
        orient = orient_ref[number]
        kappa = [kappa_ref[dim, orient] for dim in range(3)]
        for plane in range(width):
            value = phase_ref[number, plane]
            low = low_halo[number] if plane == 0 else phase_ref[number, plane - 1]
            high = high_halo[number] if plane == width - 1 else phase_ref[number, plane + 1]
            twice = 2.0 * value
            laplace = kappa[0] * (low + high - twice)
            laplace = laplace + kappa[1] * (
                pltpu.roll(value, 1, 0) + pltpu.roll(value, ny - 1, 0) - twice
            )
            laplace = laplace + kappa[2] * (
                pltpu.roll(value, 1, 1) + pltpu.roll(value, nz - 1, 1) - twice
            )
            square = value * value
            chemical = twice - 6.0 * square + 4.0 * square * value
            chemical = chemical - 2.0 * CROSS_COUPLING * value * square
            base_ref[number, plane] = value - TIME_STEP * (chemical - laplace)
        return carry

    for right in (True, False):

        @pl.when(way_of(right)[3])
        def _():
            def one(number, carry):
                for turn in range(last):
                    during(number, turn, chunks, lambda chunk: sum_copy(right, turn, chunk).start())
                return carry

            lax.fori_loop(0, chunks + last - 1, one, 0)

    lower = mine_v * 2 < groups
    share = 4
    slots = max(
        chunks + GATHER_LAG + last, REACT_SLOT - (-count // share), SQUARE_SLOT + SQUARE_LAG * groups + width
    )

    def slot(number, carry):
        for right in (True, False):

            @pl.when(lower if right else jnp.logical_not(lower))
            def _():
                pass_sums(right, number)
                pass_sums(not right, number - 1)

        def own(chunk):
            end_sums(chunk)
            send_cross(chunk)

        during(number, SUM_LAG, chunks, own)

        during(number, GATHER_LAG, chunks, send_gather)

        @pl.when(number == my_chunk + SOLVE_LAG)
        def _():
            solve_row()

        for stage in range(1, groups):
            during(number, GATHER_LAG + stage, chunks, lambda chunk: relay_gather(stage, chunk))
        for hop in range(1, last):
            for index in range(0, width, SQUARE_SPAN):

                @pl.when(number == SQUARE_SLOT + SQUARE_LAG * (hop - 1) + index // SQUARE_SPAN)
                def _():
                    square_hop(hop, plane_order[index : index + SQUARE_SPAN])

        @pl.when(number == REACT_SLOT)
        def _():
            for item in halo_copies:
                item.wait_recv()

        def react_share(index):
            begin = index * share
            lax.fori_loop(
                jnp.minimum(begin, count), jnp.minimum(begin + share, count), react, 0
            )

        during(number, REACT_SLOT, -(-count // share), react_share)
        return carry

    lax.fori_loop(0, slots, slot, 0)
    lax.fori_loop(relayed, chunks, end_spread, 0)
    for right, at_last in ((True, mine_v == last), (False, mine_v == 0)):

        @pl.when(at_last)
        def _():
            for plane in range(width):
                square_copy(right, plane).wait_recv()

    square_total[...] = square_ref[...]

    @pl.when(has_left)
    def _():
        square_total[...] = square_total[...] + square_recv[0]

    @pl.when(has_right)
    def _():
        square_total[...] = square_total[...] + square_recv[1]

    for item in halo_copies:
        item.wait_send()

    def end_cross(place, carry):
        target = source_of(place // piece, lax.rem(place, piece))

        @pl.when(target != mine_x)
        def _():
            cross_copy(place, mine_x, target).wait_send()

        return carry

    lax.fori_loop(0, slabs, end_cross, 0)
    over_others(lambda target: back_copy(my_place, target).wait_send())

    def end_chunk(chunk, carry):
        for right, able in ((True, has_right), (False, has_left)):
            for turn in range(last):

                @pl.when(sends_sum(right, turn))
                def _():
                    sum_copy(right, turn, chunk).wait_send()

            for stage in range(groups):
                group = mine_v - stage if right else mine_v + stage
                exists = able & ((mine_v >= stage) if right else (mine_v + stage <= last))

                first_group = group == (0 if right else last)

                @pl.when(exists & (chunk < chunks - 1) & jnp.logical_not(first_group & (chunk >= relayed)))
                def _():
                    gather_copy(right, group, chunk).wait_send()

        @pl.when((at_end & (chunk >= relayed)) | (chunk == chunks - 1))
        def _():
            over_targets(chunk, lambda item: item.wait_send())

        return carry

    lax.fori_loop(0, chunks, end_chunk, 0)
    for right, able in ((True, has_right), (False, has_left)):

        @pl.when(able)
        def _():
            for plane in range(width):
                square_copy(right, plane).wait_send()


def update_kernel(
    family_ref, eps_ref, hat_ref, phase_ref, base_ref, square_ref, y_ref, z_ref,
    next_ref, stress_ref, lines_ref,
):
    count, _, ny, nz = next_ref.shape
    width = square_ref.shape[0]
    plane = pl.program_id(0)
    half = nz // 2
    size = 2 * width * ny

    @pl.when(plane == 0)
    def _():
        shape = (size, half)
        first = first_lane(shape)
        ends = jnp.zeros(shape, jnp.float32)
        for comp in range(6):
            block = hat_ref[:, comp].reshape(shape)
            ends = jnp.where(lane_is(shape, comp), to_lane(block, comp), ends)
        full_table, edge_table = (y_ref.at[:, pl.ds(index * size, size)] for index in range(2))
        end_lines = table_product(edge_table, *halves(ends))
        for pair in range(3):
            modes = [hat_ref[:, 2 * pair + side].reshape(shape) for side in range(2)]
            both = table_product(full_table, *halves(jnp.concatenate(modes, axis=1)))
            for side in range(2):
                comp = 2 * pair + side
                lanes = slice(side * half, (side + 1) * half)
                picked = jnp.where(first, from_lane(end_lines, comp), both[:, lanes])
                lines = jnp.concatenate([picked[: size // 2], picked[size // 2 :]], axis=1)
                lines_ref[comp] = lines.reshape(width, ny, nz)

    lines = lines_ref[:, pl.ds(plane, 1)].reshape(6 * ny, nz)
    stress_ref[...] = table_right(lines, z_ref).reshape(6, 1, ny, nz)
    step = 16

    def finish(index, carry):
        rows = pl.ds(pl.multiple_of(index * step, step), step)
        stress = [stress_ref[comp, 0, rows, :] for comp in range(6)]
        shared = (-2.0 * TIME_STEP * CROSS_COUPLING) * square_ref[plane, rows, :]
        for number in range(count):
            family = family_ref[number]
            total = shared
            for comp in range(6):
                factor = eps_ref[comp, family] * (2.0 * TIME_STEP * (1.0 if comp < 3 else 2.0))
                total = total + factor * stress[comp]
            value = phase_ref[number, plane, rows, :]
            next_ref[number, 0, rows, :] = base_ref[number, plane, rows, :] + value * total
        return carry

    lax.fori_loop(0, ny // step, finish, 0)


def body(phase_field, kappa_table, eps_table, orient_index, family_index):
    slabs = lax.axis_size("gx")
    groups = lax.axis_size("vert")
    count, width, ny, nz = phase_field.shape
    half = nz // 2
    whole_rows = slabs * groups == ny and slabs % 2 == 0 and groups >= 2
    if not whole_rows or width * 2 != 8 or half % 128 or ny % 32:
        return general_body(phase_field, kappa_table, eps_table, orient_index, family_index)
    f32 = jnp.float32
    chunks = slabs // 2
    places = np.arange(slabs)
    order = np.concatenate([
        group * slabs + places // 2 + chunks * (places % 2) for group in range(groups)
    ])
    y_forward, y_inverse = (split_table(table) for table in y_tables(ny, width, order))
    z_forward, z_inverse = (split_table(table) for table in z_tables(nz))
    x_forward, x_inverse = (stacked_table(table) for table in x_tables(slabs, width))
    tile = (6, 2 * width, half)
    dma = pltpu.SemaphoreType.DMA
    halo = (count, ny, nz)
    squares = (width, ny, nz)
    tables = (z_forward, y_forward, x_forward, x_inverse)
    in_place = functools.partial(pltpu.with_memory_space_constraint, memory_space=pltpu.HBM)
    small = [in_place(item) for item in (family_index, orient_index, eps_table.T, kappa_table.T)]
    hat, base, phase, square = pl.pallas_call(
        transform_kernel,
        out_shape=(
            pltpu.VMEM((ny, *tile), f32),
            pltpu.VMEM(phase_field.shape, f32),
            pltpu.VMEM(phase_field.shape, f32),
            pltpu.VMEM(squares, f32),
        ),
        in_specs=[SMEM_SPEC] * 4 + [HBM_SPEC] * 5,
        out_specs=(VMEM_SPEC,) * 4,
        scratch_shapes=[
            *[pltpu.VMEM(table.shape, table.dtype) for table in tables],
            pltpu.VMEM((6, ny, nz), f32),
            *[pltpu.VMEM((3, 2 * width * ny, nz), jnp.bfloat16) for _ in range(2)],
            *[pltpu.VMEM((2 * width * ny, half), jnp.bfloat16) for _ in range(2)],
            pltpu.VMEM((ny, *tile), f32),
            *[pltpu.VMEM((groups - 1, slabs, *tile), f32) for _ in range(2)],
            *[pltpu.VMEM((slabs, *tile), f32) for _ in range(2)],
            pltpu.VMEM(halo, f32), pltpu.VMEM(halo, f32),
            pltpu.VMEM(squares, f32),
            pltpu.VMEM((2, *squares), f32), pltpu.VMEM((2, *squares), f32),
            dma((width,)), dma((len(tables),)),
            dma((2, groups - 1, chunks)), dma((2, groups - 1, chunks)),
            dma((slabs,)), dma((slabs,)),
            dma((slabs,)), dma((slabs,)),
            dma((2, groups, chunks)), dma((2, groups, chunks)), dma((groups, max(min(SPREAD, chunks), 1))),
            dma((2, width)), dma((2, width)),
            dma((2,)), dma((2,)),
        ],
        compiler_params=pltpu.CompilerParams(
            vmem_limit_bytes=VMEM_LIMIT, collective_id=0, has_side_effects=True
        ),
        name="transform",
    )(*small, in_place(phase_field), *[in_place(table) for table in tables])
    phase_next, stress = pl.pallas_call(
        update_kernel,
        grid=(width,),
        out_shape=(
            jax.ShapeDtypeStruct(phase_field.shape, f32),
            jax.ShapeDtypeStruct((6, width, ny, nz), f32),
        ),
        in_specs=[SMEM_SPEC] * 2 + [VMEM_SPEC] * 6,
        out_specs=(
            pl.BlockSpec((count, 1, ny, nz), lambda i: (0, i, 0, 0)),
            pl.BlockSpec((6, 1, ny, nz), lambda i: (0, i, 0, 0)),
        ),
        scratch_shapes=[pltpu.VMEM((6, width, ny, nz), f32)],
        compiler_params=pltpu.CompilerParams(vmem_limit_bytes=VMEM_LIMIT),
        name="update",
    )(small[0], small[2], hat, phase, base, square, y_inverse, z_inverse)
    return (phase_next, stress)


def solution(mesh):
    return jax.shard_map(
        body,
        mesh=mesh,
        in_specs=(P("vert", "gx", None, None), P(), P(), P("vert"), P("vert")),
        out_specs=(P("vert", "gx", None, None), P(None, "gx", None, None)),
        check_vma=False,
    )
```
